32 devices in a mesh: dp: 8 (over z, y), ctx: 4 (over x, core).
Axes of the slice: x: 2, y: 2, z: 4, core: 2. Of those that a mesh axis runs over, the one named last changes fastest.
Arguments:
- tokens: bfloat16 [8, 2048, 1024], P('dp', 'ctx'), may hold values from -6 to 6
- time_feat: bfloat16 [8, 1024], P('dp'), may hold values from -6 to 6
- cotangent: bfloat16 [8, 2048, 1024], P('dp', 'ctx'), may hold values from -6 to 6
- segment_ids: int32 [8, 2048], P('dp'), may hold values from 0 to 7, never falling along the last dimension, each value on 1 to 1024 neighbouring positions
- time_weight: bfloat16 [1024, 1024], P(('dp', 'ctx')), may hold values from -0.1875 to 0.1875
- time_bias: bfloat16 [1024], P(('dp', 'ctx')), may hold values from -3 to 3
- query_weight: bfloat16 [1024, 1024], P(('dp', 'ctx')), may hold values from -0.1875 to 0.1875
- query_bias: bfloat16 [1024], P(('dp', 'ctx')), may hold values from -3 to 3
- key_weight: bfloat16 [1024, 1024], P(('dp', 'ctx')), may hold values from -0.1875 to 0.1875
- value_weight: bfloat16 [1024, 1024], P(('dp', 'ctx')), may hold values from -0.1875 to 0.1875
- value_bias: bfloat16 [1024], P(('dp', 'ctx')), may hold values from -3 to 3
- output_weight: bfloat16 [1024, 1024], P(('dp', 'ctx')), may hold values from -3 to 3
- output_bias: bfloat16 [1024], P(('dp', 'ctx')), may hold values from -3 to 3
- mixing_gain: bfloat16 [1024], P(('dp', 'ctx')), may hold values from 0.5 to 1.5
- mixing_bias: bfloat16 [1024], P(('dp', 'ctx')), may hold values from -3 to 3
- up_weight: bfloat16 [1024, 4096], P(('dp', 'ctx')), may hold values from -0.1875 to 0.1875
- up_bias: bfloat16 [4096], P(('dp', 'ctx')), may hold values from -3 to 3
- down_weight: bfloat16 [4096, 1024], P(('dp', 'ctx')), may hold values from -0.09375 to 0.09375
- down_bias: bfloat16 [1024], P(('dp', 'ctx')), may hold values from -3 to 3
- final_gain: bfloat16 [1024], P(('dp', 'ctx')), may hold values from 0.5 to 1.5
- final_bias: bfloat16 [1024], P(('dp', 'ctx')), may hold values from -3 to 3
Outputs:
- layer_out: bfloat16 [8, 2048, 1024], P('dp', 'ctx')
- tokens_grad: bfloat16 [8, 2048, 1024], P('dp', 'ctx')
- time_weight_grad: float32 [1024, 1024], P(('dp', 'ctx'))
- time_bias_grad: float32 [1024], P(('dp', 'ctx'))
- query_weight_grad: float32 [1024, 1024], P(('dp', 'ctx'))
- query_bias_grad: float32 [1024], P(('dp', 'ctx'))
- key_weight_grad: float32 [1024, 1024], P(('dp', 'ctx'))
- value_weight_grad: float32 [1024, 1024], P(('dp', 'ctx'))
- value_bias_grad: float32 [1024], P(('dp', 'ctx'))
- output_weight_grad: float32 [1024, 1024], P(('dp', 'ctx'))
- output_bias_grad: float32 [1024], P(('dp', 'ctx'))
- mixing_gain_grad: float32 [1024], P(('dp', 'ctx'))
- mixing_bias_grad: float32 [1024], P(('dp', 'ctx'))
- up_weight_grad: float32 [1024, 4096], P(('dp', 'ctx'))
- up_bias_grad: float32 [4096], P(('dp', 'ctx'))
- down_weight_grad: float32 [4096, 1024], P(('dp', 'ctx'))
- down_bias_grad: float32 [1024], P(('dp', 'ctx'))
- final_gain_grad: float32 [1024], P(('dp', 'ctx'))
- final_bias_grad: float32 [1024], P(('dp', 'ctx'))
The draws below stay inside these ranges and needn't reach their ends.
Inputs may be any that keep to these rules, and one draw needn't show every extreme that they name: `segment_ids`: in each row the document numbers never fall, every number appears, each document holds 1 to 1024 tokens and some document of every row holds exactly 1024.
All inputs are finite; a program needn't handle non-finite values.
Results may differ from the reference program's by a relative error of at most 0.018.
Values may be sent and summed in bfloat16 or wider, within the bound.
No kernel may reach another device: no remote copies, remote signals or barrier semaphores. Data moves between devices by JAX's collectives and lax.ppermute only.
A program may use at most 192 MiB of HBM per device.

```python
import math
import jax
import jax.numpy as jnp
import numpy as np
from jax import lax

D = 1024
HEADS = 16
HEAD_DIM = 64
FF = 4096
SEQ = 2048
DOCS = 8
MOST = 1024
ROWS = 8


def with_spikes(drawn, rng, source, target, blocks, factor):
    def block_of(dim):
        return (jnp.arange(drawn.shape[dim]) // (drawn.shape[dim] // blocks)).reshape((-1,) + (1,) * (drawn.ndim - 1 - dim))

    one_side = jax.random.permutation(rng, blocks)[block_of(target)]
    other_side = (block_of(target) + blocks // 2) % blocks
    return jnp.where((block_of(source) == one_side) | (block_of(source) == other_side), factor * drawn, drawn)


def block_scale(rng, dims, shards, smallest, largest):
    level, own = 1.0, jax.random.fold_in(rng, 6)
    for position, blocks in shards:
        steps = jnp.exp(jax.random.uniform(jax.random.fold_in(own, position), (blocks,), jnp.float32, smallest / len(shards), largest / len(shards)))
        level = level * jnp.repeat(steps, dims[position] // blocks).reshape([-1 if axis == position else 1 for axis in range(len(dims))])
    return level


def length_profile(number_of, total, most, lean):
    portions = [(1 << 20) // math.isqrt(rank ** lean) + 1 for rank in range(2, number_of + 1)]
    surplus, given = total - most - (number_of - 1), [1] * (number_of - 1)
    while surplus > 0:
        free = [i for i in range(number_of - 1) if given[i] < most]
        pool, left = sum([portions[i] for i in free]), surplus
        for i in free:
            extra = min(most - given[i], max(1, left * portions[i] // pool), surplus)
            given[i] = given[i] + extra
            surplus = surplus - extra
    return np.array([most] + given)


def ragged(rng, amount, total, bound, skew):
    if amount == 2:
        one = jax.random.randint(rng, (), max(1, total - bound), min(bound, total - 1) + 1)
        return jnp.stack([one, total - one])
    lengths = jnp.asarray(length_profile(amount, total, bound, skew), jnp.int32)
    pairs = (amount - 1) // 2
    donor, taker = lengths[1:1 + 2 * pairs:2], lengths[2:2 + 2 * pairs:2]
    margin = jnp.minimum(donor - 1, bound - taker)
    passed = jax.random.randint(jax.random.fold_in(rng, 1), (pairs,), 0, 1 << 20) % (margin + 1)
    lengths = lengths.at[1:1 + 2 * pairs:2].set(donor - passed).at[2:2 + 2 * pairs:2].set(taker + passed)
    return lengths[jax.random.permutation(jax.random.fold_in(rng, 2), amount)]


def scatter_about(key, extent, deviation, bound, cuts=(), kind=jnp.bfloat16):
    values = deviation * jax.random.normal(key, extent, jnp.float32)
    if cuts:
        values = values * block_scale(key, extent, cuts, -0.22, 0.18)
    return jnp.clip(values, -bound, bound).astype(kind)


def noise_with(rng, dims, width, bound, split, heavy, kind=jnp.bfloat16):
    entries = width * jax.random.normal(rng, dims, jnp.float32)
    if split:
        entries = entries * block_scale(rng, dims, split, -0.22, 0.18)
    return jnp.clip(with_spikes(entries, jax.random.fold_in(rng, 3), *heavy), -bound, bound).astype(kind)


def setup_inputs(seed: int = 0) -> dict:
    keys = jax.random.split(jax.random.key(seed), 22)
    return {
        "tokens": noise_with(keys[0], (ROWS, SEQ, D), 1.0, 6.0, ((0, 8), (1, 4)), (0, 2, 8, 2.0)),
        "time_feat": scatter_about(keys[1], (ROWS, D), 1.0, 6.0, ((0, 8),)),
        "cotangent": scatter_about(keys[2], (ROWS, SEQ, D), 1.0, 6.0, ((0, 8), (1, 4))),
        "segment_ids": jax.vmap(lambda own: jnp.searchsorted(jnp.cumsum(ragged(own, DOCS, SEQ, MOST, 2)), jnp.arange(SEQ), side="right"))(jax.random.split(keys[3], ROWS)).reshape((ROWS, SEQ)).astype(jnp.int32),
        "time_weight": scatter_about(keys[4], (D, D), D ** -0.5, 0.1875, ((0, 32),)),
        "time_bias": scatter_about(keys[5], (D,), 0.5, 3.0, ((0, 32),)),
        "query_weight": scatter_about(keys[6], (D, D), D ** -0.5, 0.1875, ((0, 32),)),
        "query_bias": scatter_about(keys[7], (D,), 0.5, 3.0, ((0, 32),)),
        "key_weight": scatter_about(keys[8], (D, D), D ** -0.5, 0.1875, ((0, 32),)),
        "value_weight": scatter_about(keys[9], (D, D), D ** -0.5, 0.1875, ((0, 32),)),
        "value_bias": scatter_about(keys[10], (D,), 0.5, 3.0, ((0, 32),)),
        "output_weight": scatter_about(keys[11], (D, D), (D * DOCS // SEQ) ** -0.5, 3.0, ((0, 32),)),
        "output_bias": scatter_about(keys[12], (D,), 0.5, 3.0, ((0, 32),)),
        "mixing_gain": jnp.clip(1.0 + 0.1 * jax.random.normal(keys[13], (D,), jnp.float32), 0.5, 1.5).astype(jnp.bfloat16),
        "mixing_bias": scatter_about(keys[14], (D,), 0.5, 3.0, ((0, 32),)),
        "up_weight": scatter_about(keys[15], (D, FF), D ** -0.5, 0.1875, ((0, 32),)),
        "up_bias": scatter_about(keys[16], (FF,), 0.5, 3.0, ((0, 32),)),
        "down_weight": scatter_about(keys[17], (FF, D), FF ** -0.5, 0.09375, ((0, 32),)),
        "down_bias": scatter_about(keys[18], (D,), 0.5, 3.0, ((0, 32),)),
        "final_gain": jnp.clip(1.0 + 0.1 * jax.random.normal(keys[19], (D,), jnp.float32), 0.5, 1.5).astype(jnp.bfloat16),
        "final_bias": scatter_about(keys[20], (D,), 0.5, 3.0, ((0, 32),)),
    }


@jax.custom_vjp
def low(v):
    return lax.optimization_barrier(v.astype(jnp.bfloat16)).astype(jnp.float32)

@jax.custom_vjp
def low_back(v):
    return v

def low_keep(v):
    return (low(v), None)

def low_pass(kept, grad):
    return (grad,)

def back_keep(v):
    return (v, None)

def back_low(kept, grad):
    return (low(grad),)
low.defvjp(low_keep, low_pass)
low_back.defvjp(back_keep, back_low)
highest = lax.Precision.HIGHEST
norm_epsilon = 1e-05
masked_score = -1e+30

def matmul_plain(left, right):
    return jnp.dot(left, right, precision=highest, preferred_element_type=jnp.float32)

def layer_norm(values, gain, shift):
    average = lax.optimization_barrier(jnp.mean(values, axis=-1, keepdims=True))
    centered = values - average
    variance = lax.optimization_barrier(jnp.mean(centered * centered, axis=-1, keepdims=True))
    return centered * lax.rsqrt(variance + norm_epsilon) * gain + shift

def split_heads(matrix):
    return matrix.reshape(SEQ, HEADS, HEAD_DIM).transpose(1, 0, 2)

def layer(params, tokens_row, time_row, same_doc):
    time_weight, time_bias, query_weight, query_bias, key_weight, value_weight, value_bias, output_weight, output_bias, mixing_gain, mixing_bias, up_weight, up_bias, down_weight, down_bias, final_gain, final_bias = params
    time_shift = matmul_plain(time_row[None, :], time_weight)[0] + time_bias
    residual_in = tokens_row + time_shift[None, :]
    start_low = low(residual_in)
    queries = low(low_back(matmul_plain(start_low, query_weight) + query_bias))
    keys_all = low(low_back(matmul_plain(start_low, key_weight)))
    values_all = low(low_back(matmul_plain(start_low, value_weight) + value_bias))

    def one_head(triple):
        query_head, key_head, value_head = triple
        scores = jnp.einsum('qd,kd->qk', query_head, key_head, precision=highest) * HEAD_DIM ** (-0.5)
        scores = jnp.where(same_doc, low_back(scores), masked_score)
        row_peak = lax.optimization_barrier(jnp.max(scores, axis=-1, keepdims=True))
        unscaled = jnp.exp(scores - row_peak)
        attn_probs = low(unscaled / lax.optimization_barrier(jnp.sum(unscaled, axis=-1, keepdims=True)))
        return matmul_plain(attn_probs, value_head)
    mixture = lax.map(jax.checkpoint(one_head), (split_heads(queries), split_heads(keys_all), split_heads(values_all)))
    attended = low(low_back(mixture.transpose(1, 0, 2).reshape(SEQ, D)))
    branch = low_back(matmul_plain(attended, output_weight) + output_bias)
    hidden_one = layer_norm(residual_in + branch, mixing_gain, mixing_bias)
    pre_gelu = low_back(matmul_plain(low(hidden_one), up_weight) + up_bias)
    activated = low(jax.nn.gelu(pre_gelu, approximate=False))
    feed_out = low_back(matmul_plain(activated, down_weight) + down_bias)
    return layer_norm(hidden_one + feed_out, final_gain, final_bias)

def reference(tokens, time_feat, cotangent, segment_ids, time_weight, time_bias, query_weight, query_bias, key_weight, value_weight, value_bias, output_weight, output_bias, mixing_gain, mixing_bias, up_weight, up_bias, down_weight, down_bias, final_gain, final_bias):
    params = tuple((weight.astype(jnp.float32) for weight in (time_weight, time_bias, query_weight, query_bias, key_weight, value_weight, value_bias, output_weight, output_bias, mixing_gain, mixing_bias, up_weight, up_bias, down_weight, down_bias, final_gain, final_bias)))

    def one_row(totals, row_item):
        tokens_row, time_row, cotangent_row, ids_row = row_item
        same_doc = ids_row[:, None] == ids_row[None, :]

        def forward(weights, inputs):
            return layer(weights, inputs, time_row, same_doc)
        result, pullback = jax.vjp(forward, params, tokens_row)
        weight_grads, input_grad = pullback(cotangent_row)
        totals = tuple((left + right for left, right in zip(totals, weight_grads)))
        return (totals, (result.astype(jnp.bfloat16), input_grad.astype(jnp.bfloat16)))
    zero_grads = tuple((jnp.zeros(weight.shape, jnp.float32) for weight in params))
    totals, (layer_out, tokens_grad) = lax.scan(one_row, zero_grads, (tokens.astype(jnp.float32), time_feat.astype(jnp.float32), cotangent.astype(jnp.float32), segment_ids))
    return (layer_out, tokens_grad, totals[0], totals[1], totals[2], totals[3], totals[4], totals[5], totals[6], totals[7], totals[8], totals[9], totals[10], totals[11], totals[12], totals[13], totals[14], totals[15], totals[16])
```

```python
import functools

import jax
import jax.numpy as jnp
from jax import lax
from jax.experimental import pallas as pl
from jax.experimental.pallas import tpu as pltpu
from jax.sharding import PartitionSpec as P

HEAD_DIM = 64
BLOCK = 256
MASKED = -1e30
EPSILON = 1e-05
SCALE = HEAD_DIM**-0.5
SCALE_LOG2 = SCALE * 1.4426950408889634
BOTH = ("dp", "ctx")
f32, bf16 = jnp.float32, jnp.bfloat16


def nn(left, right):
    return jnp.dot(left, right, preferred_element_type=f32)


def tn(left, right):
    return lax.dot_general(left, right, (((0,), (0,)), ((), ())), preferred_element_type=f32)


def nt(left, right):
    return lax.dot_general(left, right, (((1,), (1,)), ((), ())), preferred_element_type=f32)


def head_only(pair, which):
    lane = lax.broadcasted_iota(jnp.int32, pair.shape, 1)
    keep = (lane < HEAD_DIM) if which == 0 else (lane >= HEAD_DIM)
    return jnp.where(keep, pair, jnp.zeros_like(pair))


def place(block, me, per_chunk):
    return lax.bitwise_xor(block // per_chunk, me) * per_chunk + lax.rem(block, per_chunk)


def forward_kernel(
    per_chunk, pairs, info, q_ref, k_ref, v_ref, idc_ref, idr_ref, o_ref, lse_ref, o_acc, m_acc, l_acc
):
    i = pl.program_id(0)
    me = info[2, 0]
    m_acc[...] = jnp.full_like(m_acc, MASKED)
    l_acc[...] = jnp.zeros_like(l_acc)
    o_acc[...] = jnp.zeros_like(o_acc)
    ids_q = idr_ref[pl.ds(i, 1)][0]

    def step(j, carry):
        at = pl.multiple_of(place(j, me, per_chunk) * BLOCK, BLOCK)
        same = idc_ref[pl.ds(pl.multiple_of(j * BLOCK, BLOCK), BLOCK), :] == ids_q
        for p in range(pairs):
            cols = slice(p * 128, (p + 1) * 128)
            k_pair, v_pair, q_pair = k_ref[pl.ds(at, BLOCK), cols], v_ref[pl.ds(at, BLOCK), cols], q_ref[:, cols]
            for w in range(2):
                h = 2 * p + w
                t = jnp.where(same, nt(k_pair, head_only(q_pair, w)) * SCALE_LOG2, MASKED)
                m_old = m_acc[h]
                m_new = jnp.maximum(m_old, jnp.max(t, axis=0, keepdims=True))
                alpha = jnp.exp2(m_old - m_new)
                e = jnp.exp2(t - m_new)
                l_acc[h] = l_acc[h] * alpha + jnp.sum(e, axis=0, keepdims=True)
                m_acc[h] = m_new
                rows = slice(h * HEAD_DIM, (h + 1) * HEAD_DIM)
                o_acc[rows] = o_acc[rows] * alpha + tn(v_pair, e.astype(bf16))[w * HEAD_DIM : (w + 1) * HEAD_DIM]
        return carry

    lax.fori_loop(info[0, i], info[1, i], step, 0)
    for p in range(pairs):
        parts = []
        for w in range(2):
            h = 2 * p + w
            parts.append(o_acc[h * HEAD_DIM : (h + 1) * HEAD_DIM] / l_acc[h])
            lse_ref[0, h : h + 1, :] = m_acc[h] + jnp.log2(l_acc[h])
        o_ref[:, p * 128 : (p + 1) * 128] = jnp.concatenate(parts, axis=0).T.astype(bf16)


def attention_forward(info, qkv, ids_col, ids_row, per_chunk):
    rows, width = qkv.shape[0], qkv.shape[1] // 3
    blocks, heads = rows // BLOCK, width // HEAD_DIM
    return pl.pallas_call(
        functools.partial(forward_kernel, per_chunk, heads // 2),
        grid_spec=pltpu.PrefetchScalarGridSpec(
            num_scalar_prefetch=1,
            grid=(blocks,),
            in_specs=[
                pl.BlockSpec((BLOCK, width), lambda i, info: (place(i, info[2, 0], per_chunk), 0)),
                pl.BlockSpec((rows, width), lambda i, info: (0, 1)),
                pl.BlockSpec((rows, width), lambda i, info: (0, 2)),
                pl.BlockSpec((rows, 1), lambda i, info: (0, 0)),
                pl.BlockSpec((blocks, 1, BLOCK), lambda i, info: (0, 0, 0)),
            ],
            out_specs=[
                pl.BlockSpec((BLOCK, width), lambda i, info: (place(i, info[2, 0], per_chunk), 0)),
                pl.BlockSpec((1, heads, BLOCK), lambda i, info: (i, 0, 0)),
            ],
            scratch_shapes=[
                pltpu.VMEM((width, BLOCK), f32),
                pltpu.VMEM((heads, 1, BLOCK), f32),
                pltpu.VMEM((heads, 1, BLOCK), f32),
            ],
        ),
        out_shape=[
            jax.ShapeDtypeStruct((rows, width), bf16),
            jax.ShapeDtypeStruct((blocks, heads, BLOCK), f32),
        ],
        name="attention_forward",
    )(info, qkv, qkv, qkv, ids_col, ids_row)


def backward_kernel(
    per_chunk, pairs, info, q_ref, k_ref, v_ref, do_ref, o_ref, lse_ref, idc_ref, idr_ref,
    out_ref, delta_ref, dq_acc, dk_acc, dv_acc,
):
    j = pl.program_id(0)
    blocks = pl.num_programs(0)
    me = info[2, 0]
    width = 128 * pairs

    @pl.when(j == 0)
    def _():
        dq_acc[...] = jnp.zeros_like(dq_acc)

        def fill(i, carry):
            at = pl.multiple_of(place(i, me, per_chunk) * BLOCK, BLOCK)
            for p in range(pairs):
                cols = slice(p * 128, (p + 1) * 128)
                prod = (do_ref[pl.ds(at, BLOCK), cols].astype(f32) * o_ref[pl.ds(at, BLOCK), cols].astype(f32)).T
                for w in range(2):
                    h = 2 * p + w
                    delta_ref[i, h : h + 1, :] = jnp.sum(
                        prod[w * HEAD_DIM : (w + 1) * HEAD_DIM], axis=0, keepdims=True
                    )
            return carry

        lax.fori_loop(0, blocks, fill, 0)

    dk_acc[...] = jnp.zeros_like(dk_acc)
    dv_acc[...] = jnp.zeros_like(dv_acc)
    ids_k = idc_ref[pl.ds(pl.multiple_of(j * BLOCK, BLOCK), BLOCK), :]

    def step(i, carry):
        at = pl.multiple_of(place(i, me, per_chunk) * BLOCK, BLOCK)
        same = ids_k == idr_ref[pl.ds(i, 1)][0]
        for p in range(pairs):
            cols = slice(p * 128, (p + 1) * 128)
            k_pair, v_pair = k_ref[:, cols], v_ref[:, cols]
            q_pair, do_pair = q_ref[pl.ds(at, BLOCK), cols], do_ref[pl.ds(at, BLOCK), cols]
            for w in range(2):
                h = 2 * p + w
                q_one, do_one = head_only(q_pair, w), head_only(do_pair, w)
                t = nt(k_pair, q_one) * SCALE_LOG2 - lse_ref[i, h : h + 1, :]
                e = jnp.exp2(jnp.where(same, t, MASKED))
                ds = (e * (nt(v_pair, do_one) - delta_ref[i, h : h + 1, :])).astype(bf16)
                dv_acc[:, cols] += nn(e.astype(bf16), do_one)
                dk_acc[:, cols] += nn(ds, q_one)
                dq_acc[pl.ds(at, BLOCK), cols] += tn(ds, head_only(k_pair, w))
        return carry

    lax.fori_loop(info[0, j], info[1, j], step, 0)
    mine = pl.multiple_of(place(j, me, per_chunk) * BLOCK, BLOCK)
    out_ref[pl.ds(mine, BLOCK), width : 2 * width] = (dk_acc[...] * SCALE).astype(bf16)
    out_ref[pl.ds(mine, BLOCK), 2 * width : 3 * width] = dv_acc[...].astype(bf16)

    @pl.when(j == blocks - 1)
    def _():
        out_ref[:, 0:width] = (dq_acc[...] * SCALE).astype(bf16)


def attention_backward(info, qkv, do, o, lse, ids_col, ids_row, per_chunk):
    rows, width = o.shape
    blocks, heads = rows // BLOCK, width // HEAD_DIM
    return pl.pallas_call(
        functools.partial(backward_kernel, per_chunk, heads // 2),
        grid_spec=pltpu.PrefetchScalarGridSpec(
            num_scalar_prefetch=1,
            grid=(blocks,),
            in_specs=[
                pl.BlockSpec((rows, width), lambda i, info: (0, 0)),
                pl.BlockSpec((BLOCK, width), lambda i, info: (place(i, info[2, 0], per_chunk), 1)),
                pl.BlockSpec((BLOCK, width), lambda i, info: (place(i, info[2, 0], per_chunk), 2)),
                pl.BlockSpec((rows, width), lambda i, info: (0, 0)),
                pl.BlockSpec((rows, width), lambda i, info: (0, 0)),
                pl.BlockSpec((blocks, heads, BLOCK), lambda i, info: (0, 0, 0)),
                pl.BlockSpec((rows, 1), lambda i, info: (0, 0)),
                pl.BlockSpec((blocks, 1, BLOCK), lambda i, info: (0, 0, 0)),
            ],
            out_specs=pl.BlockSpec((rows, 3 * width), lambda i, info: (0, 0)),
            scratch_shapes=[
                pltpu.VMEM((blocks, heads, BLOCK), f32),
                pltpu.VMEM((rows, width), f32),
                pltpu.VMEM((BLOCK, width), f32),
                pltpu.VMEM((BLOCK, width), f32),
            ],
        ),
        out_shape=jax.ShapeDtypeStruct((rows, 3 * width), bf16),
        name="attention_backward",
    )(info, qkv, qkv, qkv, do, o, lse, ids_col, ids_row)


def spans(ids, me):
    blocks = ids.shape[0] // BLOCK
    per_block = ids.reshape(blocks, BLOCK)
    low = jnp.sum(ids[None, :] < per_block[:, :1], axis=1) // BLOCK
    high = (jnp.sum(ids[None, :] <= per_block[:, -1:], axis=1) + BLOCK - 1) // BLOCK
    return jnp.stack([low, high, jnp.full((blocks,), me)]).astype(jnp.int32)


def swap(value, axis, mask):
    size = lax.axis_size(axis)
    return lax.ppermute(value, axis, [(i, i ^ mask) for i in range(size)])


def bits(size):
    return [1 << b for b in range(size.bit_length() - 1)]


def gather_relative(value, axis):
    held = {0: value}
    for bit in reversed(bits(lax.axis_size(axis))):
        held.update({k | bit: swap(v, axis, bit) for k, v in list(held.items())})
    return [held[k] for k in range(len(held))]


def trade(pieces, axis):
    return [pieces[0]] + [swap(pieces[k], axis, k) for k in range(1, len(pieces))]


def to_absolute(pieces, me):
    stacked = jnp.stack(pieces)
    return [lax.dynamic_index_in_dim(stacked, lax.bitwise_xor(me, c), 0, False) for c in range(len(pieces))]


def halve(value, axis, dtype):
    me, size = lax.axis_index(axis), lax.axis_size(axis)
    count = size
    for bit in bits(size):
        value = value.reshape((count // 2, 2) + value.shape[1:])
        mine = lax.rem(me // bit, 2)
        give = lax.dynamic_index_in_dim(value, 1 - mine, 1, False).astype(dtype)
        keep = lax.dynamic_index_in_dim(value, mine, 1, False)
        value = keep + swap(give, axis, bit).astype(f32)
        count //= 2
    return value[0]


def normalize(values, gain, shift):
    average = jnp.mean(values, axis=-1, keepdims=True)
    centered = values - average
    inverse = lax.rsqrt(jnp.mean(centered * centered, axis=-1, keepdims=True) + EPSILON)
    normed = centered * inverse
    return normed * gain + shift, normed, inverse


def normalize_back(upstream, normed, inverse, gain):
    scaled = upstream * gain
    plain = jnp.mean(scaled, axis=-1, keepdims=True)
    cross = jnp.mean(scaled * normed, axis=-1, keepdims=True)
    result = inverse * (scaled - plain - normed * cross)
    return result, jnp.sum(upstream * normed, axis=0), jnp.sum(upstream, axis=0)


def shards(
    tokens, time_feat, cotangent, segment_ids, time_weight, time_bias, query_weight, query_bias, key_weight,
    value_weight, value_bias, output_weight, output_bias, mixing_gain, mixing_bias, up_weight, up_bias,
    down_weight, down_bias, final_gain, final_bias,
):
    me_dp, me = lax.axis_index("dp"), lax.axis_index("ctx")
    dp, ctx = lax.axis_size("dp"), lax.axis_size("ctx")
    devices = dp * ctx
    piece, width = tokens.shape[1], tokens.shape[2]
    hidden = up_weight.shape[1]
    own, ratio = width // devices, hidden // width
    cols = width // ctx
    per_chunk = piece // BLOCK
    tokens, cotangent, ids = tokens[0], cotangent[0], segment_ids[0]

    vectors = [
        time_bias, query_bias, value_bias, output_bias, mixing_gain, mixing_bias, down_bias, final_gain, final_bias
    ]
    small = jnp.concatenate([jnp.stack(vectors), up_bias.reshape(ratio, own)]).T
    small = jnp.pad(small, ((0, 0), (0, 128 - small.shape[1])))
    first = lax.all_gather(
        jnp.concatenate([query_weight, key_weight, value_weight, time_weight, small], axis=1), BOTH, axis=0, tiled=True
    )
    second = lax.all_gather(jnp.concatenate([up_weight, output_weight], axis=1), BOTH, axis=0, tiled=True)
    down_full = lax.all_gather(down_weight, BOTH, axis=0, tiled=True)
    up_full, output_full = second[:, :hidden], second[:, hidden:]

    token_chunks = gather_relative(tokens, "ctx")
    time_feats = jnp.concatenate(gather_relative(time_feat, "dp"))

    table = first[:, 4 * width :].astype(f32).T
    time_shift_bias, query_shift, value_shift, output_shift, gain_one, bias_one, down_shift, gain_two, bias_two = [
        table[n] for n in range(len(vectors))
    ]
    up_shift = table[len(vectors) : len(vectors) + ratio].reshape(ratio, devices, own).transpose(1, 0, 2).reshape(hidden)
    time_shift = nn(time_feat, first[:, 3 * width : 4 * width]) + time_shift_bias

    def my_cols(n):
        return lax.dynamic_slice_in_dim(first, n * width + me * cols, cols, 1)

    qkv_weight = jnp.concatenate([my_cols(n) for n in range(3)], axis=1)
    qkv_shift = jnp.concatenate(
        [
            lax.dynamic_slice_in_dim(query_shift, me * cols, cols),
            jnp.zeros((cols,), f32),
            lax.dynamic_slice_in_dim(value_shift, me * cols, cols),
        ]
    )
    start_row = (jnp.concatenate(token_chunks).astype(f32) + time_shift).astype(bf16)
    residual_in = tokens.astype(f32) + time_shift
    qkv = (nn(start_row, qkv_weight) + qkv_shift).astype(bf16)

    info = spans(ids, me)
    ids_col, ids_row = ids.reshape(-1, 1), ids.reshape(-1, 1, BLOCK)
    mixed, logsum = attention_forward(info, qkv, ids_col, ids_row, per_chunk)
    returned = trade([mixed[k * piece : (k + 1) * piece] for k in range(ctx)], "ctx")
    attended = jnp.concatenate(to_absolute(returned, me), axis=1)

    branch = nn(attended, output_full) + output_shift
    hidden_one, normed_one, inverse_one = normalize(residual_in + branch, gain_one, bias_one)
    hidden_low = hidden_one.astype(bf16)
    pre_gelu = nn(hidden_low, up_full) + up_shift
    share = 0.5 * (1.0 + lax.erf(pre_gelu * 0.5**0.5))
    activated = (pre_gelu * share).astype(bf16)
    slope = (share + pre_gelu * jnp.exp(-0.5 * pre_gelu * pre_gelu) * 0.3989422804014327).astype(bf16)
    activated, slope = lax.optimization_barrier((activated, slope))
    feed_out = nn(activated, down_full) + down_shift
    result, normed_two, inverse_two = normalize(hidden_one + feed_out, gain_two, bias_two)
    layer_out = result.astype(bf16)

    upstream = cotangent.astype(f32)
    grad_two, gain_two_grad, bias_two_grad = normalize_back(upstream, normed_two, inverse_two, gain_two)
    grad_feed = grad_two.astype(bf16)
    down_grad = tn(activated, grad_feed).astype(bf16)
    down_shift_grad = jnp.sum(grad_feed.astype(f32), axis=0)
    grad_inner = (nt(grad_feed, down_full) * slope.astype(f32)).astype(bf16)
    up_grad = tn(hidden_low, grad_inner).astype(bf16)
    up_shift_grad = jnp.sum(grad_inner.astype(f32), axis=0)
    grad_hidden = grad_two + nt(grad_inner, up_full)
    grad_one, gain_one_grad, bias_one_grad = normalize_back(grad_hidden, normed_one, inverse_one, gain_one)
    grad_branch = grad_one.astype(bf16)
    output_grad = tn(attended, grad_branch).astype(bf16)
    output_shift_grad = jnp.sum(grad_branch.astype(f32), axis=0)
    down_blocks = down_grad.reshape(devices, ratio, own, width)
    packed = jnp.concatenate(
        [up_grad] + [down_blocks[:, n].reshape(width, width) for n in range(ratio)] + [output_grad], axis=1
    )
    packed = lax.psum_scatter(packed, BOTH, scatter_dimension=0, tiled=True).astype(f32)
    up_weight_grad = packed[:, :hidden]
    down_weight_grad = jnp.concatenate(
        [packed[:, hidden + n * width : hidden + (n + 1) * width] for n in range(ratio)], axis=0
    )
    output_weight_grad = packed[:, 2 * hidden :]

    grad_attended = nt(grad_branch, output_full).astype(bf16)
    pieces = [lax.dynamic_slice_in_dim(grad_attended, lax.bitwise_xor(me, k) * cols, cols, 1) for k in range(ctx)]
    grad_mixed = jnp.concatenate(trade(pieces, "ctx"))
    grad_qkv = attention_backward(info, qkv, grad_mixed, mixed, logsum, ids_col, ids_row, per_chunk)

    partial = {}
    for k in reversed(range(ctx)):
        partial[k] = nt(grad_qkv[k * piece : (k + 1) * piece], qkv_weight)
    for bit in bits(ctx):
        for k in [k for k in partial if k & bit]:
            partial[k ^ bit] = partial[k ^ bit] + swap(partial.pop(k).astype(bf16), "ctx", bit).astype(f32)
    tokens_grad = (grad_one + partial[0]).astype(bf16)

    qkv_grad = tn(start_row, grad_qkv)
    qkv_sum = jnp.sum(grad_qkv.astype(f32), axis=0)
    row_sum = jnp.sum(grad_one, axis=0, keepdims=True) + lax.dot_general(
        qkv_sum[None],
        qkv_weight.astype(f32),
        (((1,), (1,)), ((), ())),
        precision=lax.Precision.HIGHEST,
        preferred_element_type=f32,
    )
    for bit in bits(ctx):
        row_sum = row_sum + swap(row_sum, "ctx", bit)
    row_sums = jnp.concatenate(gather_relative(row_sum, "dp"))
    mine = (me_dp * ctx + me) * own
    time_weight_grad = lax.dot_general(
        lax.dynamic_slice_in_dim(time_feats, mine, own, 1).astype(f32),
        row_sums,
        (((0,), (0,)), ((), ())),
        precision=lax.Precision.HIGHEST,
        preferred_element_type=f32,
    )
    time_bias_grad = lax.dynamic_slice_in_dim(jnp.sum(row_sums, axis=0), mine, own)

    summed = halve(qkv_grad.reshape(dp, ctx * own, 3 * cols), "dp", bf16).reshape(ctx, own, 3 * cols)
    blocks_out = to_absolute(
        trade([lax.dynamic_index_in_dim(summed, lax.bitwise_xor(me, k), 0, False) for k in range(ctx)], "ctx"), me
    )
    query_weight_grad, key_weight_grad, value_weight_grad = [
        jnp.concatenate([block[:, n * cols : (n + 1) * cols] for block in blocks_out], axis=1) for n in range(3)
    ]

    def spread(part):
        return lax.dynamic_update_slice_in_dim(jnp.zeros((width,), f32), part, me * cols, 0)

    vector_grads = jnp.stack(
        [
            spread(qkv_sum[:cols]),
            spread(qkv_sum[2 * cols :]),
            output_shift_grad,
            gain_one_grad,
            bias_one_grad,
            down_shift_grad,
            gain_two_grad,
            bias_two_grad,
        ]
    ).reshape(8, devices, own)
    vector_grads = jnp.concatenate(
        [vector_grads.transpose(1, 0, 2).reshape(devices, 8 * own), up_shift_grad.reshape(devices, ratio * own)], axis=1
    )
    vector_grads = halve(halve(vector_grads.reshape(dp, ctx, -1), "dp", f32), "ctx", f32)
    (
        query_bias_grad,
        value_bias_grad,
        output_bias_grad,
        mixing_gain_grad,
        mixing_bias_grad,
        down_bias_grad,
        final_gain_grad,
        final_bias_grad,
    ) = [vector_grads[n * own : (n + 1) * own] for n in range(8)]
    up_bias_grad = vector_grads[8 * own :]
    return (
        layer_out[None],
        tokens_grad[None],
        time_weight_grad,
        time_bias_grad,
        query_weight_grad,
        query_bias_grad,
        key_weight_grad,
        value_weight_grad,
        value_bias_grad,
        output_weight_grad,
        output_bias_grad,
        mixing_gain_grad,
        mixing_bias_grad,
        up_weight_grad,
        up_bias_grad,
        down_weight_grad,
        down_bias_grad,
        final_gain_grad,
        final_bias_grad,
    )


def solution(mesh):
    rows, split_rows, split = P("dp", "ctx", None), P(BOTH, None), P(BOTH)
    return jax.shard_map(
        shards,
        mesh=mesh,
        in_specs=(
            rows, P("dp", None), rows, P("dp", None), split_rows, split, split_rows, split, split_rows, split_rows,
            split, split_rows, split, split, split, split_rows, split, split_rows, split, split, split,
        ),
        out_specs=(
            rows, rows, split_rows, split, split_rows, split, split_rows, split_rows, split, split_rows, split, split,
            split, split_rows, split, split_rows, split, split, split,
        ),
        check_vma=False,
    )
```

```python
import functools

import jax
import jax.numpy as jnp
from jax import lax
from jax.experimental import pallas as pl
from jax.experimental.pallas import tpu as pltpu
from jax.sharding import PartitionSpec as P

HEAD_DIM = 64
BLOCK = 256
MASKED = -1e30
EPSILON = 1e-05
SCALE = HEAD_DIM**-0.5
SCALE_LOG2 = SCALE * 1.4426950408889634
BOTH = ("dp", "ctx")
f32, bf16 = jnp.float32, jnp.bfloat16


def nn(left, right):
    return jnp.dot(left, right, preferred_element_type=f32)


def tn(left, right):
    return lax.dot_general(left, right, (((0,), (0,)), ((), ())), preferred_element_type=f32)


def nt(left, right):
    return lax.dot_general(left, right, (((1,), (1,)), ((), ())), preferred_element_type=f32)


def head_only(pair, which):
    lane = lax.broadcasted_iota(jnp.int32, pair.shape, 1)
    keep = (lane < HEAD_DIM) if which == 0 else (lane >= HEAD_DIM)
    return jnp.where(keep, pair, jnp.zeros_like(pair))


def place(block, me, per_chunk):
    return lax.bitwise_xor(block // per_chunk, me) * per_chunk + lax.rem(block, per_chunk)


def forward_kernel(
    per_chunk, pairs, info, q_ref, k_ref, v_ref, idc_ref, idr_ref, o_ref, lse_ref, o_acc, m_acc, l_acc
):
    i = pl.program_id(0)
    me = info[2, 0]
    m_acc[...] = jnp.full_like(m_acc, MASKED)
    l_acc[...] = jnp.zeros_like(l_acc)
    o_acc[...] = jnp.zeros_like(o_acc)
    ids_q = idr_ref[pl.ds(i, 1)][0]

    def step(j, carry):
        at = pl.multiple_of(place(j, me, per_chunk) * BLOCK, BLOCK)
        same = idc_ref[pl.ds(pl.multiple_of(j * BLOCK, BLOCK), BLOCK), :] == ids_q
        for p in range(pairs):
            cols = slice(p * 128, (p + 1) * 128)
            k_pair, v_pair, q_pair = k_ref[pl.ds(at, BLOCK), cols], v_ref[pl.ds(at, BLOCK), cols], q_ref[:, cols]
            for w in range(2):
                h = 2 * p + w
                t = jnp.where(same, nt(k_pair, head_only(q_pair, w)) * SCALE_LOG2, MASKED)
                m_old = m_acc[h]
                m_new = jnp.maximum(m_old, jnp.max(t, axis=0, keepdims=True))
                alpha = jnp.exp2(m_old - m_new)
                e = jnp.exp2(t - m_new)
                l_acc[h] = l_acc[h] * alpha + jnp.sum(e, axis=0, keepdims=True)
                m_acc[h] = m_new
                rows = slice(h * HEAD_DIM, (h + 1) * HEAD_DIM)
                o_acc[rows] = o_acc[rows] * alpha + tn(v_pair, e.astype(bf16))[w * HEAD_DIM : (w + 1) * HEAD_DIM]
        return carry

    lax.fori_loop(info[0, i], info[1, i], step, 0)
    for p in range(pairs):
        parts = []
        for w in range(2):
            h = 2 * p + w
            parts.append(o_acc[h * HEAD_DIM : (h + 1) * HEAD_DIM] / l_acc[h])
            lse_ref[0, h : h + 1, :] = m_acc[h] + jnp.log2(l_acc[h])
        o_ref[:, p * 128 : (p + 1) * 128] = jnp.concatenate(parts, axis=0).T.astype(bf16)


def attention_forward(info, qkv, ids_col, ids_row, per_chunk):
    rows, width = qkv.shape[0], qkv.shape[1] // 3
    blocks, heads = rows // BLOCK, width // HEAD_DIM
    return pl.pallas_call(
        functools.partial(forward_kernel, per_chunk, heads // 2),
        grid_spec=pltpu.PrefetchScalarGridSpec(
            num_scalar_prefetch=1,
            grid=(blocks,),
            in_specs=[
                pl.BlockSpec((BLOCK, width), lambda i, info: (place(i, info[2, 0], per_chunk), 0)),
                pl.BlockSpec((rows, width), lambda i, info: (0, 1)),
                pl.BlockSpec((rows, width), lambda i, info: (0, 2)),
                pl.BlockSpec((rows, 1), lambda i, info: (0, 0)),
                pl.BlockSpec((blocks, 1, BLOCK), lambda i, info: (0, 0, 0)),
            ],
            out_specs=[
                pl.BlockSpec((BLOCK, width), lambda i, info: (place(i, info[2, 0], per_chunk), 0)),
                pl.BlockSpec((1, heads, BLOCK), lambda i, info: (i, 0, 0)),
            ],
            scratch_shapes=[
                pltpu.VMEM((width, BLOCK), f32),
                pltpu.VMEM((heads, 1, BLOCK), f32),
                pltpu.VMEM((heads, 1, BLOCK), f32),
            ],
        ),
        out_shape=[
            jax.ShapeDtypeStruct((rows, width), bf16),
            jax.ShapeDtypeStruct((blocks, heads, BLOCK), f32),
        ],
        name="attention_forward",
    )(info, qkv, qkv, qkv, ids_col, ids_row)


def backward_kernel(
    per_chunk, pairs, info, q_ref, k_ref, v_ref, do_ref, o_ref, lse_ref, idc_ref, idr_ref,
    out_ref, delta_ref, dq_acc, dk_acc, dv_acc,
):
    j = pl.program_id(0)
    blocks = pl.num_programs(0)
    me = info[2, 0]
    width = 128 * pairs

    @pl.when(j == 0)
    def _():
        dq_acc[...] = jnp.zeros_like(dq_acc)

        def fill(i, carry):
            at = pl.multiple_of(place(i, me, per_chunk) * BLOCK, BLOCK)
            for p in range(pairs):
                cols = slice(p * 128, (p + 1) * 128)
                prod = (do_ref[pl.ds(at, BLOCK), cols].astype(f32) * o_ref[pl.ds(at, BLOCK), cols].astype(f32)).T
                for w in range(2):
                    h = 2 * p + w
                    delta_ref[i, h : h + 1, :] = jnp.sum(
                        prod[w * HEAD_DIM : (w + 1) * HEAD_DIM], axis=0, keepdims=True
                    )
            return carry

        lax.fori_loop(0, blocks, fill, 0)

    dk_acc[...] = jnp.zeros_like(dk_acc)
    dv_acc[...] = jnp.zeros_like(dv_acc)
    ids_k = idc_ref[pl.ds(pl.multiple_of(j * BLOCK, BLOCK), BLOCK), :]

    def step(i, carry):
        at = pl.multiple_of(place(i, me, per_chunk) * BLOCK, BLOCK)
        same = ids_k == idr_ref[pl.ds(i, 1)][0]
        for p in range(pairs):
            cols = slice(p * 128, (p + 1) * 128)
            k_pair, v_pair = k_ref[:, cols], v_ref[:, cols]
            q_pair, do_pair = q_ref[pl.ds(at, BLOCK), cols], do_ref[pl.ds(at, BLOCK), cols]
            for w in range(2):
                h = 2 * p + w
                q_one, do_one = head_only(q_pair, w), head_only(do_pair, w)
                t = nt(k_pair, q_one) * SCALE_LOG2 - lse_ref[i, h : h + 1, :]
                e = jnp.exp2(jnp.where(same, t, MASKED))
                ds = (e * (nt(v_pair, do_one) - delta_ref[i, h : h + 1, :])).astype(bf16)
                dv_acc[:, cols] += nn(e.astype(bf16), do_one)
                dk_acc[:, cols] += nn(ds, q_one)
                dq_acc[pl.ds(at, BLOCK), cols] += tn(ds, head_only(k_pair, w))
        return carry

    lax.fori_loop(info[0, j], info[1, j], step, 0)
    mine = pl.multiple_of(place(j, me, per_chunk) * BLOCK, BLOCK)
    out_ref[pl.ds(mine, BLOCK), width : 2 * width] = (dk_acc[...] * SCALE).astype(bf16)
    out_ref[pl.ds(mine, BLOCK), 2 * width : 3 * width] = dv_acc[...].astype(bf16)

    @pl.when(j == blocks - 1)
    def _():
        out_ref[:, 0:width] = (dq_acc[...] * SCALE).astype(bf16)


def attention_backward(info, qkv, do, o, lse, ids_col, ids_row, per_chunk):
    rows, width = o.shape
    blocks, heads = rows // BLOCK, width // HEAD_DIM
    return pl.pallas_call(
        functools.partial(backward_kernel, per_chunk, heads // 2),
        grid_spec=pltpu.PrefetchScalarGridSpec(
            num_scalar_prefetch=1,
            grid=(blocks,),
            in_specs=[
                pl.BlockSpec((rows, width), lambda i, info: (0, 0)),
                pl.BlockSpec((BLOCK, width), lambda i, info: (place(i, info[2, 0], per_chunk), 1)),
                pl.BlockSpec((BLOCK, width), lambda i, info: (place(i, info[2, 0], per_chunk), 2)),
                pl.BlockSpec((rows, width), lambda i, info: (0, 0)),
                pl.BlockSpec((rows, width), lambda i, info: (0, 0)),
                pl.BlockSpec((blocks, heads, BLOCK), lambda i, info: (0, 0, 0)),
                pl.BlockSpec((rows, 1), lambda i, info: (0, 0)),
                pl.BlockSpec((blocks, 1, BLOCK), lambda i, info: (0, 0, 0)),
            ],
            out_specs=pl.BlockSpec((rows, 3 * width), lambda i, info: (0, 0)),
            scratch_shapes=[
                pltpu.VMEM((blocks, heads, BLOCK), f32),
                pltpu.VMEM((rows, width), f32),
                pltpu.VMEM((BLOCK, width), f32),
                pltpu.VMEM((BLOCK, width), f32),
            ],
        ),
        out_shape=jax.ShapeDtypeStruct((rows, 3 * width), bf16),
        name="attention_backward",
    )(info, qkv, qkv, qkv, do, o, lse, ids_col, ids_row)


def spans(ids, me):
    blocks = ids.shape[0] // BLOCK
    per_block = ids.reshape(blocks, BLOCK)
    low = jnp.sum(ids[None, :] < per_block[:, :1], axis=1) // BLOCK
    high = (jnp.sum(ids[None, :] <= per_block[:, -1:], axis=1) + BLOCK - 1) // BLOCK
    return jnp.stack([low, high, jnp.full((blocks,), me)]).astype(jnp.int32)


def swap(value, axis, mask):
    size = lax.axis_size(axis)
    return lax.ppermute(value, axis, [(i, i ^ mask) for i in range(size)])


def bits(size):
    return [1 << b for b in range(size.bit_length() - 1)]


def gather_relative(value, axis):
    held = {0: value}
    for bit in reversed(bits(lax.axis_size(axis))):
        held.update({k | bit: swap(v, axis, bit) for k, v in list(held.items())})
    return [held[k] for k in range(len(held))]


def gather_stacked(value, axis):
    for bit in reversed(bits(lax.axis_size(axis))):
        value = jnp.concatenate([value, swap(value, axis, bit)])
    return value


def flipped(index, size):
    flags = bits(size)
    return sum(lax.bitwise_and(index // bit, 1) * mirror for bit, mirror in zip(flags, reversed(flags)))


def trade(pieces, axis):
    return [pieces[0]] + [swap(pieces[k], axis, k) for k in range(1, len(pieces))]


def to_absolute(pieces, me):
    stacked = jnp.stack(pieces)
    return [lax.dynamic_index_in_dim(stacked, lax.bitwise_xor(me, c), 0, False) for c in range(len(pieces))]


def halve(value, axis, dtype):
    me, size = lax.axis_index(axis), lax.axis_size(axis)
    count = size
    for bit in bits(size):
        value = value.reshape((count // 2, 2) + value.shape[1:])
        mine = lax.rem(me // bit, 2)
        give = lax.dynamic_index_in_dim(value, 1 - mine, 1, False).astype(dtype)
        keep = lax.dynamic_index_in_dim(value, mine, 1, False)
        value = keep + swap(give, axis, bit).astype(f32)
        count //= 2
    return value[0]


def normalize(values, gain, shift):
    average = jnp.mean(values, axis=-1, keepdims=True)
    centered = values - average
    inverse = lax.rsqrt(jnp.mean(centered * centered, axis=-1, keepdims=True) + EPSILON)
    normed = centered * inverse
    return normed * gain + shift, normed, inverse


def normalize_back(upstream, normed, inverse, gain):
    scaled = upstream * gain
    plain = jnp.mean(scaled, axis=-1, keepdims=True)
    cross = jnp.mean(scaled * normed, axis=-1, keepdims=True)
    result = inverse * (scaled - plain - normed * cross)
    return result, jnp.sum(upstream * normed, axis=0), jnp.sum(upstream, axis=0)


def shards(
    tokens, time_feat, cotangent, segment_ids, time_weight, time_bias, query_weight, query_bias, key_weight,
    value_weight, value_bias, output_weight, output_bias, mixing_gain, mixing_bias, up_weight, up_bias,
    down_weight, down_bias, final_gain, final_bias,
):
    me_dp, me = lax.axis_index("dp"), lax.axis_index("ctx")
    dp, ctx = lax.axis_size("dp"), lax.axis_size("ctx")
    devices = dp * ctx
    piece, width = tokens.shape[1], tokens.shape[2]
    hidden = up_weight.shape[1]
    own, ratio = width // devices, hidden // width
    cols = width // ctx
    per_chunk = piece // BLOCK
    tokens, cotangent, ids = tokens[0], cotangent[0], segment_ids[0]

    second = lax.all_gather(jnp.concatenate([up_weight, output_weight], axis=1), BOTH, axis=0, tiled=True)
    down_full = lax.all_gather(down_weight, BOTH, axis=0, tiled=True)
    up_full, output_full = second[:, :hidden], second[:, hidden:]

    token_chunks = gather_relative(tokens, "ctx")
    vectors = [
        time_bias, query_bias, value_bias, output_bias, mixing_gain, mixing_bias, down_bias, final_gain, final_bias
    ]
    small = jnp.concatenate([jnp.stack(vectors), up_bias.reshape(ratio, own)]).T
    small = jnp.pad(small, ((0, 0), (0, 128 - small.shape[1])))
    pieces = []
    for k in range(ctx):
        at = lax.bitwise_xor(me, k) * cols
        parts = [
            lax.dynamic_slice_in_dim(w, at, cols, 1) for w in (query_weight, key_weight, value_weight, time_weight)
        ]
        pieces.append(jnp.concatenate(parts + [small], axis=1))
    first = jnp.concatenate(to_absolute(trade(pieces, "ctx"), me))
    first = gather_stacked(first[None], "dp")
    first = jnp.concatenate(
        [
            lax.dynamic_index_in_dim(first, flipped(lax.bitwise_xor(me_dp, c), dp), 0, False)
            for c in range(dp)
        ]
    )
    qkv_weight = first[:, : 3 * cols]
    table = first[:, 4 * cols :].astype(f32).T
    time_shift_bias, query_shift, value_shift, output_shift, gain_one, bias_one, down_shift, gain_two, bias_two = [
        table[n] for n in range(len(vectors))
    ]
    up_shift = table[len(vectors) : len(vectors) + ratio].reshape(ratio, devices, own).transpose(1, 0, 2).reshape(hidden)
    shift_cols = trade([nn(time_feat, first[:, 3 * cols : 4 * cols])] * ctx, "ctx")
    time_shift = jnp.concatenate(to_absolute(shift_cols, me), axis=1) + time_shift_bias
    qkv_shift = jnp.concatenate(
        [
            lax.dynamic_slice_in_dim(query_shift, me * cols, cols),
            jnp.zeros((cols,), f32),
            lax.dynamic_slice_in_dim(value_shift, me * cols, cols),
        ]
    )
    start_row = (jnp.concatenate(token_chunks).astype(f32) + time_shift).astype(bf16)
    residual_in = tokens.astype(f32) + time_shift
    qkv = (nn(start_row, qkv_weight) + qkv_shift).astype(bf16)

    info = spans(ids, me)
    ids_col, ids_row = ids.reshape(-1, 1), ids.reshape(-1, 1, BLOCK)
    mixed, logsum = attention_forward(info, qkv, ids_col, ids_row, per_chunk)
    returned = trade([mixed[k * piece : (k + 1) * piece] for k in range(ctx)], "ctx")
    attended = jnp.concatenate(to_absolute(returned, me), axis=1)

    branch = nn(attended, output_full) + output_shift
    hidden_one, normed_one, inverse_one = normalize(residual_in + branch, gain_one, bias_one)
    hidden_low = hidden_one.astype(bf16)
    pre_gelu = nn(hidden_low, up_full) + up_shift
    share = 0.5 * (1.0 + lax.erf(pre_gelu * 0.5**0.5))
    activated = (pre_gelu * share).astype(bf16)
    slope = (share + pre_gelu * jnp.exp(-0.5 * pre_gelu * pre_gelu) * 0.3989422804014327).astype(bf16)
    activated, slope = lax.optimization_barrier((activated, slope))
    feed_out = nn(activated, down_full) + down_shift
    result, normed_two, inverse_two = normalize(hidden_one + feed_out, gain_two, bias_two)
    layer_out = result.astype(bf16)

    upstream = cotangent.astype(f32)
    grad_two, gain_two_grad, bias_two_grad = normalize_back(upstream, normed_two, inverse_two, gain_two)
    grad_feed = grad_two.astype(bf16)
    down_grad = tn(activated, grad_feed).astype(bf16)
    down_shift_grad = jnp.sum(grad_feed.astype(f32), axis=0)
    grad_inner = (nt(grad_feed, down_full) * slope.astype(f32)).astype(bf16)
    up_grad = tn(hidden_low, grad_inner).astype(bf16)
    up_shift_grad = jnp.sum(grad_inner.astype(f32), axis=0)
    grad_hidden = grad_two + nt(grad_inner, up_full)
    grad_one, gain_one_grad, bias_one_grad = normalize_back(grad_hidden, normed_one, inverse_one, gain_one)
    grad_branch = grad_one.astype(bf16)
    output_grad = tn(attended, grad_branch).astype(bf16)
    output_shift_grad = jnp.sum(grad_branch.astype(f32), axis=0)
    down_blocks = down_grad.reshape(devices, ratio, own, width)
    vector_grads = jnp.stack(
        [output_shift_grad, gain_one_grad, bias_one_grad, down_shift_grad, gain_two_grad, bias_two_grad]
    )
    up_shift_grad = up_shift_grad.reshape(devices, ratio, own).transpose(1, 0, 2).reshape(ratio, width)
    vector_grads = jnp.concatenate([vector_grads, up_shift_grad])
    vector_grads = jnp.pad(vector_grads, ((0, 128 - vector_grads.shape[0]), (0, 0))).T.astype(bf16)
    packed = jnp.concatenate(
        [up_grad] + [down_blocks[:, n].reshape(width, width) for n in range(ratio)] + [output_grad, vector_grads],
        axis=1,
    )
    packed = lax.psum_scatter(packed, BOTH, scatter_dimension=0, tiled=True).astype(f32)
    up_weight_grad = packed[:, :hidden]
    down_weight_grad = jnp.concatenate(
        [packed[:, hidden + n * width : hidden + (n + 1) * width] for n in range(ratio)], axis=0
    )
    output_weight_grad = packed[:, 2 * hidden : 2 * hidden + width]
    vector_grads = packed[:, 2 * hidden + width :].T
    output_bias_grad, mixing_gain_grad, mixing_bias_grad, down_bias_grad, final_gain_grad, final_bias_grad = [
        vector_grads[n] for n in range(6)
    ]
    up_bias_grad = vector_grads[6 : 6 + ratio].reshape(ratio * own)

    grad_attended = nt(grad_branch, output_full).astype(bf16)
    pieces = [lax.dynamic_slice_in_dim(grad_attended, lax.bitwise_xor(me, k) * cols, cols, 1) for k in range(ctx)]
    grad_mixed = jnp.concatenate(trade(pieces, "ctx"))
    grad_qkv = attention_backward(info, qkv, grad_mixed, mixed, logsum, ids_col, ids_row, per_chunk)

    partial = {}
    for k in reversed(range(ctx)):
        partial[k] = nt(grad_qkv[k * piece : (k + 1) * piece], qkv_weight)
    for bit in bits(ctx):
        for k in [k for k in partial if k & bit]:
            partial[k ^ bit] = partial[k ^ bit] + swap(partial.pop(k).astype(bf16), "ctx", bit).astype(f32)
    tokens_grad = (grad_one + partial[0]).astype(bf16)

    qkv_grad = tn(start_row, grad_qkv)
    qkv_sum = jnp.sum(grad_qkv.astype(f32), axis=0)
    row_sum = jnp.sum(grad_one, axis=0, keepdims=True) + lax.dot_general(
        qkv_sum[None],
        qkv_weight.astype(f32),
        (((1,), (1,)), ((), ())),
        precision=lax.Precision.HIGHEST,
        preferred_element_type=f32,
    )
    message = jnp.concatenate(
        [row_sum, qkv_sum[None, :cols], qkv_sum[None, 2 * cols :], time_feat.astype(f32)], axis=1
    )
    message = gather_stacked(gather_stacked(message, "dp"), "ctx").reshape(ctx, dp, -1)
    mine = (me_dp * ctx + me) * own
    row_sums = jnp.sum(message[:, :, :width], axis=0)
    time_weight_grad = lax.dot_general(
        lax.dynamic_slice_in_dim(message[0, :, width + 2 * cols :], mine, own, 1),
        row_sums,
        (((0,), (0,)), ((), ())),
        precision=lax.Precision.HIGHEST,
        preferred_element_type=f32,
    )
    time_bias_grad = lax.dynamic_slice_in_dim(jnp.sum(row_sums, axis=0), mine, own)
    sums = jnp.sum(message[:, :, width : width + 2 * cols], axis=1)
    sums = lax.dynamic_index_in_dim(sums, flipped(lax.bitwise_xor(mine // cols, me), ctx), 0, False)
    query_bias_grad = lax.dynamic_slice_in_dim(sums[:cols], lax.rem(mine, cols), own)
    value_bias_grad = lax.dynamic_slice_in_dim(sums[cols:], lax.rem(mine, cols), own)

    summed = halve(qkv_grad.reshape(dp, ctx * own, 3 * cols), "dp", bf16).reshape(ctx, own, 3 * cols)
    blocks_out = to_absolute(
        trade([lax.dynamic_index_in_dim(summed, lax.bitwise_xor(me, k), 0, False) for k in range(ctx)], "ctx"), me
    )
    query_weight_grad, key_weight_grad, value_weight_grad = [
        jnp.concatenate([block[:, n * cols : (n + 1) * cols] for block in blocks_out], axis=1) for n in range(3)
    ]

    return (
        layer_out[None],
        tokens_grad[None],
        time_weight_grad,
        time_bias_grad,
        query_weight_grad,
        query_bias_grad,
        key_weight_grad,
        value_weight_grad,
        value_bias_grad,
        output_weight_grad,
        output_bias_grad,
        mixing_gain_grad,
        mixing_bias_grad,
        up_weight_grad,
        up_bias_grad,
        down_weight_grad,
        down_bias_grad,
        final_gain_grad,
        final_bias_grad,
    )


def solution(mesh):
    rows, split_rows, split = P("dp", "ctx", None), P(BOTH, None), P(BOTH)
    return jax.shard_map(
        shards,
        mesh=mesh,
        in_specs=(
            rows, P("dp", None), rows, P("dp", None), split_rows, split, split_rows, split, split_rows, split_rows,
            split, split_rows, split, split, split, split_rows, split, split_rows, split, split, split,
        ),
        out_specs=(
            rows, rows, split_rows, split, split_rows, split, split_rows, split_rows, split, split_rows, split, split,
            split, split_rows, split, split_rows, split, split, split,
        ),
        check_vma=False,
    )
```

```python
import functools

import jax
import jax.numpy as jnp
from jax import lax
from jax.experimental import pallas as pl
from jax.experimental.pallas import tpu as pltpu
from jax.sharding import PartitionSpec as P

HEAD_DIM = 64
BLOCK = 256
MASKED = -1e30
EPSILON = 1e-05
SCALE = HEAD_DIM**-0.5
SCALE_LOG2 = SCALE * 1.4426950408889634
BOTH = ("dp", "ctx")
f32, bf16 = jnp.float32, jnp.bfloat16


def nn(left, right):
    return jnp.dot(left, right, preferred_element_type=f32)


def tn(left, right):
    return lax.dot_general(left, right, (((0,), (0,)), ((), ())), preferred_element_type=f32)


def nt(left, right):
    return lax.dot_general(left, right, (((1,), (1,)), ((), ())), preferred_element_type=f32)


def head_only(pair, which):
    lane = lax.broadcasted_iota(jnp.int32, pair.shape, 1)
    keep = (lane < HEAD_DIM) if which == 0 else (lane >= HEAD_DIM)
    return jnp.where(keep, pair, jnp.zeros_like(pair))


def place(block, me, per_chunk):
    return lax.bitwise_xor(block // per_chunk, me) * per_chunk + lax.rem(block, per_chunk)


def forward_kernel(per_chunk, pairs, info, qkv_ref, idc_ref, idr_ref, o_ref, lse_ref, o_acc, m_acc, l_acc):
    i = pl.program_id(0)
    me = info[2, 0]
    m_acc[...] = jnp.full_like(m_acc, MASKED)
    l_acc[...] = jnp.zeros_like(l_acc)
    o_acc[...] = jnp.zeros_like(o_acc)
    ids_q = idr_ref[pl.ds(i, 1)][0]
    here = pl.multiple_of(place(i, me, per_chunk) * BLOCK, BLOCK)

    def step(j, carry):
        at = pl.multiple_of(place(j, me, per_chunk) * BLOCK, BLOCK)
        same = idc_ref[pl.ds(pl.multiple_of(j * BLOCK, BLOCK), BLOCK), :] == ids_q
        for p in range(pairs):
            q_pair = qkv_ref[pl.ds(here, BLOCK), (3 * p) * 128 : (3 * p + 1) * 128]
            k_pair = qkv_ref[pl.ds(at, BLOCK), (3 * p + 1) * 128 : (3 * p + 2) * 128]
            v_pair = qkv_ref[pl.ds(at, BLOCK), (3 * p + 2) * 128 : (3 * p + 3) * 128]
            for w in range(2):
                h = 2 * p + w
                t = jnp.where(same, nt(k_pair, head_only(q_pair, w)) * SCALE_LOG2, MASKED)
                m_old = m_acc[h]
                m_new = jnp.maximum(m_old, jnp.max(t, axis=0, keepdims=True))
                alpha = jnp.exp2(m_old - m_new)
                e = jnp.exp2(t - m_new)
                l_acc[h] = l_acc[h] * alpha + jnp.sum(e, axis=0, keepdims=True)
                m_acc[h] = m_new
                rows = slice(h * HEAD_DIM, (h + 1) * HEAD_DIM)
                o_acc[rows] = o_acc[rows] * alpha + tn(v_pair, e.astype(bf16))[w * HEAD_DIM : (w + 1) * HEAD_DIM]
        return carry

    lax.fori_loop(info[0, i], info[1, i], step, 0)
    for p in range(pairs):
        parts = []
        for w in range(2):
            h = 2 * p + w
            parts.append(o_acc[h * HEAD_DIM : (h + 1) * HEAD_DIM] / l_acc[h])
            lse_ref[0, h : h + 1, :] = m_acc[h] + jnp.log2(l_acc[h])
        o_ref[:, p * 128 : (p + 1) * 128] = jnp.concatenate(parts, axis=0).T.astype(bf16)


def attention_forward(info, qkv, ids_col, ids_row, per_chunk):
    rows, width = qkv.shape[0], qkv.shape[1] // 3
    blocks, heads = rows // BLOCK, width // HEAD_DIM
    return pl.pallas_call(
        functools.partial(forward_kernel, per_chunk, heads // 2),
        grid_spec=pltpu.PrefetchScalarGridSpec(
            num_scalar_prefetch=1,
            grid=(blocks,),
            in_specs=[
                pl.BlockSpec((rows, 3 * width), lambda i, info: (0, 0)),
                pl.BlockSpec((rows, 1), lambda i, info: (0, 0)),
                pl.BlockSpec((blocks, 1, BLOCK), lambda i, info: (0, 0, 0)),
            ],
            out_specs=[
                pl.BlockSpec((BLOCK, width), lambda i, info: (place(i, info[2, 0], per_chunk), 0)),
                pl.BlockSpec((1, heads, BLOCK), lambda i, info: (i, 0, 0)),
            ],
            scratch_shapes=[
                pltpu.VMEM((width, BLOCK), f32),
                pltpu.VMEM((heads, 1, BLOCK), f32),
                pltpu.VMEM((heads, 1, BLOCK), f32),
            ],
        ),
        out_shape=[
            jax.ShapeDtypeStruct((rows, width), bf16),
            jax.ShapeDtypeStruct((blocks, heads, BLOCK), f32),
        ],
        cost_estimate=pl.CostEstimate(flops=30 * 10**9, bytes_accessed=6 * rows * width, transcendentals=10**7),
        name="attention_forward",
    )(info, qkv, ids_col, ids_row)


def backward_kernel(
    per_chunk, first, info, q_ref, k_ref, v_ref, do_ref, o_ref, lse_ref, idc_ref, idr_ref,
    out_ref, delta_ref, dq_acc, dk_acc, dv_acc,
):
    j = pl.program_id(0)
    blocks = pl.num_programs(0)
    me = info[2, 0]

    @pl.when(j == 0)
    def _():
        dq_acc[...] = jnp.zeros_like(dq_acc)

        def fill(i, carry):
            at = pl.multiple_of(place(i, me, per_chunk) * BLOCK, BLOCK)
            prod = (do_ref[pl.ds(at, BLOCK), :].astype(f32) * o_ref[pl.ds(at, BLOCK), :].astype(f32)).T
            for w in range(2):
                delta_ref[i, w : w + 1, :] = jnp.sum(prod[w * HEAD_DIM : (w + 1) * HEAD_DIM], axis=0, keepdims=True)
            return carry

        lax.fori_loop(0, blocks, fill, 0)

    dk_acc[...] = jnp.zeros_like(dk_acc)
    dv_acc[...] = jnp.zeros_like(dv_acc)
    ids_k = idc_ref[pl.ds(pl.multiple_of(j * BLOCK, BLOCK), BLOCK), :]

    def step(i, carry):
        at = pl.multiple_of(place(i, me, per_chunk) * BLOCK, BLOCK)
        same = ids_k == idr_ref[pl.ds(i, 1)][0]
        k_pair, v_pair = k_ref[...], v_ref[...]
        q_pair, do_pair = q_ref[pl.ds(at, BLOCK), :], do_ref[pl.ds(at, BLOCK), :]
        dv, dk, dq = [], [], []
        for w in range(2):
            q_one, do_one = head_only(q_pair, w), head_only(do_pair, w)
            t = nt(k_pair, q_one) * SCALE_LOG2 - lse_ref[i, first + w : first + w + 1, :]
            e = jnp.exp2(jnp.where(same, t, MASKED))
            ds = (e * (nt(v_pair, do_one) - delta_ref[i, w : w + 1, :])).astype(bf16)
            dv.append(nn(e.astype(bf16), do_one))
            dk.append(nn(ds, q_one))
            dq.append(tn(ds, head_only(k_pair, w)))
        dv_acc[...] += dv[0] + dv[1]
        dk_acc[...] += dk[0] + dk[1]
        dq_acc[pl.ds(at, BLOCK), :] += dq[0] + dq[1]
        return carry

    lax.fori_loop(info[0, j], info[1, j], step, 0)
    mine = pl.multiple_of(place(j, me, per_chunk) * BLOCK, BLOCK)
    out_ref[pl.ds(mine, BLOCK), 128:256] = (dk_acc[...] * SCALE).astype(bf16)
    out_ref[pl.ds(mine, BLOCK), 256:384] = dv_acc[...].astype(bf16)

    @pl.when(j == blocks - 1)
    def _():
        out_ref[:, 0:128] = (dq_acc[...] * SCALE).astype(bf16)


def attention_backward(pair, info, qkv, do, o, lse, ids_col, ids_row, per_chunk):
    rows, width = o.shape
    blocks, heads = rows // BLOCK, width // HEAD_DIM
    return pl.pallas_call(
        functools.partial(backward_kernel, per_chunk, 2 * pair),
        grid_spec=pltpu.PrefetchScalarGridSpec(
            num_scalar_prefetch=1,
            grid=(blocks,),
            in_specs=[
                pl.BlockSpec((rows, 128), lambda i, info: (0, 3 * pair)),
                pl.BlockSpec((BLOCK, 128), lambda i, info: (place(i, info[2, 0], per_chunk), 3 * pair + 1)),
                pl.BlockSpec((BLOCK, 128), lambda i, info: (place(i, info[2, 0], per_chunk), 3 * pair + 2)),
                pl.BlockSpec((rows, 128), lambda i, info: (0, pair)),
                pl.BlockSpec((rows, 128), lambda i, info: (0, pair)),
                pl.BlockSpec((blocks, heads, BLOCK), lambda i, info: (0, 0, 0)),
                pl.BlockSpec((rows, 1), lambda i, info: (0, 0)),
                pl.BlockSpec((blocks, 1, BLOCK), lambda i, info: (0, 0, 0)),
            ],
            out_specs=pl.BlockSpec((rows, 384), lambda i, info: (0, 0)),
            scratch_shapes=[
                pltpu.VMEM((blocks, 2, BLOCK), f32),
                pltpu.VMEM((rows, 128), f32),
                pltpu.VMEM((BLOCK, 128), f32),
                pltpu.VMEM((BLOCK, 128), f32),
            ],
        ),
        out_shape=jax.ShapeDtypeStruct((rows, 384), bf16),
        cost_estimate=pl.CostEstimate(flops=25 * 10**9, bytes_accessed=8 * rows * 128, transcendentals=10**7),
        name="attention_backward",
    )(info, qkv, qkv, qkv, do, o, lse, ids_col, ids_row)


def spans(ids, me):
    blocks = ids.shape[0] // BLOCK
    per_block = ids.reshape(blocks, BLOCK)
    low = jnp.sum(ids[None, :] < per_block[:, :1], axis=1) // BLOCK
    high = (jnp.sum(ids[None, :] <= per_block[:, -1:], axis=1) + BLOCK - 1) // BLOCK
    return jnp.stack([low, high, jnp.full((blocks,), me.astype(low.dtype))]).astype(jnp.int32)


def own_index(axis):
    return lax.axis_index(axis).astype(jnp.uint32)


def swap(value, axis, mask):
    size = lax.axis_size(axis)
    return lax.ppermute(value, axis, [(i, i ^ mask) for i in range(size)])


def bits(size):
    return [1 << b for b in range(size.bit_length() - 1)]


def gather_relative(value, axis):
    held = {0: value}
    for bit in reversed(bits(lax.axis_size(axis))):
        held.update({k | bit: swap(v, axis, bit) for k, v in list(held.items())})
    return [held[k] for k in range(len(held))]


def gather_stacked(value, axis):
    for bit in reversed(bits(lax.axis_size(axis))):
        value = jnp.concatenate([value, swap(value, axis, bit)])
    return value


def flipped(index, size):
    flags = bits(size)
    return sum(((index >> n) & 1) << (len(flags) - 1 - n) for n in range(len(flags)))


def trade(pieces, axis):
    return [pieces[0]] + [swap(pieces[k], axis, k) for k in range(1, len(pieces))]


def to_absolute(pieces, me):
    stacked = jnp.stack(pieces)
    return [lax.dynamic_index_in_dim(stacked, (me ^ c), 0, False) for c in range(len(pieces))]


class Halving:
    def __init__(self, names, shape):
        self.me = {n: (own_index(n[0]) >> (n[1].bit_length() - 1)) & 1 for n in names}
        self.names, self.terms, self.fixed, self.shape = list(names), [], {}, shape

    def cut(self, term, chosen):
        array, names, part = term
        starts, sizes = [], []
        for n in names:
            starts.append(chosen.get(n, jnp.uint32(0)))
            sizes.append(1 if n in chosen else 2)
        for low, high in part:
            starts.append(jnp.uint32(low))
            sizes.append(high - low)
        left = [2 for n in names if n not in chosen]
        return lax.dynamic_slice(array, starts, sizes).reshape(left + [h - l for l, h in part])

    def total(self, chosen):
        groups = []
        for group in self.terms:
            pieces = [self.cut(t, chosen).astype(f32) for t in group]
            groups.append(pieces[0] if len(pieces) == 1 else jnp.concatenate(pieces, axis=-1))
        return sum(groups[1:], groups[0])

    def outgoing(self, name):
        return self.total({**self.fixed, name: 1 - self.me[name]}).astype(bf16)

    def arrived(self, name, value):
        self.fixed[name] = self.me[name]
        names = [n for n in self.names if n not in self.fixed]
        self.terms.append([(value, names, [(0, d) for d in self.shape])])

    def exchange(self, name):
        self.arrived(name, swap(self.outgoing(name), *name))

    def result(self):
        return self.total(self.fixed)


def normalize(values, gain, shift):
    average = jnp.mean(values, axis=-1, keepdims=True)
    centered = values - average
    inverse = lax.rsqrt(jnp.mean(centered * centered, axis=-1, keepdims=True) + EPSILON)
    normed = centered * inverse
    return normed * gain + shift, normed, inverse


def normalize_back(upstream, normed, inverse, gain):
    scaled = upstream * gain
    plain = jnp.mean(scaled, axis=-1, keepdims=True)
    cross = jnp.mean(scaled * normed, axis=-1, keepdims=True)
    result = inverse * (scaled - plain - normed * cross)
    return result, jnp.sum(upstream * normed, axis=0), jnp.sum(upstream, axis=0)


def shards(
    tokens, time_feat, cotangent, segment_ids, time_weight, time_bias, query_weight, query_bias, key_weight,
    value_weight, value_bias, output_weight, output_bias, mixing_gain, mixing_bias, up_weight, up_bias,
    down_weight, down_bias, final_gain, final_bias,
):
    me_dp, me = own_index("dp"), own_index("ctx")
    dp, ctx = lax.axis_size("dp"), lax.axis_size("ctx")
    devices = dp * ctx
    piece, width = tokens.shape[1], tokens.shape[2]
    hidden = up_weight.shape[1]
    own, ratio = width // devices, hidden // width
    cols = width // ctx
    per_chunk = piece // BLOCK
    tokens, cotangent, ids = tokens[0], cotangent[0], segment_ids[0]

    second = lax.all_gather(jnp.concatenate([up_weight, output_weight], axis=1), BOTH, axis=0, tiled=True)
    down_full = lax.all_gather(down_weight, BOTH, axis=0, tiled=True)
    up_full, output_full = second[:, :hidden], second[:, hidden:]

    token_chunks = gather_relative(tokens, "ctx")
    vectors = [
        time_bias, query_bias, value_bias, output_bias, mixing_gain, mixing_bias, down_bias, final_gain, final_bias
    ]
    small = jnp.concatenate([jnp.stack(vectors), up_bias.reshape(ratio, own)]).T
    small = jnp.pad(small, ((0, 0), (0, 128 - small.shape[1])))
    pieces = []
    for k in range(ctx):
        at = (me ^ k) * cols
        parts = [
            lax.dynamic_slice_in_dim(w, at + p * 128, 128, 1)
            for p in range(cols // 128)
            for w in (query_weight, key_weight, value_weight)
        ] + [lax.dynamic_slice_in_dim(time_weight, at, cols, 1)]
        pieces.append(jnp.concatenate(parts + [small], axis=1))
    first = jnp.concatenate(to_absolute(trade(pieces, "ctx"), me))
    first = gather_stacked(first[None], "dp")
    first = jnp.concatenate(
        [
            lax.dynamic_index_in_dim(first, flipped((me_dp ^ c), dp), 0, False)
            for c in range(dp)
        ]
    )
    qkv_weight = first[:, : 3 * cols]
    table = first[:, 4 * cols :].astype(f32).T
    time_shift_bias, query_shift, value_shift, output_shift, gain_one, bias_one, down_shift, gain_two, bias_two = [
        table[n] for n in range(len(vectors))
    ]
    up_shift = table[len(vectors) : len(vectors) + ratio].reshape(ratio, devices, own).transpose(1, 0, 2).reshape(hidden)
    shift_cols = trade([nn(time_feat, first[:, 3 * cols : 4 * cols])] * ctx, "ctx")
    time_shift = jnp.concatenate(to_absolute(shift_cols, me), axis=1) + time_shift_bias
    qkv_shift = []
    for p in range(cols // 128):
        at = me * cols + p * 128
        qkv_shift.append(lax.dynamic_slice_in_dim(query_shift, at, 128))
        qkv_shift.append(jnp.zeros((128,), f32))
        qkv_shift.append(lax.dynamic_slice_in_dim(value_shift, at, 128))
    qkv_shift = jnp.concatenate(qkv_shift)
    start_row = (jnp.concatenate(token_chunks).astype(f32) + time_shift).astype(bf16)
    residual_in = tokens.astype(f32) + time_shift
    qkv = (nn(start_row, qkv_weight) + qkv_shift).astype(bf16)

    info = spans(ids, me)
    ids_col, ids_row = ids.reshape(-1, 1), ids.reshape(-1, 1, BLOCK)
    mixed, logsum = attention_forward(info, qkv, ids_col, ids_row, per_chunk)
    returned = trade([mixed[k * piece : (k + 1) * piece] for k in range(ctx)], "ctx")
    attended = jnp.concatenate(to_absolute(returned, me), axis=1)

    branch = nn(attended, output_full) + output_shift
    hidden_one, normed_one, inverse_one = normalize(residual_in + branch, gain_one, bias_one)
    hidden_low = hidden_one.astype(bf16)
    pre_gelu = nn(hidden_low, up_full) + up_shift
    share = 0.5 * (1.0 + lax.erf(pre_gelu * 0.5**0.5))
    activated = (pre_gelu * share).astype(bf16)
    slope = (share + pre_gelu * jnp.exp(-0.5 * pre_gelu * pre_gelu) * 0.3989422804014327).astype(bf16)
    activated, slope = lax.optimization_barrier((activated, slope))
    feed_out = nn(activated, down_full) + down_shift
    result, normed_two, inverse_two = normalize(hidden_one + feed_out, gain_two, bias_two)
    layer_out = result.astype(bf16)

    upstream = cotangent.astype(f32)
    grad_two, gain_two_grad, bias_two_grad = normalize_back(upstream, normed_two, inverse_two, gain_two)
    grad_feed = grad_two.astype(bf16)
    down_grad = tn(activated, grad_feed).astype(bf16)
    down_shift_grad = jnp.sum(grad_feed.astype(f32), axis=0)
    grad_inner = (nt(grad_feed, down_full) * slope.astype(f32)).astype(bf16)
    up_grad = tn(hidden_low, grad_inner).astype(bf16)
    up_shift_grad = jnp.sum(grad_inner.astype(f32), axis=0)
    grad_hidden = grad_two + nt(grad_inner, up_full)
    grad_one, gain_one_grad, bias_one_grad = normalize_back(grad_hidden, normed_one, inverse_one, gain_one)
    grad_branch = grad_one.astype(bf16)
    output_grad = tn(attended, grad_branch).astype(bf16)
    output_shift_grad = jnp.sum(grad_branch.astype(f32), axis=0)
    vector_grads = jnp.stack(
        [output_shift_grad, gain_one_grad, bias_one_grad, down_shift_grad, gain_two_grad, bias_two_grad]
    )
    up_shift_grad = up_shift_grad.reshape(devices, ratio, own).transpose(1, 0, 2).reshape(ratio, width)
    vector_grads = jnp.concatenate([vector_grads, up_shift_grad])
    vector_grads = jnp.pad(vector_grads, ((0, 128 - vector_grads.shape[0]), (0, 0))).T.astype(bf16)
    rest_grad = jnp.concatenate([output_grad, vector_grads], axis=1)

    dp_names, ctx_names = [("dp", b) for b in bits(dp)], [("ctx", b) for b in bits(ctx)]
    names = dp_names[::-1] + ctx_names[::-1]
    core, turn, rest = ctx_names[0], dp_names[:2] + ctx_names[1:], dp_names[2:]
    whole = {}
    for label, array, height in (("down", down_grad, ratio * own), ("up", up_grad, own), ("rest", rest_grad, own)):
        size = (height, array.shape[1])
        sums = Halving(names, size)
        sums.terms = [[(array.reshape([2] * len(names) + list(size)), names, [(0, d) for d in size])]]
        sums.exchange(core)
        whole[label] = [term[0] for term in sums.terms]

    def stream(parts, shape):
        sums = Halving(names, shape)
        sums.fixed = {core: sums.me[core]}
        sums.terms = [[(whole[l][n][0], whole[l][n][1], part) for l, part in parts] for n in range(2)]
        return sums

    most = 3 * hidden // 4
    streams = [
        stream([("up", [(0, own), (0, most)])], (own, most)),
        stream([("down", [(0, (ratio - 1) * own), (0, width)])], ((ratio - 1) * own, width)),
        stream(
            [
                ("up", [(0, own), (most, hidden)]),
                ("down", [((ratio - 1) * own, ratio * own), (0, width)]),
                ("rest", [(0, own), (0, width + 128)]),
            ],
            (own, hidden - most + 2 * width + 128),
        ),
    ]
    order = [turn[2:] + turn[:2], turn, turn[1:] + turn[:1]]

    grad_attended = nt(grad_branch, output_full).astype(bf16)
    pieces = [lax.dynamic_slice_in_dim(grad_attended, (me ^ k) * cols, cols, 1) for k in range(ctx)]
    grad_mixed = jnp.concatenate(trade(pieces, "ctx"))
    grads = []
    for stage in range(len(turn)):
        going = [s.outgoing(o[stage]) for s, o in zip(streams, order)]
        grad_mixed, grads, going = lax.optimization_barrier((grad_mixed, grads, going))
        for s, o, value in zip(streams, order, going):
            s.arrived(o[stage], swap(value, *o[stage]))
        if stage < cols // 128:
            grads.append(
                attention_backward(stage, info, qkv, grad_mixed, mixed, logsum, ids_col, ids_row, per_chunk)
            )
            grad_mixed, grads[-1] = lax.optimization_barrier((grad_mixed, grads[-1]))
    grad_qkv = jnp.concatenate(grads, axis=1)

    partial = {}
    for k in reversed(range(ctx)):
        partial[k] = nt(grad_qkv[k * piece : (k + 1) * piece], qkv_weight)
    for bit in bits(ctx):
        for k in [k for k in partial if k & bit]:
            partial[k ^ bit] = partial[k ^ bit] + swap(partial.pop(k).astype(bf16), "ctx", bit).astype(f32)
    tokens_grad = (grad_one + partial[0]).astype(bf16)

    for s, o in zip(streams, order):
        for name in rest:
            s.exchange(name)
    up_left, down_left, mixed_left = [s.result() for s in streams]
    up_weight_grad = jnp.concatenate([up_left, mixed_left[:, : hidden - most]], axis=1)
    mixed_left = mixed_left[:, hidden - most :]
    down_weight_grad = jnp.concatenate([down_left, mixed_left[:, :width]])
    output_weight_grad = mixed_left[:, width : 2 * width]
    vector_grads = mixed_left[:, 2 * width :].T
    output_bias_grad, mixing_gain_grad, mixing_bias_grad, down_bias_grad, final_gain_grad, final_bias_grad = [
        vector_grads[n] for n in range(6)
    ]
    up_bias_grad = vector_grads[6 : 6 + ratio].reshape(ratio * own)

    qkv_sum = jnp.sum(grad_qkv.astype(f32), axis=0)
    qkv_grad = tn(start_row, grad_qkv)
    row_sum = jnp.sum(grad_one, axis=0, keepdims=True) + lax.dot_general(
        qkv_sum[None],
        qkv_weight.astype(f32),
        (((1,), (1,)), ((), ())),
        precision=lax.Precision.HIGHEST,
        preferred_element_type=f32,
    )
    message = jnp.concatenate(
        [row_sum]
        + [qkv_sum[None, (3 * p + n) * 128 : (3 * p + n + 1) * 128] for n in (0, 2) for p in range(cols // 128)]
        + [time_feat.astype(f32)],
        axis=1,
    )
    message = gather_stacked(gather_stacked(message, "dp"), "ctx").reshape(ctx, dp, -1)
    mine = (me_dp * ctx + me) * own
    row_sums = jnp.sum(message[:, :, :width], axis=0)
    time_weight_grad = lax.dot_general(
        lax.dynamic_slice_in_dim(message[0, :, width + 2 * cols :], mine, own, 1),
        row_sums,
        (((0,), (0,)), ((), ())),
        precision=lax.Precision.HIGHEST,
        preferred_element_type=f32,
    )
    time_bias_grad = lax.dynamic_slice_in_dim(jnp.sum(row_sums, axis=0), mine, own)
    sums = jnp.sum(message[:, :, width : width + 2 * cols], axis=1)
    sums = lax.dynamic_index_in_dim(sums, flipped((mine // cols ^ me), ctx), 0, False)
    query_bias_grad = lax.dynamic_slice_in_dim(sums[:cols], mine % cols, own)
    value_bias_grad = lax.dynamic_slice_in_dim(sums[cols:], mine % cols, own)

    size = (ctx * own, 3 * cols)
    summed = Halving(dp_names[::-1], size)
    summed.terms = [
        [(qkv_grad.reshape([2] * len(dp_names) + list(size)), dp_names[::-1], [(0, d) for d in size])]
    ]
    for name in dp_names:
        summed.exchange(name)
    summed = summed.result().reshape(ctx, own, 3 * cols)
    blocks_out = to_absolute(
        trade([lax.dynamic_index_in_dim(summed, (me ^ k), 0, False) for k in range(ctx)], "ctx"), me
    )
    query_weight_grad, key_weight_grad, value_weight_grad = [
        jnp.concatenate(
            [
                block[:, (3 * p + n) * 128 : (3 * p + n + 1) * 128]
                for block in blocks_out
                for p in range(cols // 128)
            ],
            axis=1,
        )
        for n in range(3)
    ]
    return (
        layer_out[None],
        tokens_grad[None],
        time_weight_grad,
        time_bias_grad,
        query_weight_grad,
        query_bias_grad,
        key_weight_grad,
        value_weight_grad,
        value_bias_grad,
        output_weight_grad,
        output_bias_grad,
        mixing_gain_grad,
        mixing_bias_grad,
        up_weight_grad,
        up_bias_grad,
        down_weight_grad,
        down_bias_grad,
        final_gain_grad,
        final_bias_grad,
    )


def solution(mesh):
    rows, split_rows, split = P("dp", "ctx", None), P(BOTH, None), P(BOTH)
    return jax.shard_map(
        shards,
        mesh=mesh,
        in_specs=(
            rows, P("dp", None), rows, P("dp", None), split_rows, split, split_rows, split, split_rows, split_rows,
            split, split_rows, split, split, split, split_rows, split, split_rows, split, split, split,
        ),
        out_specs=(
            rows, rows, split_rows, split, split_rows, split, split_rows, split_rows, split, split_rows, split, split,
            split, split_rows, split, split_rows, split, split, split,
        ),
        check_vma=False,
    )
```

```python
import functools

import jax
import jax.numpy as jnp
from jax import lax
from jax.experimental import pallas as pl
from jax.experimental.pallas import tpu as pltpu
from jax.sharding import PartitionSpec as P

HEAD_DIM = 64
BLOCK = 256
MASKED = -1e30
EPSILON = 1e-05
SCALE = HEAD_DIM**-0.5
SCALE_LOG2 = SCALE * 1.4426950408889634
BOTH = ("dp", "ctx")
f32, bf16 = jnp.float32, jnp.bfloat16


def nn(left, right):
    return jnp.dot(left, right, preferred_element_type=f32)


def tn(left, right):
    return lax.dot_general(left, right, (((0,), (0,)), ((), ())), preferred_element_type=f32)


def nt(left, right):
    return lax.dot_general(left, right, (((1,), (1,)), ((), ())), preferred_element_type=f32)


def head_only(pair, which):
    lane = lax.broadcasted_iota(jnp.int32, pair.shape, 1)
    keep = (lane < HEAD_DIM) if which == 0 else (lane >= HEAD_DIM)
    return jnp.where(keep, pair, jnp.zeros_like(pair))


def place(block, me, per_chunk):
    return lax.bitwise_xor(block // per_chunk, me) * per_chunk + lax.rem(block, per_chunk)


def forward_kernel(per_chunk, pairs, info, qkv_ref, idc_ref, idr_ref, o_ref, lse_ref, o_acc, m_acc, l_acc):
    i = pl.program_id(0)
    me = info[2, 0]
    m_acc[...] = jnp.full_like(m_acc, MASKED)
    l_acc[...] = jnp.zeros_like(l_acc)
    o_acc[...] = jnp.zeros_like(o_acc)
    ids_q = idr_ref[pl.ds(i, 1)][0]
    here = pl.multiple_of(place(i, me, per_chunk) * BLOCK, BLOCK)

    def step(j, carry):
        at = pl.multiple_of(place(j, me, per_chunk) * BLOCK, BLOCK)
        same = idc_ref[pl.ds(pl.multiple_of(j * BLOCK, BLOCK), BLOCK), :] == ids_q
        for p in range(pairs):
            q_pair = qkv_ref[pl.ds(here, BLOCK), (3 * p) * 128 : (3 * p + 1) * 128]
            k_pair = qkv_ref[pl.ds(at, BLOCK), (3 * p + 1) * 128 : (3 * p + 2) * 128]
            v_pair = qkv_ref[pl.ds(at, BLOCK), (3 * p + 2) * 128 : (3 * p + 3) * 128]
            for w in range(2):
                h = 2 * p + w
                t = jnp.where(same, nt(k_pair, head_only(q_pair, w)) * SCALE_LOG2, MASKED)
                m_old = m_acc[h]
                m_new = jnp.maximum(m_old, jnp.max(t, axis=0, keepdims=True))
                alpha = jnp.exp2(m_old - m_new)
                e = jnp.exp2(t - m_new)
                l_acc[h] = l_acc[h] * alpha + jnp.sum(e, axis=0, keepdims=True)
                m_acc[h] = m_new
                rows = slice(h * HEAD_DIM, (h + 1) * HEAD_DIM)
                o_acc[rows] = o_acc[rows] * alpha + tn(v_pair, e.astype(bf16))[w * HEAD_DIM : (w + 1) * HEAD_DIM]
        return carry

    lax.fori_loop(info[0, i], info[1, i], step, 0)
    for p in range(pairs):
        parts = []
        for w in range(2):
            h = 2 * p + w
            parts.append(o_acc[h * HEAD_DIM : (h + 1) * HEAD_DIM] / l_acc[h])
            lse_ref[0, h : h + 1, :] = m_acc[h] + jnp.log2(l_acc[h])
        o_ref[:, p * 128 : (p + 1) * 128] = jnp.concatenate(parts, axis=0).T.astype(bf16)


def attention_forward(info, qkv, ids_col, ids_row, per_chunk):
    rows, width = qkv.shape[0], qkv.shape[1] // 3
    blocks, heads = rows // BLOCK, width // HEAD_DIM
    return pl.pallas_call(
        functools.partial(forward_kernel, per_chunk, heads // 2),
        grid_spec=pltpu.PrefetchScalarGridSpec(
            num_scalar_prefetch=1,
            grid=(blocks,),
            in_specs=[
                pl.BlockSpec((rows, 3 * width), lambda i, info: (0, 0)),
                pl.BlockSpec((rows, 1), lambda i, info: (0, 0)),
                pl.BlockSpec((blocks, 1, BLOCK), lambda i, info: (0, 0, 0)),
            ],
            out_specs=[
                pl.BlockSpec((BLOCK, width), lambda i, info: (place(i, info[2, 0], per_chunk), 0)),
                pl.BlockSpec((1, heads, BLOCK), lambda i, info: (i, 0, 0)),
            ],
            scratch_shapes=[
                pltpu.VMEM((width, BLOCK), f32),
                pltpu.VMEM((heads, 1, BLOCK), f32),
                pltpu.VMEM((heads, 1, BLOCK), f32),
            ],
        ),
        out_shape=[
            jax.ShapeDtypeStruct((rows, width), bf16),
            jax.ShapeDtypeStruct((blocks, heads, BLOCK), f32),
        ],
        cost_estimate=pl.CostEstimate(flops=30 * 10**9, bytes_accessed=6 * rows * width, transcendentals=10**7),
        name="attention_forward",
    )(info, qkv, ids_col, ids_row)


def backward_kernel(
    per_chunk, first, info, q_ref, k_ref, v_ref, do_ref, o_ref, lse_ref, idc_ref, idr_ref,
    out_ref, delta_ref, dq_acc, dk_acc, dv_acc,
):
    j = pl.program_id(0)
    blocks = pl.num_programs(0)
    me = info[2, 0]

    @pl.when(j == 0)
    def _():
        dq_acc[...] = jnp.zeros_like(dq_acc)

        def fill(i, carry):
            at = pl.multiple_of(place(i, me, per_chunk) * BLOCK, BLOCK)
            prod = (do_ref[pl.ds(at, BLOCK), :].astype(f32) * o_ref[pl.ds(at, BLOCK), :].astype(f32)).T
            for w in range(2):
                delta_ref[i, w : w + 1, :] = jnp.sum(prod[w * HEAD_DIM : (w + 1) * HEAD_DIM], axis=0, keepdims=True)
            return carry

        lax.fori_loop(0, blocks, fill, 0)

    dk_acc[...] = jnp.zeros_like(dk_acc)
    dv_acc[...] = jnp.zeros_like(dv_acc)
    ids_k = idc_ref[pl.ds(pl.multiple_of(j * BLOCK, BLOCK), BLOCK), :]

    def step(i, carry):
        at = pl.multiple_of(place(i, me, per_chunk) * BLOCK, BLOCK)
        same = ids_k == idr_ref[pl.ds(i, 1)][0]
        k_pair, v_pair = k_ref[...], v_ref[...]
        q_pair, do_pair = q_ref[pl.ds(at, BLOCK), :], do_ref[pl.ds(at, BLOCK), :]
        dv, dk, dq = [], [], []
        for w in range(2):
            q_one, do_one = head_only(q_pair, w), head_only(do_pair, w)
            t = nt(k_pair, q_one) * SCALE_LOG2 - lse_ref[i, first + w : first + w + 1, :]
            e = jnp.exp2(jnp.where(same, t, MASKED))
            ds = (e * (nt(v_pair, do_one) - delta_ref[i, w : w + 1, :])).astype(bf16)
            dv.append(nn(e.astype(bf16), do_one))
            dk.append(nn(ds, q_one))
            dq.append(tn(ds, head_only(k_pair, w)))
        dv_acc[...] += dv[0] + dv[1]
        dk_acc[...] += dk[0] + dk[1]
        dq_acc[pl.ds(at, BLOCK), :] += dq[0] + dq[1]
        return carry

    lax.fori_loop(info[0, j], info[1, j], step, 0)
    mine = pl.multiple_of(place(j, me, per_chunk) * BLOCK, BLOCK)
    out_ref[pl.ds(mine, BLOCK), 128:256] = (dk_acc[...] * SCALE).astype(bf16)
    out_ref[pl.ds(mine, BLOCK), 256:384] = dv_acc[...].astype(bf16)

    @pl.when(j == blocks - 1)
    def _():
        out_ref[:, 0:128] = (dq_acc[...] * SCALE).astype(bf16)


def attention_backward(pair, info, qkv, do, o, lse, ids_col, ids_row, per_chunk):
    rows, width = o.shape
    blocks, heads = rows // BLOCK, width // HEAD_DIM
    return pl.pallas_call(
        functools.partial(backward_kernel, per_chunk, 2 * pair),
        grid_spec=pltpu.PrefetchScalarGridSpec(
            num_scalar_prefetch=1,
            grid=(blocks,),
            in_specs=[
                pl.BlockSpec((rows, 128), lambda i, info: (0, 3 * pair)),
                pl.BlockSpec((BLOCK, 128), lambda i, info: (place(i, info[2, 0], per_chunk), 3 * pair + 1)),
                pl.BlockSpec((BLOCK, 128), lambda i, info: (place(i, info[2, 0], per_chunk), 3 * pair + 2)),
                pl.BlockSpec((rows, 128), lambda i, info: (0, pair)),
                pl.BlockSpec((rows, 128), lambda i, info: (0, pair)),
                pl.BlockSpec((blocks, heads, BLOCK), lambda i, info: (0, 0, 0)),
                pl.BlockSpec((rows, 1), lambda i, info: (0, 0)),
                pl.BlockSpec((blocks, 1, BLOCK), lambda i, info: (0, 0, 0)),
            ],
            out_specs=pl.BlockSpec((rows, 384), lambda i, info: (0, 0)),
            scratch_shapes=[
                pltpu.VMEM((blocks, 2, BLOCK), f32),
                pltpu.VMEM((rows, 128), f32),
                pltpu.VMEM((BLOCK, 128), f32),
                pltpu.VMEM((BLOCK, 128), f32),
            ],
        ),
        out_shape=jax.ShapeDtypeStruct((rows, 384), bf16),
        cost_estimate=pl.CostEstimate(flops=25 * 10**9, bytes_accessed=8 * rows * 128, transcendentals=10**7),
        name="attention_backward",
    )(info, qkv, qkv, qkv, do, o, lse, ids_col, ids_row)


def spans(ids, me):
    blocks = ids.shape[0] // BLOCK
    per_block = ids.reshape(blocks, BLOCK)
    low = jnp.sum(ids[None, :] < per_block[:, :1], axis=1) // BLOCK
    high = (jnp.sum(ids[None, :] <= per_block[:, -1:], axis=1) + BLOCK - 1) // BLOCK
    return jnp.stack([low, high, jnp.full((blocks,), me.astype(low.dtype))]).astype(jnp.int32)


def own_index(axis):
    return lax.axis_index(axis).astype(jnp.uint32)


def swap(value, axis, mask):
    size = lax.axis_size(axis)
    return lax.ppermute(value, axis, [(i, i ^ mask) for i in range(size)])


def bits(size):
    return [1 << b for b in range(size.bit_length() - 1)]


def gather_relative(value, axis):
    held = {0: value}
    for bit in reversed(bits(lax.axis_size(axis))):
        held.update({k | bit: swap(v, axis, bit) for k, v in list(held.items())})
    return [held[k] for k in range(len(held))]


def gather_stacked(value, axis):
    for bit in reversed(bits(lax.axis_size(axis))):
        value = jnp.concatenate([value, swap(value, axis, bit)])
    return value


def flipped(index, size):
    flags = bits(size)
    return sum(((index >> n) & 1) << (len(flags) - 1 - n) for n in range(len(flags)))


def trade(pieces, axis):
    return [pieces[0]] + [swap(pieces[k], axis, k) for k in range(1, len(pieces))]


def to_absolute(pieces, me):
    stacked = jnp.stack(pieces)
    return [lax.dynamic_index_in_dim(stacked, (me ^ c), 0, False) for c in range(len(pieces))]


class Halving:
    def __init__(self, names, shape):
        self.me = {n: (own_index(n[0]) >> (n[1].bit_length() - 1)) & 1 for n in names}
        self.names, self.terms, self.fixed, self.shape = list(names), [], {}, shape

    def cut(self, term, chosen):
        array, names, part = term
        starts, sizes = [], []
        for n in names:
            starts.append(chosen.get(n, jnp.uint32(0)))
            sizes.append(1 if n in chosen else 2)
        for low, high in part:
            starts.append(jnp.uint32(low))
            sizes.append(high - low)
        left = [2 for n in names if n not in chosen]
        return lax.dynamic_slice(array, starts, sizes).reshape(left + [h - l for l, h in part])

    def total(self, chosen):
        pieces = [self.cut(t, chosen).astype(f32) for t in self.terms]
        return sum(pieces[1:], pieces[0])

    def outgoing(self, name):
        return self.total({**self.fixed, name: 1 - self.me[name]}).astype(bf16)

    def arrived(self, name, value):
        self.fixed[name] = self.me[name]
        names = [n for n in self.names if n not in self.fixed]
        self.terms.append((value, names, [(0, d) for d in self.shape]))

    def exchange(self, name):
        self.arrived(name, swap(self.outgoing(name), *name))

    def result(self):
        return self.total(self.fixed)


def normalize(values, gain, shift):
    average = jnp.mean(values, axis=-1, keepdims=True)
    centered = values - average
    inverse = lax.rsqrt(jnp.mean(centered * centered, axis=-1, keepdims=True) + EPSILON)
    normed = centered * inverse
    return normed * gain + shift, normed, inverse


def normalize_back(upstream, normed, inverse, gain):
    scaled = upstream * gain
    plain = jnp.mean(scaled, axis=-1, keepdims=True)
    cross = jnp.mean(scaled * normed, axis=-1, keepdims=True)
    result = inverse * (scaled - plain - normed * cross)
    return result, jnp.sum(upstream * normed, axis=0), jnp.sum(upstream, axis=0)


def shards(
    tokens, time_feat, cotangent, segment_ids, time_weight, time_bias, query_weight, query_bias, key_weight,
    value_weight, value_bias, output_weight, output_bias, mixing_gain, mixing_bias, up_weight, up_bias,
    down_weight, down_bias, final_gain, final_bias,
):
    me_dp, me = own_index("dp"), own_index("ctx")
    dp, ctx = lax.axis_size("dp"), lax.axis_size("ctx")
    devices = dp * ctx
    piece, width = tokens.shape[1], tokens.shape[2]
    hidden = up_weight.shape[1]
    own, ratio = width // devices, hidden // width
    cols = width // ctx
    per_chunk = piece // BLOCK
    tokens, cotangent, ids = tokens[0], cotangent[0], segment_ids[0]

    second = lax.all_gather(jnp.concatenate([up_weight, output_weight], axis=1), BOTH, axis=0, tiled=True)
    down_full = lax.all_gather(down_weight, BOTH, axis=0, tiled=True)
    up_full, output_full = second[:, :hidden], second[:, hidden:]

    token_chunks = gather_relative(tokens, "ctx")
    vectors = [
        time_bias, query_bias, value_bias, output_bias, mixing_gain, mixing_bias, down_bias, final_gain, final_bias
    ]
    small = jnp.concatenate([jnp.stack(vectors), up_bias.reshape(ratio, own)]).T
    small = jnp.pad(small, ((0, 0), (0, 128 - small.shape[1])))
    pieces = []
    for k in range(ctx):
        at = (me ^ k) * cols
        parts = [
            lax.dynamic_slice_in_dim(w, at + p * 128, 128, 1)
            for p in range(cols // 128)
            for w in (query_weight, key_weight, value_weight)
        ] + [lax.dynamic_slice_in_dim(time_weight, at, cols, 1)]
        pieces.append(jnp.concatenate(parts + [small], axis=1))
    first = jnp.concatenate(to_absolute(trade(pieces, "ctx"), me))
    first = gather_stacked(first[None], "dp")
    first = jnp.concatenate(
        [
            lax.dynamic_index_in_dim(first, flipped((me_dp ^ c), dp), 0, False)
            for c in range(dp)
        ]
    )
    qkv_weight = first[:, : 3 * cols]
    table = first[:, 4 * cols :].astype(f32).T
    time_shift_bias, query_shift, value_shift, output_shift, gain_one, bias_one, down_shift, gain_two, bias_two = [
        table[n] for n in range(len(vectors))
    ]
    up_shift = table[len(vectors) : len(vectors) + ratio].reshape(ratio, devices, own).transpose(1, 0, 2).reshape(hidden)
    shift_cols = trade([nn(time_feat, first[:, 3 * cols : 4 * cols])] * ctx, "ctx")
    time_shift = jnp.concatenate(to_absolute(shift_cols, me), axis=1) + time_shift_bias
    qkv_shift = []
    for p in range(cols // 128):
        at = me * cols + p * 128
        qkv_shift.append(lax.dynamic_slice_in_dim(query_shift, at, 128))
        qkv_shift.append(jnp.zeros((128,), f32))
        qkv_shift.append(lax.dynamic_slice_in_dim(value_shift, at, 128))
    qkv_shift = jnp.concatenate(qkv_shift)
    start_row = (jnp.concatenate(token_chunks).astype(f32) + time_shift).astype(bf16)
    residual_in = tokens.astype(f32) + time_shift
    qkv = (nn(start_row, qkv_weight) + qkv_shift).astype(bf16)

    info = spans(ids, me)
    ids_col, ids_row = ids.reshape(-1, 1), ids.reshape(-1, 1, BLOCK)
    mixed, logsum = attention_forward(info, qkv, ids_col, ids_row, per_chunk)
    returned = trade([mixed[k * piece : (k + 1) * piece] for k in range(ctx)], "ctx")
    attended = jnp.concatenate(to_absolute(returned, me), axis=1)

    branch = nn(attended, output_full) + output_shift
    hidden_one, normed_one, inverse_one = normalize(residual_in + branch, gain_one, bias_one)
    hidden_low = hidden_one.astype(bf16)
    pre_gelu = nn(hidden_low, up_full) + up_shift
    share = 0.5 * (1.0 + lax.erf(pre_gelu * 0.5**0.5))
    activated = (pre_gelu * share).astype(bf16)
    slope = (share + pre_gelu * jnp.exp(-0.5 * pre_gelu * pre_gelu) * 0.3989422804014327).astype(bf16)
    activated, slope = lax.optimization_barrier((activated, slope))
    feed_out = nn(activated, down_full) + down_shift
    result, normed_two, inverse_two = normalize(hidden_one + feed_out, gain_two, bias_two)
    layer_out = result.astype(bf16)

    upstream = cotangent.astype(f32)
    grad_two, gain_two_grad, bias_two_grad = normalize_back(upstream, normed_two, inverse_two, gain_two)
    grad_feed = grad_two.astype(bf16)
    down_grad = tn(activated, grad_feed).astype(bf16)
    down_shift_grad = jnp.sum(grad_feed.astype(f32), axis=0)
    grad_inner = (nt(grad_feed, down_full) * slope.astype(f32)).astype(bf16)
    up_grad = tn(hidden_low, grad_inner).astype(bf16)
    up_shift_grad = jnp.sum(grad_inner.astype(f32), axis=0)
    grad_hidden = grad_two + nt(grad_inner, up_full)
    grad_one, gain_one_grad, bias_one_grad = normalize_back(grad_hidden, normed_one, inverse_one, gain_one)
    grad_branch = grad_one.astype(bf16)
    output_grad = tn(attended, grad_branch).astype(bf16)
    output_shift_grad = jnp.sum(grad_branch.astype(f32), axis=0)
    vector_grads = jnp.stack(
        [output_shift_grad, gain_one_grad, bias_one_grad, down_shift_grad, gain_two_grad, bias_two_grad]
    )
    up_shift_grad = up_shift_grad.reshape(devices, ratio, own).transpose(1, 0, 2).reshape(ratio, width)
    vector_grads = jnp.concatenate([vector_grads, up_shift_grad])
    vector_grads = jnp.pad(vector_grads, ((0, 128 - vector_grads.shape[0]), (0, 0))).T.astype(bf16)
    rest_grad = jnp.concatenate([output_grad, lax.optimization_barrier(vector_grads)], axis=1)

    dp_names, ctx_names = [("dp", b) for b in bits(dp)], [("ctx", b) for b in bits(ctx)]
    names = dp_names[::-1] + ctx_names[::-1]
    core, turn, rest = ctx_names[0], dp_names[:2] + ctx_names[1:], dp_names[2:]
    whole = {}
    for label, array, height in (("down", down_grad, ratio * own), ("up", up_grad, own), ("rest", rest_grad, own)):
        size = (height, array.shape[1])
        whole[label] = Halving(names, size)
        whole[label].terms = [(array.reshape([2] * len(names) + list(size)), names, [(0, d) for d in size])]
        whole[label].exchange(core)

    def stream(label, part, turned):
        sums = Halving(names, [high - low for low, high in part])
        sums.fixed = {core: sums.me[core]}
        sums.terms = [(array, left, part) for array, left, _ in whole[label].terms]
        return sums, turn[turned:] + turn[:turned] + rest

    most, tall = 3 * hidden // 4, (ratio - 1) * own
    streams = [
        stream("up", [(0, own), (0, most)], 2),
        stream("down", [(0, tall), (0, width)], 0),
        stream("up", [(0, own), (most, hidden)], 1),
        stream("down", [(tall, ratio * own), (0, width)], 1),
        stream("rest", [(0, own), (0, width + 128)], 1),
    ]

    grad_attended = nt(grad_branch, output_full).astype(bf16)
    pieces = [lax.dynamic_slice_in_dim(grad_attended, (me ^ k) * cols, cols, 1) for k in range(ctx)]
    grad_mixed = jnp.concatenate(trade(pieces, "ctx"))
    def weight_stream(grad):
        size = (ctx * own, grad.shape[1])
        sums = Halving(dp_names[::-1], size)
        array = tn(start_row, grad).reshape([2] * len(dp_names) + list(size))
        sums.terms = [(array, dp_names[::-1], [(0, d) for d in size])]
        return sums, list(dp_names)

    def start_part(k):
        rows = slice(k * piece, (k + 1) * piece)
        return nt(jnp.concatenate([g[rows] for g in grads], axis=1), qkv_weight)

    def depart(moving, beside):
        going = [s.outgoing(name) for s, name in moving]
        going, beside = lax.optimization_barrier((going, beside))
        return [(s, name, swap(value, *name)) for (s, name), value in zip(moving, going)], beside

    def land(flights, beside):
        values, beside = lax.optimization_barrier(([value for _, _, value in flights], beside))
        for (s, name, _), value in zip(flights, values):
            s.arrived(name, value)
        return beside

    def following(pairs):
        return [(s, o.pop(0)) for s, o in pairs if o]

    grads, pair_streams = [], []
    for pair in range(cols // 128):
        flights, grad_mixed = depart(following(streams + pair_streams), grad_mixed)
        grad = attention_backward(pair, info, qkv, grad_mixed, mixed, logsum, ids_col, ids_row, per_chunk)
        grad_mixed, grad = land(flights, (grad_mixed, grad))
        grads.append(grad)
        pair_streams.append(weight_stream(grad))

    qkv_sum = jnp.concatenate([jnp.sum(g.astype(f32), axis=0) for g in grads])
    row_sum = jnp.sum(grad_one, axis=0, keepdims=True) + lax.dot_general(
        qkv_sum[None],
        qkv_weight.astype(f32),
        (((1,), (1,)), ((), ())),
        precision=lax.Precision.HIGHEST,
        preferred_element_type=f32,
    )
    message = jnp.concatenate(
        [row_sum]
        + [qkv_sum[None, (3 * p + n) * 128 : (3 * p + n + 1) * 128] for n in (0, 2) for p in range(cols // 128)]
        + [time_feat.astype(f32)],
        axis=1,
    )
    message_names = dp_names[::-1]

    odd = [start_part(k).astype(bf16) for k in range(1, ctx, 2)]
    flights, (grads, odd, message) = depart(following(streams + pair_streams), (grads, odd, message))
    odd = [swap(value, *core) for value in odd]
    reply = swap(message, *message_names.pop(0))
    even = [start_part(k) for k in range(0, ctx, 2)]
    even, odd, message, reply = land(flights, (even, odd, message, reply))
    message = jnp.concatenate([message, reply])
    even = [e + o.astype(f32) for e, o in zip(even, odd)]
    away = [value.astype(bf16) for value in even[1:]]
    kept, came = [], None
    while any(o for _, o in streams + pair_streams) or message_names:
        fast, slow = following(pair_streams), following(streams)
        flights, (away, message) = depart(fast + slow, (away, message))
        if came is None:
            came = [swap(value, "ctx", 2 * n + 2) for n, value in enumerate(away)]
        if message_names:
            message = jnp.concatenate([message, swap(message, *message_names.pop(0))])
        kept += flights[len(fast) :]
        flights = flights[: len(fast)]
        if any(o for _, o in streams):
            flights, kept = flights + kept, []
        if not any(o for _, o in pair_streams):
            flights, kept = flights + kept, []
        message, came = land(flights, (message, came)) if not kept else (land(flights, message), came)
    summed = jnp.concatenate([s.result() for s, _ in pair_streams], axis=1).reshape(ctx, own, 3 * cols)
    summed = [lax.dynamic_index_in_dim(summed, (me ^ k), 0, False) for k in range(ctx)]
    summed, message = lax.optimization_barrier((summed, message))
    blocks_out = to_absolute(trade(summed, "ctx"), me)
    message = jnp.stack(trade([message] * ctx, "ctx"))
    tokens_grad = (grad_one + sum([c.astype(f32) for c in came], even[0])).astype(bf16)
    up_left, down_left, up_right, down_right, rest_left = [s.result() for s, _ in streams]
    up_weight_grad = jnp.concatenate([up_left, up_right], axis=1)
    down_weight_grad = jnp.concatenate([down_left, down_right])
    output_weight_grad = rest_left[:, :width]
    vector_grads = rest_left[:, width:].T
    output_bias_grad, mixing_gain_grad, mixing_bias_grad, down_bias_grad, final_gain_grad, final_bias_grad = [
        vector_grads[n] for n in range(6)
    ]
    up_bias_grad = vector_grads[6 : 6 + ratio].reshape(ratio * own)

    mine = (me_dp * ctx + me) * own
    row_sums = jnp.sum(message[:, :, :width], axis=0)
    time_weight_grad = lax.dot_general(
        lax.dynamic_slice_in_dim(message[0, :, width + 2 * cols :], mine, own, 1),
        row_sums,
        (((0,), (0,)), ((), ())),
        precision=lax.Precision.HIGHEST,
        preferred_element_type=f32,
    )
    time_bias_grad = lax.dynamic_slice_in_dim(jnp.sum(row_sums, axis=0), mine, own)
    sums = jnp.sum(message[:, :, width : width + 2 * cols], axis=1)
    sums = lax.dynamic_index_in_dim(sums, mine // cols ^ me, 0, False)
    query_bias_grad = lax.dynamic_slice_in_dim(sums[:cols], mine % cols, own)
    value_bias_grad = lax.dynamic_slice_in_dim(sums[cols:], mine % cols, own)

    query_weight_grad, key_weight_grad, value_weight_grad = [
        jnp.concatenate(
            [
                block[:, (3 * p + n) * 128 : (3 * p + n + 1) * 128]
                for block in blocks_out
                for p in range(cols // 128)
            ],
            axis=1,
        )
        for n in range(3)
    ]
    return (
        layer_out[None],
        tokens_grad[None],
        time_weight_grad,
        time_bias_grad,
        query_weight_grad,
        query_bias_grad,
        key_weight_grad,
        value_weight_grad,
        value_bias_grad,
        output_weight_grad,
        output_bias_grad,
        mixing_gain_grad,
        mixing_bias_grad,
        up_weight_grad,
        up_bias_grad,
        down_weight_grad,
        down_bias_grad,
        final_gain_grad,
        final_bias_grad,
    )


def solution(mesh):
    rows, split_rows, split = P("dp", "ctx", None), P(BOTH, None), P(BOTH)
    return jax.shard_map(
        shards,
        mesh=mesh,
        in_specs=(
            rows, P("dp", None), rows, P("dp", None), split_rows, split, split_rows, split, split_rows, split_rows,
            split, split_rows, split, split, split, split_rows, split, split_rows, split, split, split,
        ),
        out_specs=(
            rows, rows, split_rows, split, split_rows, split, split_rows, split_rows, split, split_rows, split, split,
            split, split_rows, split, split_rows, split, split, split,
        ),
        check_vma=False,
    )
```

```python
import functools

import jax
import jax.numpy as jnp
from jax import lax
from jax.experimental import pallas as pl
from jax.experimental.pallas import tpu as pltpu
from jax.sharding import PartitionSpec as P

HEAD_DIM = 64
BLOCK = 256
MASKED = -1e30
EPSILON = 1e-05
SCALE = HEAD_DIM**-0.5
SCALE_LOG2 = SCALE * 1.4426950408889634
BOTH = ("dp", "ctx")
f32, bf16 = jnp.float32, jnp.bfloat16


def nn(left, right):
    return jnp.dot(left, right, preferred_element_type=f32)


def tn(left, right):
    return lax.dot_general(left, right, (((0,), (0,)), ((), ())), preferred_element_type=f32)


def nt(left, right):
    return lax.dot_general(left, right, (((1,), (1,)), ((), ())), preferred_element_type=f32)


def head_only(pair, which):
    lane = lax.broadcasted_iota(jnp.int32, pair.shape, 1)
    keep = (lane < HEAD_DIM) if which == 0 else (lane >= HEAD_DIM)
    return jnp.where(keep, pair, jnp.zeros_like(pair))


def place(block, me, per_chunk):
    return lax.bitwise_xor(block // per_chunk, me) * per_chunk + lax.rem(block, per_chunk)


def forward_kernel(per_chunk, pairs, info, qkv_ref, idc_ref, idr_ref, o_ref, lse_ref, o_acc, m_acc, l_acc):
    i = pl.program_id(0)
    me = info[2, 0]
    m_acc[...] = jnp.full_like(m_acc, MASKED)
    l_acc[...] = jnp.zeros_like(l_acc)
    o_acc[...] = jnp.zeros_like(o_acc)
    ids_q = idr_ref[pl.ds(i, 1)][0]
    here = pl.multiple_of(place(i, me, per_chunk) * BLOCK, BLOCK)

    queries = []
    for p in range(pairs):
        pair = qkv_ref[pl.ds(here, BLOCK), (3 * p) * 128 : (3 * p + 1) * 128]
        queries += [head_only(pair, 0), head_only(pair, 1)]

    def step(j, carry):
        at = pl.multiple_of(place(j, me, per_chunk) * BLOCK, BLOCK)
        same = idc_ref[pl.ds(pl.multiple_of(j * BLOCK, BLOCK), BLOCK), :] == ids_q
        heads = range(2 * pairs)
        peak = [m_acc[h] for h in heads]
        count = [l_acc[h] for h in heads]
        mixed = [o_acc[h * HEAD_DIM : (h + 1) * HEAD_DIM] for h in heads]
        values, scores = [], []
        for p in range(pairs):
            k_pair = qkv_ref[pl.ds(at, BLOCK), (3 * p + 1) * 128 : (3 * p + 2) * 128]
            values.append(qkv_ref[pl.ds(at, BLOCK), (3 * p + 2) * 128 : (3 * p + 3) * 128])
            scores += [nt(k_pair, queries[2 * p + w]) for w in range(2)]
        for h in heads:
            t = jnp.where(same, scores[h] * SCALE_LOG2, MASKED)
            new = jnp.maximum(peak[h], jnp.max(t, axis=0, keepdims=True))
            alpha = jnp.exp2(peak[h] - new)
            e = jnp.exp2(t - new)
            count[h] = count[h] * alpha + jnp.sum(e, axis=0, keepdims=True)
            peak[h] = new
            w = h % 2
            mixed[h] = mixed[h] * alpha + tn(values[h // 2], e.astype(bf16))[w * HEAD_DIM : (w + 1) * HEAD_DIM]
        for h in heads:
            m_acc[h], l_acc[h] = peak[h], count[h]
            o_acc[h * HEAD_DIM : (h + 1) * HEAD_DIM] = mixed[h]
        return carry

    lax.fori_loop(info[0, i], info[1, i], step, 0)
    for p in range(pairs):
        parts = []
        for w in range(2):
            h = 2 * p + w
            parts.append(o_acc[h * HEAD_DIM : (h + 1) * HEAD_DIM] / l_acc[h])
            lse_ref[0, h : h + 1, :] = m_acc[h] + jnp.log2(l_acc[h])
        o_ref[:, p * 128 : (p + 1) * 128] = jnp.concatenate(parts, axis=0).T.astype(bf16)


def attention_forward(info, qkv, ids_col, ids_row, per_chunk):
    rows, width = qkv.shape[0], qkv.shape[1] // 3
    blocks, heads = rows // BLOCK, width // HEAD_DIM
    return pl.pallas_call(
        functools.partial(forward_kernel, per_chunk, heads // 2),
        grid_spec=pltpu.PrefetchScalarGridSpec(
            num_scalar_prefetch=1,
            grid=(blocks,),
            in_specs=[
                pl.BlockSpec((rows, 3 * width), lambda i, info: (0, 0)),
                pl.BlockSpec((rows, 1), lambda i, info: (0, 0)),
                pl.BlockSpec((blocks, 1, BLOCK), lambda i, info: (0, 0, 0)),
            ],
            out_specs=[
                pl.BlockSpec((BLOCK, width), lambda i, info: (place(i, info[2, 0], per_chunk), 0)),
                pl.BlockSpec((1, heads, BLOCK), lambda i, info: (i, 0, 0)),
            ],
            scratch_shapes=[
                pltpu.VMEM((width, BLOCK), f32),
                pltpu.VMEM((heads, 1, BLOCK), f32),
                pltpu.VMEM((heads, 1, BLOCK), f32),
            ],
        ),
        out_shape=[
            jax.ShapeDtypeStruct((rows, width), bf16),
            jax.ShapeDtypeStruct((blocks, heads, BLOCK), f32),
        ],
        cost_estimate=pl.CostEstimate(flops=30 * 10**9, bytes_accessed=6 * rows * width, transcendentals=10**7),
        name="attention_forward",
    )(info, qkv, ids_col, ids_row)


def backward_kernel(
    per_chunk, first, info, q_ref, k_ref, v_ref, do_ref, o_ref, lse_ref, idc_ref, idr_ref,
    out_ref, delta_ref, dq_acc, dk_acc, dv_acc,
):
    j = pl.program_id(0)
    blocks = pl.num_programs(0)
    me = info[2, 0]

    @pl.when(j == 0)
    def _():
        dq_acc[...] = jnp.zeros_like(dq_acc)

        def fill(i, carry):
            at = pl.multiple_of(place(i, me, per_chunk) * BLOCK, BLOCK)
            prod = (do_ref[pl.ds(at, BLOCK), :].astype(f32) * o_ref[pl.ds(at, BLOCK), :].astype(f32)).T
            for w in range(2):
                delta_ref[i, w : w + 1, :] = jnp.sum(prod[w * HEAD_DIM : (w + 1) * HEAD_DIM], axis=0, keepdims=True)
            return carry

        lax.fori_loop(0, blocks, fill, 0)

    dk_acc[...] = jnp.zeros_like(dk_acc)
    dv_acc[...] = jnp.zeros_like(dv_acc)
    ids_k = idc_ref[pl.ds(pl.multiple_of(j * BLOCK, BLOCK), BLOCK), :]

    def step(i, carry):
        at = pl.multiple_of(place(i, me, per_chunk) * BLOCK, BLOCK)
        same = ids_k == idr_ref[pl.ds(i, 1)][0]
        k_pair, v_pair = k_ref[...], v_ref[...]
        q_pair, do_pair = q_ref[pl.ds(at, BLOCK), :], do_ref[pl.ds(at, BLOCK), :]
        dv, dk, dq = [], [], []
        for w in range(2):
            q_one, do_one = head_only(q_pair, w), head_only(do_pair, w)
            t = nt(k_pair, q_one) * SCALE_LOG2 - lse_ref[i, first + w : first + w + 1, :]
            e = jnp.exp2(jnp.where(same, t, MASKED))
            ds = (e * (nt(v_pair, do_one) - delta_ref[i, w : w + 1, :])).astype(bf16)
            dv.append(nn(e.astype(bf16), do_one))
            dk.append(nn(ds, q_one))
            dq.append(tn(ds, head_only(k_pair, w)))
        dv_acc[...] += dv[0] + dv[1]
        dk_acc[...] += dk[0] + dk[1]
        dq_acc[pl.ds(at, BLOCK), :] += dq[0] + dq[1]
        return carry

    lax.fori_loop(info[0, j], info[1, j], step, 0)
    mine = pl.multiple_of(place(j, me, per_chunk) * BLOCK, BLOCK)
    out_ref[pl.ds(mine, BLOCK), 128:256] = (dk_acc[...] * SCALE).astype(bf16)
    out_ref[pl.ds(mine, BLOCK), 256:384] = dv_acc[...].astype(bf16)

    @pl.when(j == blocks - 1)
    def _():
        out_ref[:, 0:128] = (dq_acc[...] * SCALE).astype(bf16)


def attention_backward(pair, info, qkv, do, o, lse, ids_col, ids_row, per_chunk):
    rows, width = o.shape
    blocks, heads = rows // BLOCK, width // HEAD_DIM
    return pl.pallas_call(
        functools.partial(backward_kernel, per_chunk, 2 * pair),
        grid_spec=pltpu.PrefetchScalarGridSpec(
            num_scalar_prefetch=1,
            grid=(blocks,),
            in_specs=[
                pl.BlockSpec((rows, 128), lambda i, info: (0, 3 * pair)),
                pl.BlockSpec((BLOCK, 128), lambda i, info: (place(i, info[2, 0], per_chunk), 3 * pair + 1)),
                pl.BlockSpec((BLOCK, 128), lambda i, info: (place(i, info[2, 0], per_chunk), 3 * pair + 2)),
                pl.BlockSpec((rows, 128), lambda i, info: (0, pair)),
                pl.BlockSpec((rows, 128), lambda i, info: (0, pair)),
                pl.BlockSpec((blocks, heads, BLOCK), lambda i, info: (0, 0, 0)),
                pl.BlockSpec((rows, 1), lambda i, info: (0, 0)),
                pl.BlockSpec((blocks, 1, BLOCK), lambda i, info: (0, 0, 0)),
            ],
            out_specs=pl.BlockSpec((rows, 384), lambda i, info: (0, 0)),
            scratch_shapes=[
                pltpu.VMEM((blocks, 2, BLOCK), f32),
                pltpu.VMEM((rows, 128), f32),
                pltpu.VMEM((BLOCK, 128), f32),
                pltpu.VMEM((BLOCK, 128), f32),
            ],
        ),
        out_shape=jax.ShapeDtypeStruct((rows, 384), bf16),
        cost_estimate=pl.CostEstimate(flops=25 * 10**9, bytes_accessed=8 * rows * 128, transcendentals=10**7),
        name="attention_backward",
    )(info, qkv, qkv, qkv, do, o, lse, ids_col, ids_row)


def spans(ids, me):
    blocks = ids.shape[0] // BLOCK
    per_block = ids.reshape(blocks, BLOCK)
    low = jnp.sum(ids[None, :] < per_block[:, :1], axis=1) // BLOCK
    high = (jnp.sum(ids[None, :] <= per_block[:, -1:], axis=1) + BLOCK - 1) // BLOCK
    return jnp.stack([low, high, jnp.full((blocks,), me.astype(low.dtype))]).astype(jnp.int32)


def own_index(axis):
    return lax.axis_index(axis).astype(jnp.uint32)


def swap(value, axis, mask):
    size = lax.axis_size(axis)
    return lax.ppermute(value, axis, [(i, i ^ mask) for i in range(size)])


def bits(size):
    return [1 << b for b in range(size.bit_length() - 1)]


def gather_relative(value, axis):
    held = {0: value}
    for bit in reversed(bits(lax.axis_size(axis))):
        held.update({k | bit: swap(v, axis, bit) for k, v in list(held.items())})
    return [held[k] for k in range(len(held))]


def gather_stacked(value, axis):
    for bit in reversed(bits(lax.axis_size(axis))):
        value = jnp.concatenate([value, swap(value, axis, bit)])
    return value


def flipped(index, size):
    flags = bits(size)
    return sum(((index >> n) & 1) << (len(flags) - 1 - n) for n in range(len(flags)))


def trade(pieces, axis):
    return [pieces[0]] + [swap(pieces[k], axis, k) for k in range(1, len(pieces))]


def to_absolute(pieces, me):
    stacked = jnp.stack(pieces)
    return [lax.dynamic_index_in_dim(stacked, (me ^ c), 0, False) for c in range(len(pieces))]


class Halving:
    def __init__(self, names, shape):
        self.me = {n: (own_index(n[0]) >> (n[1].bit_length() - 1)) & 1 for n in names}
        self.names, self.terms, self.fixed, self.shape = list(names), [], {}, shape

    def cut(self, term, chosen):
        array, names, part = term
        starts, sizes = [], []
        for n in names:
            starts.append(chosen.get(n, jnp.uint32(0)))
            sizes.append(1 if n in chosen else 2)
        for low, high in part:
            starts.append(jnp.uint32(low))
            sizes.append(high - low)
        left = [2 for n in names if n not in chosen]
        return lax.dynamic_slice(array, starts, sizes).reshape(left + [h - l for l, h in part])

    def total(self, chosen):
        pieces = [self.cut(t, chosen).astype(f32) for t in self.terms]
        return sum(pieces[1:], pieces[0])

    def outgoing(self, name):
        return self.total({**self.fixed, name: 1 - self.me[name]}).astype(bf16)

    def arrived(self, name, value):
        self.fixed[name] = self.me[name]
        names = [n for n in self.names if n not in self.fixed]
        self.terms.append((value, names, [(0, d) for d in self.shape]))

    def exchange(self, name):
        self.arrived(name, swap(self.outgoing(name), *name))

    def result(self):
        return self.total(self.fixed)


def normalize(values, gain, shift):
    average = jnp.mean(values, axis=-1, keepdims=True)
    centered = values - average
    inverse = lax.rsqrt(jnp.mean(centered * centered, axis=-1, keepdims=True) + EPSILON)
    normed = centered * inverse
    return normed * gain + shift, normed, inverse


def normalize_back(upstream, normed, inverse, gain):
    scaled = upstream * gain
    plain = jnp.mean(scaled, axis=-1, keepdims=True)
    cross = jnp.mean(scaled * normed, axis=-1, keepdims=True)
    result = inverse * (scaled - plain - normed * cross)
    return result, jnp.sum(upstream * normed, axis=0), jnp.sum(upstream, axis=0)


def shards(
    tokens, time_feat, cotangent, segment_ids, time_weight, time_bias, query_weight, query_bias, key_weight,
    value_weight, value_bias, output_weight, output_bias, mixing_gain, mixing_bias, up_weight, up_bias,
    down_weight, down_bias, final_gain, final_bias,
):
    me_dp, me = own_index("dp"), own_index("ctx")
    dp, ctx = lax.axis_size("dp"), lax.axis_size("ctx")
    devices = dp * ctx
    piece, width = tokens.shape[1], tokens.shape[2]
    hidden = up_weight.shape[1]
    own, ratio = width // devices, hidden // width
    cols = width // ctx
    per_chunk = piece // BLOCK
    tokens, cotangent, ids = tokens[0], cotangent[0], segment_ids[0]

    second = lax.all_gather(
        jnp.concatenate([up_weight, output_weight] + [down_weight[n * own : (n + 1) * own] for n in range(ratio)], axis=1),
        BOTH,
        axis=0,
        tiled=True,
    )
    up_full, output_full = second[:, :hidden], second[:, hidden : hidden + width]
    down_full = jnp.stack(
        [second[:, hidden + n * width : hidden + (n + 1) * width].reshape(devices, own, width) for n in range(1, 1 + ratio)],
        axis=1,
    ).reshape(hidden, width)

    token_chunks = gather_relative(tokens, "ctx")
    vectors = [
        time_bias, query_bias, value_bias, output_bias, mixing_gain, mixing_bias, down_bias, final_gain, final_bias
    ]
    small = jnp.concatenate([jnp.stack(vectors), up_bias.reshape(ratio, own)]).T
    small = jnp.pad(small, ((0, 0), (0, 128 - small.shape[1])))
    pieces = []
    for k in range(ctx):
        at = (me ^ k) * cols
        parts = [
            lax.dynamic_slice_in_dim(w, at + p * 128, 128, 1)
            for p in range(cols // 128)
            for w in (query_weight, key_weight, value_weight)
        ] + [lax.dynamic_slice_in_dim(time_weight, at, cols, 1)]
        pieces.append(jnp.concatenate(parts + [small], axis=1))
    first = jnp.concatenate(to_absolute(trade(pieces, "ctx"), me))
    first = gather_stacked(first[None], "dp")
    first = jnp.concatenate(
        [
            lax.dynamic_index_in_dim(first, flipped((me_dp ^ c), dp), 0, False)
            for c in range(dp)
        ]
    )
    qkv_weight = first[:, : 3 * cols]
    table = first[:, 4 * cols :].astype(f32).T
    time_shift_bias, query_shift, value_shift, output_shift, gain_one, bias_one, down_shift, gain_two, bias_two = [
        table[n] for n in range(len(vectors))
    ]
    up_shift = table[len(vectors) : len(vectors) + ratio].reshape(ratio, devices, own).transpose(1, 0, 2).reshape(hidden)
    shift_cols = trade([nn(time_feat, first[:, 3 * cols : 4 * cols])] * ctx, "ctx")
    time_shift = jnp.concatenate(to_absolute(shift_cols, me), axis=1) + time_shift_bias
    qkv_shift = []
    for p in range(cols // 128):
        at = me * cols + p * 128
        qkv_shift.append(lax.dynamic_slice_in_dim(query_shift, at, 128))
        qkv_shift.append(jnp.zeros((128,), f32))
        qkv_shift.append(lax.dynamic_slice_in_dim(value_shift, at, 128))
    qkv_shift = jnp.concatenate(qkv_shift)
    start_row = (jnp.concatenate(token_chunks).astype(f32) + time_shift).astype(bf16)
    residual_in = tokens.astype(f32) + time_shift
    qkv = (nn(start_row, qkv_weight) + qkv_shift).astype(bf16)

    info = spans(ids, me)
    ids_col, ids_row = ids.reshape(-1, 1), ids.reshape(-1, 1, BLOCK)
    mixed, logsum = attention_forward(info, qkv, ids_col, ids_row, per_chunk)
    returned = trade([mixed[k * piece : (k + 1) * piece] for k in range(ctx)], "ctx")
    attended = jnp.concatenate(to_absolute(returned, me), axis=1)

    branch = nn(attended, output_full) + output_shift
    hidden_one, normed_one, inverse_one = normalize(residual_in + branch, gain_one, bias_one)
    hidden_low = hidden_one.astype(bf16)
    pre_gelu = nn(hidden_low, up_full) + up_shift
    share = 0.5 * (1.0 + lax.erf(pre_gelu * 0.5**0.5))
    activated = (pre_gelu * share).astype(bf16)
    slope = (share + pre_gelu * jnp.exp(-0.5 * pre_gelu * pre_gelu) * 0.3989422804014327).astype(bf16)
    activated, slope = lax.optimization_barrier((activated, slope))
    feed_out = nn(activated, down_full) + down_shift
    result, normed_two, inverse_two = normalize(hidden_one + feed_out, gain_two, bias_two)
    layer_out = result.astype(bf16)

    upstream = cotangent.astype(f32)
    grad_two, gain_two_grad, bias_two_grad = normalize_back(upstream, normed_two, inverse_two, gain_two)
    grad_feed = grad_two.astype(bf16)
    down_grad = tn(activated, grad_feed).astype(bf16)
    down_shift_grad = jnp.sum(grad_feed.astype(f32), axis=0)
    grad_inner = (nt(grad_feed, down_full) * slope.astype(f32)).astype(bf16)
    up_grad = tn(hidden_low, grad_inner).astype(bf16)
    up_shift_grad = jnp.sum(grad_inner.astype(f32), axis=0)
    grad_hidden = grad_two + nt(grad_inner, up_full)
    grad_one, gain_one_grad, bias_one_grad = normalize_back(grad_hidden, normed_one, inverse_one, gain_one)
    grad_branch = grad_one.astype(bf16)
    output_grad = tn(attended, grad_branch).astype(bf16)
    output_shift_grad = jnp.sum(grad_branch.astype(f32), axis=0)
    vector_grads = jnp.stack(
        [output_shift_grad, gain_one_grad, bias_one_grad, down_shift_grad, gain_two_grad, bias_two_grad]
    )
    vector_grads = lax.optimization_barrier(vector_grads).reshape(6, devices, own).transpose(1, 0, 2).reshape(devices, 6 * own)
    vector_grads = jnp.concatenate([vector_grads, up_shift_grad.reshape(devices, ratio * own)], axis=1)
    vector_grads = jnp.pad(vector_grads, ((0, 0), (0, width - vector_grads.shape[1]))).astype(bf16)
    extra = 8
    rest_grad = jnp.concatenate(
        [output_grad.reshape(devices, own, width), jnp.broadcast_to(vector_grads[:, None], (devices, extra, width))],
        axis=1,
    )

    dp_names, ctx_names = [("dp", b) for b in bits(dp)], [("ctx", b) for b in bits(ctx)]
    names = dp_names[::-1] + ctx_names[::-1]
    core, turn, rest = ctx_names[0], dp_names[:2] + ctx_names[1:], dp_names[2:]
    whole = {}
    for label, array, height in (("down", down_grad, ratio * own), ("up", up_grad, own), ("rest", rest_grad, own + extra)):
        size = (height, array.shape[-1])
        whole[label] = Halving(names, size)
        whole[label].terms = [(array.reshape([2] * len(names) + list(size)), names, [(0, d) for d in size])]
        whole[label].exchange(core)

    def stream(label, part, turned):
        sums = Halving(names, [high - low for low, high in part])
        sums.fixed = {core: sums.me[core]}
        sums.terms = [(array, left, part) for array, left, _ in whole[label].terms]
        return sums, turn[turned:] + turn[:turned] + rest

    most, tall = 3 * hidden // 4, (ratio - 1) * own
    streams = [
        stream("up", [(0, own), (0, most)], 2),
        stream("down", [(0, tall), (0, width)], 0),
        stream("up", [(0, own), (most, hidden)], 1),
        stream("down", [(tall, ratio * own), (0, width)], 1),
        stream("rest", [(0, own + extra), (0, width)], 1),
    ]

    grad_attended = nt(grad_branch, output_full).astype(bf16)
    pieces = [lax.dynamic_slice_in_dim(grad_attended, (me ^ k) * cols, cols, 1) for k in range(ctx)]
    grad_mixed = jnp.concatenate(trade(pieces, "ctx"))
    def weight_stream(grad):
        size = (ctx * own, grad.shape[1])
        sums = Halving(dp_names[::-1], size)
        array = tn(start_row, grad).reshape([2] * len(dp_names) + list(size))
        sums.terms = [(array, dp_names[::-1], [(0, d) for d in size])]
        return sums, list(dp_names)

    def start_part(k):
        rows = slice(k * piece, (k + 1) * piece)
        return nt(jnp.concatenate([g[rows] for g in grads], axis=1), qkv_weight)

    def depart(moving, beside):
        going = [s.outgoing(name) for s, name in moving]
        going, beside = lax.optimization_barrier((going, beside))
        return [(s, name, swap(value, *name)) for (s, name), value in zip(moving, going)], beside

    def land(flights, beside):
        values, beside = lax.optimization_barrier(([value for _, _, value in flights], beside))
        for (s, name, _), value in zip(flights, values):
            s.arrived(name, value)
        return beside

    def following(pairs):
        return [(s, o.pop(0)) for s, o in pairs if o]

    grads, pair_streams = [], []
    for pair in range(cols // 128):
        flights, grad_mixed = depart(following(streams + pair_streams), grad_mixed)
        grad = attention_backward(pair, info, qkv, grad_mixed, mixed, logsum, ids_col, ids_row, per_chunk)
        grad_mixed, grad = land(flights, (grad_mixed, grad))
        grads.append(grad)
        pair_streams.append(weight_stream(grad))

    qkv_sum = jnp.concatenate([jnp.sum(g.astype(f32), axis=0) for g in grads])
    row_sum = jnp.sum(grad_one, axis=0, keepdims=True) + lax.dot_general(
        qkv_sum[None],
        qkv_weight.astype(f32),
        (((1,), (1,)), ((), ())),
        precision=lax.Precision.HIGHEST,
        preferred_element_type=f32,
    )
    message = jnp.concatenate(
        [row_sum]
        + [qkv_sum[None, (3 * p + n) * 128 : (3 * p + n + 1) * 128] for n in (0, 2) for p in range(cols // 128)]
        + [time_feat.astype(f32)],
        axis=1,
    )
    message_names = dp_names[::-1]

    odd = [start_part(k).astype(bf16) for k in range(1, ctx, 2)]
    flights, (grads, odd, message) = depart(following(streams + pair_streams), (grads, odd, message))
    odd = [swap(value, *core) for value in odd]
    reply = swap(message, *message_names.pop(0))
    even = [start_part(k) for k in range(0, ctx, 2)]
    even, odd, message, reply = land(flights, (even, odd, message, reply))
    message = jnp.concatenate([message, reply])
    even = [e + o.astype(f32) for e, o in zip(even, odd)]
    away = [value.astype(bf16) for value in even[1:]]
    kept, came = [], None
    while any(o for _, o in streams + pair_streams) or message_names:
        fast, slow = following(pair_streams), following(streams)
        flights, (away, message) = depart(fast + slow, (away, message))
        if came is None:
            came = [swap(value, "ctx", 2 * n + 2) for n, value in enumerate(away)]
        if message_names:
            message = jnp.concatenate([message, swap(message, *message_names.pop(0))])
        kept += flights[len(fast) :]
        flights = flights[: len(fast)]
        if any(o for _, o in streams):
            flights, kept = flights + kept, []
        if not any(o for _, o in pair_streams):
            flights, kept = flights + kept, []
        message, came = land(flights, (message, came)) if not kept else (land(flights, message), came)
    summed = jnp.concatenate([s.result() for s, _ in pair_streams], axis=1).reshape(ctx, own, 3 * cols)
    summed = [lax.dynamic_index_in_dim(summed, (me ^ k), 0, False) for k in range(ctx)]
    summed, message = lax.optimization_barrier((summed, message))
    blocks_out = to_absolute(trade(summed, "ctx"), me)
    message = jnp.stack(trade([message] * ctx, "ctx"))
    tokens_grad = (grad_one + sum([c.astype(f32) for c in came], even[0])).astype(bf16)
    up_left, down_left, up_right, down_right, rest_left = [s.result() for s, _ in streams]
    up_weight_grad = jnp.concatenate([up_left, up_right], axis=1)
    down_weight_grad = jnp.concatenate([down_left, down_right])
    output_weight_grad, vector_grads = rest_left[:own], rest_left[own]
    output_bias_grad, mixing_gain_grad, mixing_bias_grad, down_bias_grad, final_gain_grad, final_bias_grad = [
        vector_grads[n * own : (n + 1) * own] for n in range(6)
    ]
    up_bias_grad = vector_grads[6 * own : (6 + ratio) * own]

    mine = (me_dp * ctx + me) * own
    row_sums = jnp.sum(message[:, :, :width], axis=0)
    time_weight_grad = lax.dot_general(
        lax.dynamic_slice_in_dim(message[0, :, width + 2 * cols :], mine, own, 1),
        row_sums,
        (((0,), (0,)), ((), ())),
        precision=lax.Precision.HIGHEST,
        preferred_element_type=f32,
    )
    time_bias_grad = lax.dynamic_slice_in_dim(jnp.sum(row_sums, axis=0), mine, own)
    sums = jnp.sum(message[:, :, width : width + 2 * cols], axis=1)
    sums = lax.dynamic_index_in_dim(sums, mine // cols ^ me, 0, False)
    query_bias_grad = lax.dynamic_slice_in_dim(sums[:cols], mine % cols, own)
    value_bias_grad = lax.dynamic_slice_in_dim(sums[cols:], mine % cols, own)

    query_weight_grad, key_weight_grad, value_weight_grad = [
        jnp.concatenate(
            [
                block[:, (3 * p + n) * 128 : (3 * p + n + 1) * 128]
                for block in blocks_out
                for p in range(cols // 128)
            ],
            axis=1,
        )
        for n in range(3)
    ]
    return (
        layer_out[None],
        tokens_grad[None],
        time_weight_grad,
        time_bias_grad,
        query_weight_grad,
        query_bias_grad,
        key_weight_grad,
        value_weight_grad,
        value_bias_grad,
        output_weight_grad,
        output_bias_grad,
        mixing_gain_grad,
        mixing_bias_grad,
        up_weight_grad,
        up_bias_grad,
        down_weight_grad,
        down_bias_grad,
        final_gain_grad,
        final_bias_grad,
    )


def solution(mesh):
    rows, split_rows, split = P("dp", "ctx", None), P(BOTH, None), P(BOTH)
    return jax.shard_map(
        shards,
        mesh=mesh,
        in_specs=(
            rows, P("dp", None), rows, P("dp", None), split_rows, split, split_rows, split, split_rows, split_rows,
            split, split_rows, split, split, split, split_rows, split, split_rows, split, split, split,
        ),
        out_specs=(
            rows, rows, split_rows, split, split_rows, split, split_rows, split_rows, split, split_rows, split, split,
            split, split_rows, split, split_rows, split, split, split,
        ),
        check_vma=False,
    )
```

```python
import functools

import jax
import jax.numpy as jnp
from jax import lax
from jax.experimental import pallas as pl
from jax.experimental.pallas import tpu as pltpu
from jax.sharding import PartitionSpec as P

HEAD_DIM = 64
BLOCK = 256
MASKED = -1e30
EPSILON = 1e-05
SCALE = HEAD_DIM**-0.5
SCALE_LOG2 = SCALE * 1.4426950408889634
BOTH = ("dp", "ctx")
f32, bf16 = jnp.float32, jnp.bfloat16


def nn(left, right):
    return jnp.dot(left, right, preferred_element_type=f32)


def tn(left, right):
    return lax.dot_general(left, right, (((0,), (0,)), ((), ())), preferred_element_type=f32)


def nt(left, right):
    return lax.dot_general(left, right, (((1,), (1,)), ((), ())), preferred_element_type=f32)


def head_only(pair, which):
    lane = lax.broadcasted_iota(jnp.int32, pair.shape, 1)
    keep = (lane < HEAD_DIM) if which == 0 else (lane >= HEAD_DIM)
    return jnp.where(keep, pair, jnp.zeros_like(pair))


def place(block, me, per_chunk):
    return lax.bitwise_xor(block // per_chunk, me) * per_chunk + lax.rem(block, per_chunk)


def forward_kernel(per_chunk, pairs, info, qkv_ref, idc_ref, idr_ref, o_ref, lse_ref, o_acc, m_acc, l_acc):
    i = pl.program_id(0)
    me = info[2, 0]
    m_acc[...] = jnp.full_like(m_acc, MASKED)
    l_acc[...] = jnp.zeros_like(l_acc)
    o_acc[...] = jnp.zeros_like(o_acc)
    ids_q = idr_ref[pl.ds(i, 1)][0]
    here = pl.multiple_of(place(i, me, per_chunk) * BLOCK, BLOCK)

    queries = []
    for p in range(pairs):
        pair = qkv_ref[pl.ds(here, BLOCK), (3 * p) * 128 : (3 * p + 1) * 128]
        queries += [head_only(pair, 0), head_only(pair, 1)]

    def step(j, carry):
        at = pl.multiple_of(place(j, me, per_chunk) * BLOCK, BLOCK)
        same = idc_ref[pl.ds(pl.multiple_of(j * BLOCK, BLOCK), BLOCK), :] == ids_q
        heads = range(2 * pairs)
        peak = [m_acc[h] for h in heads]
        count = [l_acc[h] for h in heads]
        mixed = [o_acc[h * HEAD_DIM : (h + 1) * HEAD_DIM] for h in heads]
        values, scores = [], []
        for p in range(pairs):
            k_pair = qkv_ref[pl.ds(at, BLOCK), (3 * p + 1) * 128 : (3 * p + 2) * 128]
            values.append(qkv_ref[pl.ds(at, BLOCK), (3 * p + 2) * 128 : (3 * p + 3) * 128])
            scores += [nt(k_pair, queries[2 * p + w]) for w in range(2)]
        for h in heads:
            t = jnp.where(same, scores[h] * SCALE_LOG2, MASKED)
            new = jnp.maximum(peak[h], jnp.max(t, axis=0, keepdims=True))
            alpha = jnp.exp2(peak[h] - new)
            e = jnp.exp2(t - new)
            count[h] = count[h] * alpha + jnp.sum(e, axis=0, keepdims=True)
            peak[h] = new
            w = h % 2
            mixed[h] = mixed[h] * alpha + tn(values[h // 2], e.astype(bf16))[w * HEAD_DIM : (w + 1) * HEAD_DIM]
        for h in heads:
            m_acc[h], l_acc[h] = peak[h], count[h]
            o_acc[h * HEAD_DIM : (h + 1) * HEAD_DIM] = mixed[h]
        return carry

    lax.fori_loop(info[0, i], info[1, i], step, 0)
    for p in range(pairs):
        parts = []
        for w in range(2):
            h = 2 * p + w
            parts.append(o_acc[h * HEAD_DIM : (h + 1) * HEAD_DIM] / l_acc[h])
            lse_ref[0, h : h + 1, :] = m_acc[h] + jnp.log2(l_acc[h])
        o_ref[:, p * 128 : (p + 1) * 128] = jnp.concatenate(parts, axis=0).T.astype(bf16)


def attention_forward(info, qkv, ids_col, ids_row, per_chunk):
    rows, width = qkv.shape[0], qkv.shape[1] // 3
    blocks, heads = rows // BLOCK, width // HEAD_DIM
    return pl.pallas_call(
        functools.partial(forward_kernel, per_chunk, heads // 2),
        grid_spec=pltpu.PrefetchScalarGridSpec(
            num_scalar_prefetch=1,
            grid=(blocks,),
            in_specs=[
                pl.BlockSpec((rows, 3 * width), lambda i, info: (0, 0)),
                pl.BlockSpec((rows, 1), lambda i, info: (0, 0)),
                pl.BlockSpec((blocks, 1, BLOCK), lambda i, info: (0, 0, 0)),
            ],
            out_specs=[
                pl.BlockSpec((BLOCK, width), lambda i, info: (place(i, info[2, 0], per_chunk), 0)),
                pl.BlockSpec((1, heads, BLOCK), lambda i, info: (i, 0, 0)),
            ],
            scratch_shapes=[
                pltpu.VMEM((width, BLOCK), f32),
                pltpu.VMEM((heads, 1, BLOCK), f32),
                pltpu.VMEM((heads, 1, BLOCK), f32),
            ],
        ),
        out_shape=[
            jax.ShapeDtypeStruct((rows, width), bf16),
            jax.ShapeDtypeStruct((blocks, heads, BLOCK), f32),
        ],
        cost_estimate=pl.CostEstimate(flops=30 * 10**9, bytes_accessed=6 * rows * width, transcendentals=10**7),
        name="attention_forward",
    )(info, qkv, ids_col, ids_row)


def backward_kernel(
    per_chunk, first, info, q_ref, k_ref, v_ref, do_ref, o_ref, lse_ref, idc_ref, idr_ref,
    out_ref, delta_ref, dq_acc, dk_acc, dv_acc,
):
    j = pl.program_id(0)
    blocks = pl.num_programs(0)
    me = info[2, 0]

    @pl.when(j == 0)
    def _():
        dq_acc[...] = jnp.zeros_like(dq_acc)

        def fill(i, carry):
            at = pl.multiple_of(place(i, me, per_chunk) * BLOCK, BLOCK)
            prod = (do_ref[pl.ds(at, BLOCK), :].astype(f32) * o_ref[pl.ds(at, BLOCK), :].astype(f32)).T
            for w in range(2):
                delta_ref[i, w : w + 1, :] = jnp.sum(prod[w * HEAD_DIM : (w + 1) * HEAD_DIM], axis=0, keepdims=True)
            return carry

        lax.fori_loop(0, blocks, fill, 0)

    dk_acc[...] = jnp.zeros_like(dk_acc)
    dv_acc[...] = jnp.zeros_like(dv_acc)
    ids_k = idc_ref[pl.ds(pl.multiple_of(j * BLOCK, BLOCK), BLOCK), :]

    def step(i, carry):
        at = pl.multiple_of(place(i, me, per_chunk) * BLOCK, BLOCK)
        same = ids_k == idr_ref[pl.ds(i, 1)][0]
        k_pair, v_pair = k_ref[...], v_ref[...]
        q_pair, do_pair = q_ref[pl.ds(at, BLOCK), :], do_ref[pl.ds(at, BLOCK), :]
        dv, dk, dq = [], [], []
        for w in range(2):
            q_one, do_one = head_only(q_pair, w), head_only(do_pair, w)
            t = nt(k_pair, q_one) * SCALE_LOG2 - lse_ref[i, first + w : first + w + 1, :]
            e = jnp.exp2(jnp.where(same, t, MASKED))
            ds = (e * (nt(v_pair, do_one) - delta_ref[i, w : w + 1, :])).astype(bf16)
            dv.append(nn(e.astype(bf16), do_one))
            dk.append(nn(ds, q_one))
            dq.append(tn(ds, head_only(k_pair, w)))
        dv_acc[...] += dv[0] + dv[1]
        dk_acc[...] += dk[0] + dk[1]
        dq_acc[pl.ds(at, BLOCK), :] += dq[0] + dq[1]
        return carry

    lax.fori_loop(info[0, j], info[1, j], step, 0)
    mine = pl.multiple_of(place(j, me, per_chunk) * BLOCK, BLOCK)
    out_ref[pl.ds(mine, BLOCK), 128:256] = (dk_acc[...] * SCALE).astype(bf16)
    out_ref[pl.ds(mine, BLOCK), 256:384] = dv_acc[...].astype(bf16)

    @pl.when(j == blocks - 1)
    def _():
        out_ref[:, 0:128] = (dq_acc[...] * SCALE).astype(bf16)


def attention_backward(pair, info, qkv, do, o, lse, ids_col, ids_row, per_chunk):
    rows, width = o.shape
    blocks, heads = rows // BLOCK, width // HEAD_DIM
    return pl.pallas_call(
        functools.partial(backward_kernel, per_chunk, 2 * pair),
        grid_spec=pltpu.PrefetchScalarGridSpec(
            num_scalar_prefetch=1,
            grid=(blocks,),
            in_specs=[
                pl.BlockSpec((rows, 128), lambda i, info: (0, 3 * pair)),
                pl.BlockSpec((BLOCK, 128), lambda i, info: (place(i, info[2, 0], per_chunk), 3 * pair + 1)),
                pl.BlockSpec((BLOCK, 128), lambda i, info: (place(i, info[2, 0], per_chunk), 3 * pair + 2)),
                pl.BlockSpec((rows, 128), lambda i, info: (0, pair)),
                pl.BlockSpec((rows, 128), lambda i, info: (0, pair)),
                pl.BlockSpec((blocks, heads, BLOCK), lambda i, info: (0, 0, 0)),
                pl.BlockSpec((rows, 1), lambda i, info: (0, 0)),
                pl.BlockSpec((blocks, 1, BLOCK), lambda i, info: (0, 0, 0)),
            ],
            out_specs=pl.BlockSpec((rows, 384), lambda i, info: (0, 0)),
            scratch_shapes=[
                pltpu.VMEM((blocks, 2, BLOCK), f32),
                pltpu.VMEM((rows, 128), f32),
                pltpu.VMEM((BLOCK, 128), f32),
                pltpu.VMEM((BLOCK, 128), f32),
            ],
        ),
        out_shape=jax.ShapeDtypeStruct((rows, 384), bf16),
        cost_estimate=pl.CostEstimate(flops=25 * 10**9, bytes_accessed=8 * rows * 128, transcendentals=10**7),
        name="attention_backward",
    )(info, qkv, qkv, qkv, do, o, lse, ids_col, ids_row)


def spans(ids, me):
    blocks = ids.shape[0] // BLOCK
    per_block = ids.reshape(blocks, BLOCK)
    low = jnp.sum(ids[None, :] < per_block[:, :1], axis=1) // BLOCK
    high = (jnp.sum(ids[None, :] <= per_block[:, -1:], axis=1) + BLOCK - 1) // BLOCK
    return jnp.stack([low, high, jnp.full((blocks,), me.astype(low.dtype))]).astype(jnp.int32)


def own_index(axis):
    return lax.axis_index(axis).astype(jnp.uint32)


def swap(value, axis, mask):
    size = lax.axis_size(axis)
    return lax.ppermute(value, axis, [(i, i ^ mask) for i in range(size)])


def bits(size):
    return [1 << b for b in range(size.bit_length() - 1)]


def flipped(index, size):
    flags = bits(size)
    return sum(((index >> n) & 1) << (len(flags) - 1 - n) for n in range(len(flags)))


def trade(pieces, axis):
    return [pieces[0]] + [swap(pieces[k], axis, k) for k in range(1, len(pieces))]


def to_absolute(pieces, me):
    stacked = jnp.stack(pieces)
    return [lax.dynamic_index_in_dim(stacked, (me ^ c), 0, False) for c in range(len(pieces))]


class Halving:
    def __init__(self, names, shape):
        self.me = {n: (own_index(n[0]) >> (n[1].bit_length() - 1)) & 1 for n in names}
        self.names, self.terms, self.fixed, self.shape = list(names), [], {}, shape

    def cut(self, term, chosen):
        array, names, part = term
        starts, sizes = [], []
        for n in names:
            starts.append(chosen.get(n, jnp.uint32(0)))
            sizes.append(1 if n in chosen else 2)
        for low, high in part:
            starts.append(jnp.uint32(low))
            sizes.append(high - low)
        left = [2 for n in names if n not in chosen]
        return lax.dynamic_slice(array, starts, sizes).reshape(left + [h - l for l, h in part])

    def total(self, chosen):
        pieces = [self.cut(t, chosen).astype(f32) for t in self.terms]
        return sum(pieces[1:], pieces[0])

    def outgoing(self, name):
        return self.total({**self.fixed, name: 1 - self.me[name]}).astype(bf16)

    def arrived(self, name, value):
        self.fixed[name] = self.me[name]
        names = [n for n in self.names if n not in self.fixed]
        self.terms.append((value, names, [(0, d) for d in self.shape]))

    def exchange(self, name):
        self.arrived(name, swap(self.outgoing(name), *name))

    def result(self):
        return self.total(self.fixed)


def normalize(values, gain, shift):
    average = jnp.mean(values, axis=-1, keepdims=True)
    centered = values - average
    inverse = lax.rsqrt(jnp.mean(centered * centered, axis=-1, keepdims=True) + EPSILON)
    normed = centered * inverse
    return normed * gain + shift, normed, inverse


def normalize_back(upstream, normed, inverse, gain):
    scaled = upstream * gain
    plain = jnp.mean(scaled, axis=-1, keepdims=True)
    cross = jnp.mean(scaled * normed, axis=-1, keepdims=True)
    result = inverse * (scaled - plain - normed * cross)
    return result, jnp.sum(upstream * normed, axis=0), jnp.sum(upstream, axis=0)


def shards(
    tokens, time_feat, cotangent, segment_ids, time_weight, time_bias, query_weight, query_bias, key_weight,
    value_weight, value_bias, output_weight, output_bias, mixing_gain, mixing_bias, up_weight, up_bias,
    down_weight, down_bias, final_gain, final_bias,
):
    me_dp, me = own_index("dp"), own_index("ctx")
    dp, ctx = lax.axis_size("dp"), lax.axis_size("ctx")
    devices = dp * ctx
    piece, width = tokens.shape[1], tokens.shape[2]
    hidden = up_weight.shape[1]
    own, ratio = width // devices, hidden // width
    cols = width // ctx
    per_chunk = piece // BLOCK
    tokens, cotangent, ids = tokens[0], cotangent[0], segment_ids[0]

    second = lax.all_gather(
        jnp.concatenate([up_weight, output_weight] + [down_weight[n * own : (n + 1) * own] for n in range(ratio)], axis=1),
        BOTH,
        axis=0,
        tiled=True,
    )
    up_full, output_full = second[:, :hidden], second[:, hidden : hidden + width]
    down_full = jnp.stack(
        [second[:, hidden + n * width : hidden + (n + 1) * width].reshape(devices, own, width) for n in range(1, 1 + ratio)],
        axis=1,
    ).reshape(hidden, width)

    held = {0: tokens, ctx // 2: swap(tokens, "ctx", ctx // 2)}
    vectors = [
        time_bias, query_bias, value_bias, output_bias, mixing_gain, mixing_bias, down_bias, final_gain, final_bias
    ]
    small = jnp.concatenate([jnp.stack(vectors), up_bias.reshape(ratio, own)]).T
    small = jnp.pad(small, ((0, 0), (0, 128 - small.shape[1])))
    pieces = []
    for k in range(ctx):
        at = (me ^ k) * cols
        parts = [
            lax.dynamic_slice_in_dim(w, at + p * 128, 128, 1)
            for p in range(cols // 128)
            for w in (query_weight, key_weight, value_weight)
        ] + [lax.dynamic_slice_in_dim(time_weight, at, cols, 1)]
        pieces.append(jnp.concatenate(parts + [small], axis=1))
    first = jnp.concatenate(to_absolute(trade(pieces, "ctx"), me))
    first = first[None]
    for n, bit in enumerate(reversed(bits(dp))):
        if n == 1:
            first, held[ctx // 2] = lax.optimization_barrier((first, held[ctx // 2]))
        first = jnp.concatenate([first, swap(first, "dp", bit)])
    for bit in reversed(bits(ctx)[:-1]):
        held.update({k | bit: swap(v, "ctx", bit) for k, v in list(held.items())})
    token_chunks = [held[k] for k in range(ctx)]
    first = jnp.concatenate(
        [
            lax.dynamic_index_in_dim(first, flipped((me_dp ^ c), dp), 0, False)
            for c in range(dp)
        ]
    )
    qkv_weight = first[:, : 3 * cols]
    table = first[:, 4 * cols :].astype(f32).T
    time_shift_bias, query_shift, value_shift, output_shift, gain_one, bias_one, down_shift, gain_two, bias_two = [
        table[n] for n in range(len(vectors))
    ]
    up_shift = table[len(vectors) : len(vectors) + ratio].reshape(ratio, devices, own).transpose(1, 0, 2).reshape(hidden)
    shift_cols = trade([nn(time_feat, first[:, 3 * cols : 4 * cols])] * ctx, "ctx")
    time_shift = jnp.concatenate(to_absolute(shift_cols, me), axis=1) + time_shift_bias
    qkv_shift = []
    for p in range(cols // 128):
        at = me * cols + p * 128
        qkv_shift.append(lax.dynamic_slice_in_dim(query_shift, at, 128))
        qkv_shift.append(jnp.zeros((128,), f32))
        qkv_shift.append(lax.dynamic_slice_in_dim(value_shift, at, 128))
    qkv_shift = jnp.concatenate(qkv_shift)
    start_row = (jnp.concatenate(token_chunks).astype(f32) + time_shift).astype(bf16)
    residual_in = tokens.astype(f32) + time_shift
    qkv = (nn(start_row, qkv_weight) + qkv_shift).astype(bf16)

    info = spans(ids, me)
    ids_col, ids_row = ids.reshape(-1, 1), ids.reshape(-1, 1, BLOCK)
    mixed, logsum = attention_forward(info, qkv, ids_col, ids_row, per_chunk)
    returned = trade([mixed[k * piece : (k + 1) * piece] for k in range(ctx)], "ctx")
    attended = jnp.concatenate(to_absolute(returned, me), axis=1)

    branch = nn(attended, output_full) + output_shift
    hidden_one, normed_one, inverse_one = normalize(residual_in + branch, gain_one, bias_one)
    hidden_low = hidden_one.astype(bf16)
    pre_gelu = nn(hidden_low, up_full) + up_shift
    share = 0.5 * (1.0 + lax.erf(pre_gelu * 0.5**0.5))
    activated = (pre_gelu * share).astype(bf16)
    slope = (share + pre_gelu * jnp.exp(-0.5 * pre_gelu * pre_gelu) * 0.3989422804014327).astype(bf16)
    activated, slope = lax.optimization_barrier((activated, slope))
    feed_out = nn(activated, down_full) + down_shift
    result, normed_two, inverse_two = normalize(hidden_one + feed_out, gain_two, bias_two)
    layer_out = result.astype(bf16)

    upstream = cotangent.astype(f32)
    grad_two, gain_two_grad, bias_two_grad = normalize_back(upstream, normed_two, inverse_two, gain_two)
    grad_feed = grad_two.astype(bf16)
    down_grad = tn(activated, grad_feed).astype(bf16)
    down_shift_grad = jnp.sum(grad_feed.astype(f32), axis=0)
    grad_inner = (nt(grad_feed, down_full) * slope.astype(f32)).astype(bf16)
    up_grad = tn(hidden_low, grad_inner).astype(bf16)
    up_shift_grad = jnp.sum(grad_inner.astype(f32), axis=0)
    grad_hidden = grad_two + nt(grad_inner, up_full)
    grad_one, gain_one_grad, bias_one_grad = normalize_back(grad_hidden, normed_one, inverse_one, gain_one)
    grad_branch = grad_one.astype(bf16)
    dp_names, ctx_names = [("dp", b) for b in bits(dp)], [("ctx", b) for b in bits(ctx)]
    names = dp_names[::-1] + ctx_names[::-1]
    core, turn, rest = ctx_names[0], dp_names[:2] + ctx_names[1:], dp_names[2:]
    whole = {}

    def share(label, array, height):
        size = (height, array.shape[-1])
        whole[label] = Halving(names, size)
        whole[label].terms = [(array.reshape([2] * len(names) + list(size)), names, [(0, d) for d in size])]
        whole[label].exchange(core)

    def stream(label, part, turned):
        sums = Halving(names, [high - low for low, high in part])
        sums.fixed = {core: sums.me[core]}
        sums.terms = [(array, left, part) for array, left, _ in whole[label].terms]
        return sums, turn[turned:] + turn[:turned] + rest

    def depart(moving, beside):
        going = [s.outgoing(name) for s, name in moving]
        going, beside = lax.optimization_barrier((going, beside))
        return [(s, name, swap(value, *name)) for (s, name), value in zip(moving, going)], beside

    def land(flights, beside):
        values, beside = lax.optimization_barrier(([value for _, _, value in flights], beside))
        for (s, name, _), value in zip(flights, values):
            s.arrived(name, value)
        return beside

    def following(pairs):
        return [(s, o.pop(0)) for s, o in pairs if o]

    share("down", down_grad, ratio * own)
    streams = [stream("down", [(0, ratio * own), (0, width)], 0)]
    ahead, grad_branch = depart(following(streams), grad_branch)

    output_grad = tn(attended, grad_branch).astype(bf16)
    output_shift_grad = jnp.sum(grad_branch.astype(f32), axis=0)
    vector_grads = jnp.stack(
        [output_shift_grad, gain_one_grad, bias_one_grad, down_shift_grad, gain_two_grad, bias_two_grad]
    )
    vector_grads = lax.optimization_barrier(vector_grads).reshape(6, devices, own).transpose(1, 0, 2).reshape(devices, 6 * own)
    vector_grads = jnp.concatenate([vector_grads, up_shift_grad.reshape(devices, ratio * own)], axis=1)
    vector_grads = jnp.pad(vector_grads, ((0, 0), (0, width - vector_grads.shape[1]))).astype(bf16)
    extra = 8
    rest_grad = jnp.concatenate(
        [output_grad.reshape(devices, own, width), jnp.broadcast_to(vector_grads[:, None], (devices, extra, width))],
        axis=1,
    )

    share("up", up_grad, own)
    share("rest", rest_grad, own + extra)
    streams += [
        stream("up", [(0, own), (0, hidden // 2)], 2),
        stream("up", [(0, own), (hidden // 2, hidden)], 0),
        stream("rest", [(0, own + extra), (0, width)], 0),
    ]

    grad_attended = nt(grad_branch, output_full).astype(bf16)
    pieces = [lax.dynamic_slice_in_dim(grad_attended, (me ^ k) * cols, cols, 1) for k in range(ctx)]
    grad_mixed = jnp.concatenate(trade(pieces, "ctx"))
    grad_mixed = land(ahead, grad_mixed)

    def weight_stream(grad):
        size = (ctx * own, grad.shape[1])
        sums = Halving(dp_names[::-1], size)
        array = tn(start_row, grad).reshape([2] * len(dp_names) + list(size))
        sums.terms = [(array, dp_names[::-1], [(0, d) for d in size])]
        return sums, list(dp_names)

    grads, pair_streams = [], []
    for pair in range(cols // 128):
        flights, grad_mixed = depart(following(streams + pair_streams), grad_mixed)
        grad = attention_backward(pair, info, qkv, grad_mixed, mixed, logsum, ids_col, ids_row, per_chunk)
        grad_mixed, grad = land(flights, (grad_mixed, grad))
        grads.append(grad)
        pair_streams.append(weight_stream(grad))

    qkv_sum = jnp.concatenate([jnp.sum(g.astype(f32), axis=0) for g in grads])
    row_sum = jnp.sum(grad_one, axis=0, keepdims=True) + lax.dot_general(
        qkv_sum[None],
        qkv_weight.astype(f32),
        (((1,), (1,)), ((), ())),
        precision=lax.Precision.HIGHEST,
        preferred_element_type=f32,
    )
    message = jnp.concatenate(
        [row_sum]
        + [qkv_sum[None, (3 * p + n) * 128 : (3 * p + n + 1) * 128] for n in (0, 2) for p in range(cols // 128)]
        + [time_feat.astype(f32)],
        axis=1,
    )
    message_names = dp_names[::-1]

    rows = jnp.concatenate(grads, axis=1).reshape(ctx // 2, 2, piece, 3 * cols)
    odd = nt(rows[:, 1].reshape(-1, 3 * cols), qkv_weight).astype(bf16)
    flights, (rows, odd, message) = depart(following(streams + pair_streams), (rows, odd, message))
    odd = swap(odd, *core)
    reply = swap(message, *message_names.pop(0))
    even = nt(rows[:, 0].reshape(-1, 3 * cols), qkv_weight)
    even, odd, message, reply = land(flights, (even, odd, message, reply))
    message = jnp.concatenate([message, reply])
    even = (even + odd.astype(f32)).reshape(ctx // 2, piece, width)
    away = [even[n].astype(bf16) for n in range(1, ctx // 2)]
    kept, came = [], None
    while any(o for _, o in streams + pair_streams) or message_names:
        fast, slow = following(pair_streams), following(streams)
        flights, (away, message) = depart(fast + slow, (away, message))
        if came is None:
            came = [swap(value, "ctx", 2 * n + 2) for n, value in enumerate(away)]
        if message_names:
            message = jnp.concatenate([message, swap(message, *message_names.pop(0))])
        kept += flights[len(fast) :]
        flights = flights[: len(fast)]
        if any(o for _, o in streams):
            flights, kept = flights + kept, []
        if not any(o for _, o in pair_streams):
            flights, kept = flights + kept, []
        message, came = land(flights, (message, came)) if not kept else (land(flights, message), came)
    summed = jnp.concatenate([s.result() for s, _ in pair_streams], axis=1).reshape(ctx, own, 3 * cols)
    summed = [lax.dynamic_index_in_dim(summed, (me ^ k), 0, False) for k in range(ctx)]
    summed, message = lax.optimization_barrier((summed, message))
    blocks_out = to_absolute(trade(summed, "ctx"), me)
    message = jnp.stack(trade([message] * ctx, "ctx"))
    tokens_grad = (grad_one + sum([c.astype(f32) for c in came], even[0])).astype(bf16)
    down_weight_grad, up_left, up_right, rest_left = [s.result() for s, _ in streams]
    up_weight_grad = jnp.concatenate([up_left, up_right], axis=1)
    output_weight_grad, vector_grads = rest_left[:own], rest_left[own]
    output_bias_grad, mixing_gain_grad, mixing_bias_grad, down_bias_grad, final_gain_grad, final_bias_grad = [
        vector_grads[n * own : (n + 1) * own] for n in range(6)
    ]
    up_bias_grad = vector_grads[6 * own : (6 + ratio) * own]

    mine = (me_dp * ctx + me) * own
    row_sums = jnp.sum(message[:, :, :width], axis=0)
    time_weight_grad = lax.dot_general(
        lax.dynamic_slice_in_dim(message[0, :, width + 2 * cols :], mine, own, 1),
        row_sums,
        (((0,), (0,)), ((), ())),
        precision=lax.Precision.HIGHEST,
        preferred_element_type=f32,
    )
    time_bias_grad = lax.dynamic_slice_in_dim(jnp.sum(row_sums, axis=0), mine, own)
    sums = jnp.sum(message[:, :, width : width + 2 * cols], axis=1)
    sums = lax.dynamic_index_in_dim(sums, mine // cols ^ me, 0, False)
    query_bias_grad = lax.dynamic_slice_in_dim(sums[:cols], mine % cols, own)
    value_bias_grad = lax.dynamic_slice_in_dim(sums[cols:], mine % cols, own)

    query_weight_grad, key_weight_grad, value_weight_grad = [
        jnp.concatenate(
            [
                block[:, (3 * p + n) * 128 : (3 * p + n + 1) * 128]
                for block in blocks_out
                for p in range(cols // 128)
            ],
            axis=1,
        )
        for n in range(3)
    ]
    return (
        layer_out[None],
        tokens_grad[None],
        time_weight_grad,
        time_bias_grad,
        query_weight_grad,
        query_bias_grad,
        key_weight_grad,
        value_weight_grad,
        value_bias_grad,
        output_weight_grad,
        output_bias_grad,
        mixing_gain_grad,
        mixing_bias_grad,
        up_weight_grad,
        up_bias_grad,
        down_weight_grad,
        down_bias_grad,
        final_gain_grad,
        final_bias_grad,
    )


def solution(mesh):
    rows, split_rows, split = P("dp", "ctx", None), P(BOTH, None), P(BOTH)
    return jax.shard_map(
        shards,
        mesh=mesh,
        in_specs=(
            rows, P("dp", None), rows, P("dp", None), split_rows, split, split_rows, split, split_rows, split_rows,
            split, split_rows, split, split, split, split_rows, split, split_rows, split, split, split,
        ),
        out_specs=(
            rows, rows, split_rows, split, split_rows, split, split_rows, split_rows, split, split_rows, split, split,
            split, split_rows, split, split_rows, split, split, split,
        ),
        check_vma=False,
    )
```

```python
import functools

import jax
import jax.numpy as jnp
from jax import lax
from jax.experimental import pallas as pl
from jax.experimental.pallas import tpu as pltpu
from jax.sharding import PartitionSpec as P

HEAD_DIM = 64
BLOCK = 256
MASKED = -1e30
EPSILON = 1e-05
SCALE = HEAD_DIM**-0.5
SCALE_LOG2 = SCALE * 1.4426950408889634
BOTH = ("dp", "ctx")
f32, bf16 = jnp.float32, jnp.bfloat16


def nn(left, right):
    return jnp.dot(left, right, preferred_element_type=f32)


def tn(left, right):
    return lax.dot_general(left, right, (((0,), (0,)), ((), ())), preferred_element_type=f32)


def nt(left, right):
    return lax.dot_general(left, right, (((1,), (1,)), ((), ())), preferred_element_type=f32)


def head_only(pair, which):
    lane = lax.broadcasted_iota(jnp.int32, pair.shape, 1)
    keep = (lane < HEAD_DIM) if which == 0 else (lane >= HEAD_DIM)
    return jnp.where(keep, pair, jnp.zeros_like(pair))


def place(block, me, per_chunk):
    return lax.bitwise_xor(block // per_chunk, me) * per_chunk + lax.rem(block, per_chunk)


def forward_kernel(per_chunk, pairs, info, qkv_ref, idc_ref, idr_ref, o_ref, lse_ref, o_acc, m_acc, l_acc):
    i = pl.program_id(0)
    me = info[2, 0]
    m_acc[...] = jnp.full_like(m_acc, MASKED)
    l_acc[...] = jnp.zeros_like(l_acc)
    o_acc[...] = jnp.zeros_like(o_acc)
    ids_q = idr_ref[pl.ds(i, 1)][0]
    here = pl.multiple_of(place(i, me, per_chunk) * BLOCK, BLOCK)

    queries = []
    for p in range(pairs):
        pair = qkv_ref[pl.ds(here, BLOCK), (3 * p) * 128 : (3 * p + 1) * 128]
        queries += [head_only(pair, 0), head_only(pair, 1)]

    def step(j, carry):
        at = pl.multiple_of(place(j, me, per_chunk) * BLOCK, BLOCK)
        same = idc_ref[pl.ds(pl.multiple_of(j * BLOCK, BLOCK), BLOCK), :] == ids_q
        heads = range(2 * pairs)
        peak = [m_acc[h] for h in heads]
        count = [l_acc[h] for h in heads]
        mixed = [o_acc[h * HEAD_DIM : (h + 1) * HEAD_DIM] for h in heads]
        values, scores = [], []
        for p in range(pairs):
            k_pair = qkv_ref[pl.ds(at, BLOCK), (3 * p + 1) * 128 : (3 * p + 2) * 128]
            values.append(qkv_ref[pl.ds(at, BLOCK), (3 * p + 2) * 128 : (3 * p + 3) * 128])
            scores += [nt(k_pair, queries[2 * p + w]) for w in range(2)]
        for h in heads:
            t = jnp.where(same, scores[h] * SCALE_LOG2, MASKED)
            new = jnp.maximum(peak[h], jnp.max(t, axis=0, keepdims=True))
            alpha = jnp.exp2(peak[h] - new)
            e = jnp.exp2(t - new)
            count[h] = count[h] * alpha + jnp.sum(e, axis=0, keepdims=True)
            peak[h] = new
            w = h % 2
            mixed[h] = mixed[h] * alpha + tn(values[h // 2], e.astype(bf16))[w * HEAD_DIM : (w + 1) * HEAD_DIM]
        for h in heads:
            m_acc[h], l_acc[h] = peak[h], count[h]
            o_acc[h * HEAD_DIM : (h + 1) * HEAD_DIM] = mixed[h]
        return carry

    lax.fori_loop(info[0, i], info[1, i], step, 0)
    for p in range(pairs):
        parts = []
        for w in range(2):
            h = 2 * p + w
            parts.append(o_acc[h * HEAD_DIM : (h + 1) * HEAD_DIM] / l_acc[h])
            lse_ref[0, h : h + 1, :] = m_acc[h] + jnp.log2(l_acc[h])
        o_ref[:, p * 128 : (p + 1) * 128] = jnp.concatenate(parts, axis=0).T.astype(bf16)


def attention_forward(info, qkv, ids_col, ids_row, per_chunk):
    rows, width = qkv.shape[0], qkv.shape[1] // 3
    blocks, heads = rows // BLOCK, width // HEAD_DIM
    return pl.pallas_call(
        functools.partial(forward_kernel, per_chunk, heads // 2),
        grid_spec=pltpu.PrefetchScalarGridSpec(
            num_scalar_prefetch=1,
            grid=(blocks,),
            in_specs=[
                pl.BlockSpec((rows, 3 * width), lambda i, info: (0, 0)),
                pl.BlockSpec((rows, 1), lambda i, info: (0, 0)),
                pl.BlockSpec((blocks, 1, BLOCK), lambda i, info: (0, 0, 0)),
            ],
            out_specs=[
                pl.BlockSpec((BLOCK, width), lambda i, info: (place(i, info[2, 0], per_chunk), 0)),
                pl.BlockSpec((1, heads, BLOCK), lambda i, info: (i, 0, 0)),
            ],
            scratch_shapes=[
                pltpu.VMEM((width, BLOCK), f32),
                pltpu.VMEM((heads, 1, BLOCK), f32),
                pltpu.VMEM((heads, 1, BLOCK), f32),
            ],
        ),
        out_shape=[
            jax.ShapeDtypeStruct((rows, width), bf16),
            jax.ShapeDtypeStruct((blocks, heads, BLOCK), f32),
        ],
        cost_estimate=pl.CostEstimate(flops=30 * 10**9, bytes_accessed=6 * rows * width, transcendentals=10**7),
        name="attention_forward",
    )(info, qkv, ids_col, ids_row)


def backward_kernel(
    per_chunk, first, info, q_ref, k_ref, v_ref, do_ref, o_ref, lse_ref, idc_ref, idr_ref,
    out_ref, delta_ref, dq_acc, dk_acc, dv_acc,
):
    j = pl.program_id(0)
    blocks = pl.num_programs(0)
    me = info[2, 0]

    @pl.when(j == 0)
    def _():
        dq_acc[...] = jnp.zeros_like(dq_acc)

        def fill(i, carry):
            at = pl.multiple_of(place(i, me, per_chunk) * BLOCK, BLOCK)
            prod = (do_ref[pl.ds(at, BLOCK), :].astype(f32) * o_ref[pl.ds(at, BLOCK), :].astype(f32)).T
            for w in range(2):
                delta_ref[i, w : w + 1, :] = jnp.sum(prod[w * HEAD_DIM : (w + 1) * HEAD_DIM], axis=0, keepdims=True)
            return carry

        lax.fori_loop(0, blocks, fill, 0)

    dk_acc[...] = jnp.zeros_like(dk_acc)
    dv_acc[...] = jnp.zeros_like(dv_acc)
    k_turned = k_ref[...].T
    feature = lax.broadcasted_iota(jnp.int32, k_turned.shape, 0)
    turned = [
        jnp.where(feature < HEAD_DIM, k_turned, jnp.zeros_like(k_turned)),
        jnp.where(feature >= HEAD_DIM, k_turned, jnp.zeros_like(k_turned)),
    ]
    ids_k = idc_ref[pl.ds(pl.multiple_of(j * BLOCK, BLOCK), BLOCK), :]

    def step(i, carry):
        at = pl.multiple_of(place(i, me, per_chunk) * BLOCK, BLOCK)
        same = ids_k == idr_ref[pl.ds(i, 1)][0]
        k_pair, v_pair = k_ref[...], v_ref[...]
        q_pair, do_pair = q_ref[pl.ds(at, BLOCK), :], do_ref[pl.ds(at, BLOCK), :]
        es, dss, qs, dos = [], [], [], []
        for w in range(2):
            q_one, do_one = head_only(q_pair, w), head_only(do_pair, w)
            t = nt(k_pair, q_one) * SCALE_LOG2 - lse_ref[i, first + w : first + w + 1, :]
            e = jnp.exp2(jnp.where(same, t, MASKED))
            ds = (e * (nt(v_pair, do_one) - delta_ref[i, w : w + 1, :])).astype(bf16)
            es.append(e.astype(bf16))
            dss.append(ds)
            qs.append(q_one)
            dos.append(do_one)
        dv_acc[...] += nn(jnp.concatenate(es, axis=1), jnp.concatenate(dos, axis=0))
        dk_acc[...] += nn(jnp.concatenate(dss, axis=1), jnp.concatenate(qs, axis=0))
        dq_acc[i] += nn(jnp.concatenate(turned, axis=1), jnp.concatenate(dss, axis=0))
        return carry

    lax.fori_loop(info[0, j], info[1, j], step, 0)
    mine = pl.multiple_of(place(j, me, per_chunk) * BLOCK, BLOCK)
    out_ref[pl.ds(mine, BLOCK), 128:256] = (dk_acc[...] * SCALE).astype(bf16)
    out_ref[pl.ds(mine, BLOCK), 256:384] = dv_acc[...].astype(bf16)

    @pl.when(j == blocks - 1)
    def _():
        def turn_back(i, carry):
            at = pl.multiple_of(place(i, me, per_chunk) * BLOCK, BLOCK)
            out_ref[pl.ds(at, BLOCK), 0:128] = (dq_acc[i] * SCALE).T.astype(bf16)
            return carry

        lax.fori_loop(0, blocks, turn_back, 0)


def attention_backward(pair, info, qkv, do, o, lse, ids_col, ids_row, per_chunk):
    rows, width = o.shape
    blocks, heads = rows // BLOCK, width // HEAD_DIM
    return pl.pallas_call(
        functools.partial(backward_kernel, per_chunk, 2 * pair),
        grid_spec=pltpu.PrefetchScalarGridSpec(
            num_scalar_prefetch=1,
            grid=(blocks,),
            in_specs=[
                pl.BlockSpec((rows, 128), lambda i, info: (0, 3 * pair)),
                pl.BlockSpec((BLOCK, 128), lambda i, info: (place(i, info[2, 0], per_chunk), 3 * pair + 1)),
                pl.BlockSpec((BLOCK, 128), lambda i, info: (place(i, info[2, 0], per_chunk), 3 * pair + 2)),
                pl.BlockSpec((rows, 128), lambda i, info: (0, pair)),
                pl.BlockSpec((rows, 128), lambda i, info: (0, pair)),
                pl.BlockSpec((blocks, heads, BLOCK), lambda i, info: (0, 0, 0)),
                pl.BlockSpec((rows, 1), lambda i, info: (0, 0)),
                pl.BlockSpec((blocks, 1, BLOCK), lambda i, info: (0, 0, 0)),
            ],
            out_specs=pl.BlockSpec((rows, 384), lambda i, info: (0, 0)),
            scratch_shapes=[
                pltpu.VMEM((blocks, 2, BLOCK), f32),
                pltpu.VMEM((blocks, 128, BLOCK), f32),
                pltpu.VMEM((BLOCK, 128), f32),
                pltpu.VMEM((BLOCK, 128), f32),
            ],
        ),
        out_shape=jax.ShapeDtypeStruct((rows, 384), bf16),
        cost_estimate=pl.CostEstimate(flops=25 * 10**9, bytes_accessed=8 * rows * 128, transcendentals=10**7),
        name="attention_backward",
    )(info, qkv, qkv, qkv, do, o, lse, ids_col, ids_row)


def spans(ids, me):
    blocks = ids.shape[0] // BLOCK
    per_block = ids.reshape(blocks, BLOCK)
    low = jnp.sum(ids[None, :] < per_block[:, :1], axis=1) // BLOCK
    high = (jnp.sum(ids[None, :] <= per_block[:, -1:], axis=1) + BLOCK - 1) // BLOCK
    return jnp.stack([low, high, jnp.full((blocks,), me.astype(low.dtype))]).astype(jnp.int32)


def own_index(axis):
    return lax.axis_index(axis).astype(jnp.uint32)


def swap(value, axis, mask):
    size = lax.axis_size(axis)
    return lax.ppermute(value, axis, [(i, i ^ mask) for i in range(size)])


def bits(size):
    return [1 << b for b in range(size.bit_length() - 1)]


def flipped(index, size):
    flags = bits(size)
    return sum(((index >> n) & 1) << (len(flags) - 1 - n) for n in range(len(flags)))


def trade(pieces, axis):
    return [pieces[0]] + [swap(pieces[k], axis, k) for k in range(1, len(pieces))]


def to_absolute(pieces, me):
    stacked = jnp.stack(pieces)
    return [lax.dynamic_index_in_dim(stacked, (me ^ c), 0, False) for c in range(len(pieces))]


class Halving:
    def __init__(self, names, shape):
        self.me = {n: (own_index(n[0]) >> (n[1].bit_length() - 1)) & 1 for n in names}
        self.names, self.terms, self.fixed, self.shape = list(names), [], {}, shape

    def cut(self, term, chosen):
        array, names, part = term
        starts, sizes = [], []
        for n in names:
            starts.append(chosen.get(n, jnp.uint32(0)))
            sizes.append(1 if n in chosen else 2)
        for low, high in part:
            starts.append(jnp.uint32(low))
            sizes.append(high - low)
        left = [2 for n in names if n not in chosen]
        return lax.dynamic_slice(array, starts, sizes).reshape(left + [h - l for l, h in part])

    def total(self, chosen):
        pieces = [self.cut(t, chosen).astype(f32) for t in self.terms]
        return sum(pieces[1:], pieces[0])

    def outgoing(self, name):
        return self.total({**self.fixed, name: 1 - self.me[name]}).astype(bf16)

    def arrived(self, name, value):
        self.fixed[name] = self.me[name]
        names = [n for n in self.names if n not in self.fixed]
        self.terms.append((value, names, [(0, d) for d in self.shape]))

    def exchange(self, name):
        self.arrived(name, swap(self.outgoing(name), *name))

    def result(self):
        return self.total(self.fixed)


def normalize(values, gain, shift):
    average = jnp.mean(values, axis=-1, keepdims=True)
    centered = values - average
    inverse = lax.rsqrt(jnp.mean(centered * centered, axis=-1, keepdims=True) + EPSILON)
    normed = centered * inverse
    return normed * gain + shift, normed, inverse


def normalize_back(upstream, normed, inverse, gain):
    scaled = upstream * gain
    plain = jnp.mean(scaled, axis=-1, keepdims=True)
    cross = jnp.mean(scaled * normed, axis=-1, keepdims=True)
    result = inverse * (scaled - plain - normed * cross)
    return result, jnp.sum(upstream * normed, axis=0), jnp.sum(upstream, axis=0)


def shards(
    tokens, time_feat, cotangent, segment_ids, time_weight, time_bias, query_weight, query_bias, key_weight,
    value_weight, value_bias, output_weight, output_bias, mixing_gain, mixing_bias, up_weight, up_bias,
    down_weight, down_bias, final_gain, final_bias,
):
    me_dp, me = own_index("dp"), own_index("ctx")
    dp, ctx = lax.axis_size("dp"), lax.axis_size("ctx")
    devices = dp * ctx
    piece, width = tokens.shape[1], tokens.shape[2]
    hidden = up_weight.shape[1]
    own, ratio = width // devices, hidden // width
    cols = width // ctx
    per_chunk = piece // BLOCK
    tokens, cotangent, ids = tokens[0], cotangent[0], segment_ids[0]

    second = lax.all_gather(
        jnp.concatenate([up_weight, output_weight] + [down_weight[n * own : (n + 1) * own] for n in range(ratio)], axis=1),
        BOTH,
        axis=0,
        tiled=True,
    )
    up_full, output_full = second[:, :hidden], second[:, hidden : hidden + width]
    down_full = jnp.stack(
        [second[:, hidden + n * width : hidden + (n + 1) * width].reshape(devices, own, width) for n in range(1, 1 + ratio)],
        axis=1,
    ).reshape(hidden, width)

    held = {0: tokens, ctx // 2: swap(tokens, "ctx", ctx // 2)}
    vectors = [
        time_bias, query_bias, value_bias, output_bias, mixing_gain, mixing_bias, down_bias, final_gain, final_bias
    ]
    small = jnp.concatenate([jnp.stack(vectors), up_bias.reshape(ratio, own)]).T
    small = jnp.pad(small, ((0, 0), (0, 128 - small.shape[1])))
    pieces = []
    for k in range(ctx):
        at = (me ^ k) * cols
        parts = [
            lax.dynamic_slice_in_dim(w, at + p * 128, 128, 1)
            for p in range(cols // 128)
            for w in (query_weight, key_weight, value_weight)
        ] + [lax.dynamic_slice_in_dim(time_weight, at, cols, 1)]
        pieces.append(jnp.concatenate(parts + [small], axis=1))
    first = jnp.concatenate(to_absolute(trade(pieces, "ctx"), me))
    first = first[None]
    for n, bit in enumerate(reversed(bits(dp))):
        if n == 1:
            first, held[ctx // 2] = lax.optimization_barrier((first, held[ctx // 2]))
        first = jnp.concatenate([first, swap(first, "dp", bit)])
    for bit in reversed(bits(ctx)[:-1]):
        held.update({k | bit: swap(v, "ctx", bit) for k, v in list(held.items())})
    token_chunks = [held[k] for k in range(ctx)]
    first = jnp.concatenate(
        [
            lax.dynamic_index_in_dim(first, flipped((me_dp ^ c), dp), 0, False)
            for c in range(dp)
        ]
    )
    qkv_weight = first[:, : 3 * cols]
    table = first[:, 4 * cols :].astype(f32).T
    time_shift_bias, query_shift, value_shift, output_shift, gain_one, bias_one, down_shift, gain_two, bias_two = [
        table[n] for n in range(len(vectors))
    ]
    up_shift = table[len(vectors) : len(vectors) + ratio].reshape(ratio, devices, own).transpose(1, 0, 2).reshape(hidden)
    shift_cols = trade([nn(time_feat, first[:, 3 * cols : 4 * cols])] * ctx, "ctx")
    time_shift = jnp.concatenate(to_absolute(shift_cols, me), axis=1) + time_shift_bias
    qkv_shift = []
    for p in range(cols // 128):
        at = me * cols + p * 128
        qkv_shift.append(lax.dynamic_slice_in_dim(query_shift, at, 128))
        qkv_shift.append(jnp.zeros((128,), f32))
        qkv_shift.append(lax.dynamic_slice_in_dim(value_shift, at, 128))
    qkv_shift = jnp.concatenate(qkv_shift)
    start_row = (jnp.concatenate(token_chunks).astype(f32) + time_shift).astype(bf16)
    residual_in = tokens.astype(f32) + time_shift
    qkv = (nn(start_row, qkv_weight) + qkv_shift).astype(bf16)

    info = spans(ids, me)
    ids_col, ids_row = ids.reshape(-1, 1), ids.reshape(-1, 1, BLOCK)
    mixed, logsum = attention_forward(info, qkv, ids_col, ids_row, per_chunk)
    returned = trade([mixed[k * piece : (k + 1) * piece] for k in range(ctx)], "ctx")
    returned, down_full = lax.optimization_barrier((returned, down_full))
    attended = jnp.concatenate(to_absolute(returned, me), axis=1)

    branch = nn(attended, output_full) + output_shift
    hidden_one, normed_one, inverse_one = normalize(residual_in + branch, gain_one, bias_one)
    hidden_low = hidden_one.astype(bf16)
    pre_gelu = nn(hidden_low, up_full) + up_shift
    share = 0.5 * (1.0 + lax.erf(pre_gelu * 0.5**0.5))
    activated = (pre_gelu * share).astype(bf16)
    slope = (share + pre_gelu * jnp.exp(-0.5 * pre_gelu * pre_gelu) * 0.3989422804014327).astype(bf16)
    activated, slope = lax.optimization_barrier((activated, slope))
    feed_out = nn(activated, down_full) + down_shift
    result, normed_two, inverse_two = normalize(hidden_one + feed_out, gain_two, bias_two)
    layer_out = result.astype(bf16)

    upstream = cotangent.astype(f32)
    grad_two, gain_two_grad, bias_two_grad = normalize_back(upstream, normed_two, inverse_two, gain_two)
    grad_feed = grad_two.astype(bf16)
    down_grad = tn(activated, grad_feed).astype(bf16)
    down_shift_grad = jnp.sum(grad_feed.astype(f32), axis=0)
    grad_inner = (nt(grad_feed, down_full) * slope.astype(f32)).astype(bf16)
    dp_names, ctx_names = [("dp", b) for b in bits(dp)], [("ctx", b) for b in bits(ctx)]
    names = dp_names[::-1] + ctx_names[::-1]
    core, turn, rest = ctx_names[0], dp_names[:2] + ctx_names[1:], dp_names[2:]
    whole = {}

    def share(label, array, height):
        size = (height, array.shape[-1])
        whole[label] = Halving(names, size)
        whole[label].terms = [(array.reshape([2] * len(names) + list(size)), names, [(0, d) for d in size])]
        whole[label].exchange(core)

    def stream(label, part, turned):
        sums = Halving(names, [high - low for low, high in part])
        sums.fixed = {core: sums.me[core]}
        sums.terms = [(array, left, part) for array, left, _ in whole[label].terms]
        return sums, turn[turned:] + turn[:turned] + rest

    def depart(moving, beside):
        going = [s.outgoing(name) for s, name in moving]
        going, beside = lax.optimization_barrier((going, beside))
        return [(s, name, swap(value, *name)) for (s, name), value in zip(moving, going)], beside

    def land(flights, beside):
        values, beside = lax.optimization_barrier(([value for _, _, value in flights], beside))
        for (s, name, _), value in zip(flights, values):
            s.arrived(name, value)
        return beside

    def following(pairs):
        return [(s, o.pop(0)) for s, o in pairs if o]

    share("down", down_grad, ratio * own)
    streams = [stream("down", [(0, ratio * own), (0, width)], 0)]
    ahead, grad_inner = depart(following(streams), grad_inner)
    up_grad = tn(hidden_low, grad_inner).astype(bf16)
    up_shift_grad = jnp.sum(grad_inner.astype(f32), axis=0)
    grad_hidden = grad_two + nt(grad_inner, up_full)
    grad_one, gain_one_grad, bias_one_grad = normalize_back(grad_hidden, normed_one, inverse_one, gain_one)
    grad_branch = grad_one.astype(bf16)
    output_grad = tn(attended, grad_branch).astype(bf16)
    output_shift_grad = jnp.sum(grad_branch.astype(f32), axis=0)
    vector_grads = jnp.stack(
        [output_shift_grad, gain_one_grad, bias_one_grad, down_shift_grad, gain_two_grad, bias_two_grad]
    )
    vector_grads = lax.optimization_barrier(vector_grads).reshape(6, devices, own).transpose(1, 0, 2).reshape(devices, 6 * own)
    vector_grads = jnp.concatenate([vector_grads, up_shift_grad.reshape(devices, ratio * own)], axis=1)
    vector_grads = jnp.pad(vector_grads, ((0, 0), (0, width - vector_grads.shape[1]))).astype(bf16)
    extra = 8
    rest_grad = jnp.concatenate(
        [output_grad.reshape(devices, own, width), jnp.broadcast_to(vector_grads[:, None], (devices, extra, width))],
        axis=1,
    )

    share("up", up_grad, own)
    share("rest", rest_grad, own + extra)
    streams += [
        stream("up", [(0, own), (0, hidden // 2)], 2),
        stream("up", [(0, own), (hidden // 2, hidden)], 0),
        stream("rest", [(0, own + extra), (0, width)], 0),
    ]

    grad_attended = nt(grad_branch, output_full).astype(bf16)
    pieces = [lax.dynamic_slice_in_dim(grad_attended, (me ^ k) * cols, cols, 1) for k in range(ctx)]
    grad_mixed = jnp.concatenate(trade(pieces, "ctx"))
    grad_mixed = land(ahead, grad_mixed)

    def weight_stream(grad):
        size = (ctx * own, grad.shape[1])
        sums = Halving(dp_names[::-1], size)
        array = tn(start_row, grad).reshape([2] * len(dp_names) + list(size))
        sums.terms = [(array, dp_names[::-1], [(0, d) for d in size])]
        return sums, list(dp_names)

    grads, pair_streams = [], []
    for pair in range(cols // 128):
        flights, grad_mixed = depart(following(streams + pair_streams), grad_mixed)
        grad = attention_backward(pair, info, qkv, grad_mixed, mixed, logsum, ids_col, ids_row, per_chunk)
        grad_mixed, grad = land(flights, (grad_mixed, grad))
        grads.append(grad)
        pair_streams.append(weight_stream(grad))

    qkv_sum = jnp.concatenate([jnp.sum(g.astype(f32), axis=0) for g in grads])
    row_sum = jnp.sum(grad_one, axis=0, keepdims=True) + lax.dot_general(
        qkv_sum[None],
        qkv_weight.astype(f32),
        (((1,), (1,)), ((), ())),
        precision=lax.Precision.HIGHEST,
        preferred_element_type=f32,
    )
    message = jnp.concatenate(
        [row_sum]
        + [qkv_sum[None, (3 * p + n) * 128 : (3 * p + n + 1) * 128] for n in (0, 2) for p in range(cols // 128)]
        + [time_feat.astype(f32)],
        axis=1,
    )
    message_names = dp_names[::-1]

    rows = jnp.concatenate(grads, axis=1).reshape(ctx // 2, 2, piece, 3 * cols)
    odd = nt(rows[:, 1].reshape(-1, 3 * cols), qkv_weight).astype(bf16)
    flights, (rows, odd, message) = depart(following(streams + pair_streams), (rows, odd, message))
    odd = swap(odd, *core)
    reply = swap(message, *message_names.pop(0))
    even = nt(rows[:, 0].reshape(-1, 3 * cols), qkv_weight)
    even, odd, message, reply = land(flights, (even, odd, message, reply))
    message = jnp.concatenate([message, reply])
    even = (even + odd.astype(f32)).reshape(ctx // 2, piece, width)
    away = [even[n].astype(bf16) for n in range(1, ctx // 2)]
    kept, came = [], None
    while any(o for _, o in streams + pair_streams) or message_names:
        fast, slow = following(pair_streams), following(streams)
        flights, (away, message) = depart(fast + slow, (away, message))
        if came is None:
            came = [swap(value, "ctx", 2 * n + 2) for n, value in enumerate(away)]
        if message_names:
            message = jnp.concatenate([message, swap(message, *message_names.pop(0))])
        kept += flights[len(fast) :]
        flights = flights[: len(fast)]
        if any(o for _, o in streams):
            flights, kept = flights + kept, []
        if not any(o for _, o in pair_streams):
            flights, kept = flights + kept, []
        message, came = land(flights, (message, came)) if not kept else (land(flights, message), came)
    summed = jnp.concatenate([s.result() for s, _ in pair_streams], axis=1).reshape(ctx, own, 3 * cols)
    summed = [lax.dynamic_index_in_dim(summed, (me ^ k), 0, False) for k in range(ctx)]
    summed, message = lax.optimization_barrier((summed, message))
    blocks_out = to_absolute(trade(summed, "ctx"), me)
    message = jnp.stack(trade([message] * ctx, "ctx"))
    tokens_grad = (grad_one + sum([c.astype(f32) for c in came], even[0])).astype(bf16)
    down_weight_grad, up_left, up_right, rest_left = [s.result() for s, _ in streams]
    up_weight_grad = jnp.concatenate([up_left, up_right], axis=1)
    output_weight_grad, vector_grads = rest_left[:own], rest_left[own]
    output_bias_grad, mixing_gain_grad, mixing_bias_grad, down_bias_grad, final_gain_grad, final_bias_grad = [
        vector_grads[n * own : (n + 1) * own] for n in range(6)
    ]
    up_bias_grad = vector_grads[6 * own : (6 + ratio) * own]

    mine = (me_dp * ctx + me) * own
    row_sums = jnp.sum(message[:, :, :width], axis=0)
    time_weight_grad = lax.dot_general(
        lax.dynamic_slice_in_dim(message[0, :, width + 2 * cols :], mine, own, 1),
        row_sums,
        (((0,), (0,)), ((), ())),
        precision=lax.Precision.HIGHEST,
        preferred_element_type=f32,
    )
    time_bias_grad = lax.dynamic_slice_in_dim(jnp.sum(row_sums, axis=0), mine, own)
    sums = jnp.sum(message[:, :, width : width + 2 * cols], axis=1)
    sums = lax.dynamic_index_in_dim(sums, mine // cols ^ me, 0, False)
    query_bias_grad = lax.dynamic_slice_in_dim(sums[:cols], mine % cols, own)
    value_bias_grad = lax.dynamic_slice_in_dim(sums[cols:], mine % cols, own)

    query_weight_grad, key_weight_grad, value_weight_grad = [
        jnp.concatenate(
            [
                block[:, (3 * p + n) * 128 : (3 * p + n + 1) * 128]
                for block in blocks_out
                for p in range(cols // 128)
            ],
            axis=1,
        )
        for n in range(3)
    ]
    return (
        layer_out[None],
        tokens_grad[None],
        time_weight_grad,
        time_bias_grad,
        query_weight_grad,
        query_bias_grad,
        key_weight_grad,
        value_weight_grad,
        value_bias_grad,
        output_weight_grad,
        output_bias_grad,
        mixing_gain_grad,
        mixing_bias_grad,
        up_weight_grad,
        up_bias_grad,
        down_weight_grad,
        down_bias_grad,
        final_gain_grad,
        final_bias_grad,
    )


def solution(mesh):
    rows, split_rows, split = P("dp", "ctx", None), P(BOTH, None), P(BOTH)
    return jax.shard_map(
        shards,
        mesh=mesh,
        in_specs=(
            rows, P("dp", None), rows, P("dp", None), split_rows, split, split_rows, split, split_rows, split_rows,
            split, split_rows, split, split, split, split_rows, split, split_rows, split, split, split,
        ),
        out_specs=(
            rows, rows, split_rows, split, split_rows, split, split_rows, split_rows, split, split_rows, split, split,
            split, split_rows, split, split_rows, split, split, split,
        ),
        check_vma=False,
    )
```

```python
import functools

import jax
import jax.numpy as jnp
from jax import lax
from jax.experimental import pallas as pl
from jax.experimental.pallas import tpu as pltpu
from jax.sharding import PartitionSpec as P

HEAD_DIM = 64
BLOCK = 256
MASKED = -1e30
EPSILON = 1e-05
SCALE = HEAD_DIM**-0.5
SCALE_LOG2 = SCALE * 1.4426950408889634
BOTH = ("dp", "ctx")
f32, bf16 = jnp.float32, jnp.bfloat16


def nn(left, right):
    return jnp.dot(left, right, preferred_element_type=f32)


def tn(left, right):
    return lax.dot_general(left, right, (((0,), (0,)), ((), ())), preferred_element_type=f32)


def nt(left, right):
    return lax.dot_general(left, right, (((1,), (1,)), ((), ())), preferred_element_type=f32)


def head_only(pair, which):
    lane = lax.broadcasted_iota(jnp.int32, pair.shape, 1)
    keep = (lane < HEAD_DIM) if which == 0 else (lane >= HEAD_DIM)
    return jnp.where(keep, pair, jnp.zeros_like(pair))


def place(block, me, per_chunk):
    return lax.bitwise_xor(block // per_chunk, me) * per_chunk + lax.rem(block, per_chunk)


def forward_kernel(per_chunk, pairs, info, qkv_ref, idc_ref, idr_ref, o_ref, lse_ref, o_acc, m_acc, l_acc):
    i = pl.program_id(0)
    me = info[2, 0]
    m_acc[...] = jnp.full_like(m_acc, MASKED)
    l_acc[...] = jnp.zeros_like(l_acc)
    o_acc[...] = jnp.zeros_like(o_acc)
    ids_q = idr_ref[pl.ds(i, 1)][0]
    here = pl.multiple_of(place(i, me, per_chunk) * BLOCK, BLOCK)

    queries = []
    for p in range(pairs):
        pair = qkv_ref[pl.ds(here, BLOCK), (3 * p) * 128 : (3 * p + 1) * 128]
        queries += [head_only(pair, 0), head_only(pair, 1)]

    def step(j, carry):
        at = pl.multiple_of(place(j, me, per_chunk) * BLOCK, BLOCK)
        same = idc_ref[pl.ds(pl.multiple_of(j * BLOCK, BLOCK), BLOCK), :] == ids_q
        heads = range(2 * pairs)
        peak = [m_acc[h] for h in heads]
        count = [l_acc[h] for h in heads]
        mixed = [o_acc[h * HEAD_DIM : (h + 1) * HEAD_DIM] for h in heads]
        values, scores = [], []
        for p in range(pairs):
            k_pair = qkv_ref[pl.ds(at, BLOCK), (3 * p + 1) * 128 : (3 * p + 2) * 128]
            values.append(qkv_ref[pl.ds(at, BLOCK), (3 * p + 2) * 128 : (3 * p + 3) * 128])
            scores += [nt(k_pair, queries[2 * p + w]) for w in range(2)]
        for h in heads:
            t = jnp.where(same, scores[h] * SCALE_LOG2, MASKED)
            new = jnp.maximum(peak[h], jnp.max(t, axis=0, keepdims=True))
            alpha = jnp.exp2(peak[h] - new)
            e = jnp.exp2(t - new)
            count[h] = count[h] * alpha + jnp.sum(e, axis=0, keepdims=True)
            peak[h] = new
            w = h % 2
            mixed[h] = mixed[h] * alpha + tn(values[h // 2], e.astype(bf16))[w * HEAD_DIM : (w + 1) * HEAD_DIM]
        for h in heads:
            m_acc[h], l_acc[h] = peak[h], count[h]
            o_acc[h * HEAD_DIM : (h + 1) * HEAD_DIM] = mixed[h]
        return carry

    lax.fori_loop(info[0, i], info[1, i], step, 0)
    for p in range(pairs):
        parts = []
        for w in range(2):
            h = 2 * p + w
            parts.append(o_acc[h * HEAD_DIM : (h + 1) * HEAD_DIM] / l_acc[h])
            lse_ref[0, h : h + 1, :] = m_acc[h] + jnp.log2(l_acc[h])
        o_ref[:, p * 128 : (p + 1) * 128] = jnp.concatenate(parts, axis=0).T.astype(bf16)


def attention_forward(info, qkv, ids_col, ids_row, per_chunk):
    rows, width = qkv.shape[0], qkv.shape[1] // 3
    blocks, heads = rows // BLOCK, width // HEAD_DIM
    return pl.pallas_call(
        functools.partial(forward_kernel, per_chunk, heads // 2),
        grid_spec=pltpu.PrefetchScalarGridSpec(
            num_scalar_prefetch=1,
            grid=(blocks,),
            in_specs=[
                pl.BlockSpec((rows, 3 * width), lambda i, info: (0, 0)),
                pl.BlockSpec((rows, 1), lambda i, info: (0, 0)),
                pl.BlockSpec((blocks, 1, BLOCK), lambda i, info: (0, 0, 0)),
            ],
            out_specs=[
                pl.BlockSpec((BLOCK, width), lambda i, info: (place(i, info[2, 0], per_chunk), 0)),
                pl.BlockSpec((1, heads, BLOCK), lambda i, info: (i, 0, 0)),
            ],
            scratch_shapes=[
                pltpu.VMEM((width, BLOCK), f32),
                pltpu.VMEM((heads, 1, BLOCK), f32),
                pltpu.VMEM((heads, 1, BLOCK), f32),
            ],
        ),
        out_shape=[
            jax.ShapeDtypeStruct((rows, width), bf16),
            jax.ShapeDtypeStruct((blocks, heads, BLOCK), f32),
        ],
        cost_estimate=pl.CostEstimate(flops=30 * 10**9, bytes_accessed=6 * rows * width, transcendentals=10**7),
        name="attention_forward",
    )(info, qkv, ids_col, ids_row)


def backward_kernel(
    per_chunk, first, info, q_ref, k_ref, v_ref, do_ref, o_ref, lse_ref, idc_ref, idr_ref,
    out_ref, delta_ref, dq_acc, dk_acc, dv_acc,
):
    j = pl.program_id(0)
    blocks = pl.num_programs(0)
    me = info[2, 0]

    @pl.when(j == 0)
    def _():
        dq_acc[...] = jnp.zeros_like(dq_acc)

        def fill(i, carry):
            at = pl.multiple_of(place(i, me, per_chunk) * BLOCK, BLOCK)
            prod = (do_ref[pl.ds(at, BLOCK), :].astype(f32) * o_ref[pl.ds(at, BLOCK), :].astype(f32)).T
            for w in range(2):
                delta_ref[i, w : w + 1, :] = jnp.sum(prod[w * HEAD_DIM : (w + 1) * HEAD_DIM], axis=0, keepdims=True)
            return carry

        lax.fori_loop(0, blocks, fill, 0)

    dk_acc[...] = jnp.zeros_like(dk_acc)
    dv_acc[...] = jnp.zeros_like(dv_acc)
    k_turned = k_ref[...].T
    feature = lax.broadcasted_iota(jnp.int32, k_turned.shape, 0)
    turned = [
        jnp.where(feature < HEAD_DIM, k_turned, jnp.zeros_like(k_turned)),
        jnp.where(feature >= HEAD_DIM, k_turned, jnp.zeros_like(k_turned)),
    ]
    ids_k = idc_ref[pl.ds(pl.multiple_of(j * BLOCK, BLOCK), BLOCK), :]

    def step(i, carry):
        at = pl.multiple_of(place(i, me, per_chunk) * BLOCK, BLOCK)
        same = ids_k == idr_ref[pl.ds(i, 1)][0]
        k_pair, v_pair = k_ref[...], v_ref[...]
        q_pair, do_pair = q_ref[pl.ds(at, BLOCK), :], do_ref[pl.ds(at, BLOCK), :]
        es, dss, qs, dos = [], [], [], []
        for w in range(2):
            q_one, do_one = head_only(q_pair, w), head_only(do_pair, w)
            t = nt(k_pair, q_one) * SCALE_LOG2 - lse_ref[i, first + w : first + w + 1, :]
            e = jnp.exp2(jnp.where(same, t, MASKED))
            ds = (e * (nt(v_pair, do_one) - delta_ref[i, w : w + 1, :])).astype(bf16)
            es.append(e.astype(bf16))
            dss.append(ds)
            qs.append(q_one)
            dos.append(do_one)
        dv_acc[...] += nn(jnp.concatenate(es, axis=1), jnp.concatenate(dos, axis=0))
        dk_acc[...] += nn(jnp.concatenate(dss, axis=1), jnp.concatenate(qs, axis=0))
        dq_acc[i] += nn(jnp.concatenate(turned, axis=1), jnp.concatenate(dss, axis=0))
        return carry

    lax.fori_loop(info[0, j], info[1, j], step, 0)
    mine = pl.multiple_of(place(j, me, per_chunk) * BLOCK, BLOCK)
    out_ref[pl.ds(mine, BLOCK), 128:256] = (dk_acc[...] * SCALE).astype(bf16)
    out_ref[pl.ds(mine, BLOCK), 256:384] = dv_acc[...].astype(bf16)

    @pl.when(j == blocks - 1)
    def _():
        def turn_back(i, carry):
            at = pl.multiple_of(place(i, me, per_chunk) * BLOCK, BLOCK)
            out_ref[pl.ds(at, BLOCK), 0:128] = (dq_acc[i] * SCALE).T.astype(bf16)
            return carry

        lax.fori_loop(0, blocks, turn_back, 0)


def attention_backward(pair, info, qkv, do, o, lse, ids_col, ids_row, per_chunk):
    rows, width = o.shape
    blocks, heads = rows // BLOCK, width // HEAD_DIM
    return pl.pallas_call(
        functools.partial(backward_kernel, per_chunk, 2 * pair),
        grid_spec=pltpu.PrefetchScalarGridSpec(
            num_scalar_prefetch=1,
            grid=(blocks,),
            in_specs=[
                pl.BlockSpec((rows, 128), lambda i, info: (0, 3 * pair)),
                pl.BlockSpec((BLOCK, 128), lambda i, info: (place(i, info[2, 0], per_chunk), 3 * pair + 1)),
                pl.BlockSpec((BLOCK, 128), lambda i, info: (place(i, info[2, 0], per_chunk), 3 * pair + 2)),
                pl.BlockSpec((rows, 128), lambda i, info: (0, pair)),
                pl.BlockSpec((rows, 128), lambda i, info: (0, pair)),
                pl.BlockSpec((blocks, heads, BLOCK), lambda i, info: (0, 0, 0)),
                pl.BlockSpec((rows, 1), lambda i, info: (0, 0)),
                pl.BlockSpec((blocks, 1, BLOCK), lambda i, info: (0, 0, 0)),
            ],
            out_specs=pl.BlockSpec((rows, 384), lambda i, info: (0, 0)),
            scratch_shapes=[
                pltpu.VMEM((blocks, 2, BLOCK), f32),
                pltpu.VMEM((blocks, 128, BLOCK), f32),
                pltpu.VMEM((BLOCK, 128), f32),
                pltpu.VMEM((BLOCK, 128), f32),
            ],
        ),
        out_shape=jax.ShapeDtypeStruct((rows, 384), bf16),
        cost_estimate=pl.CostEstimate(flops=25 * 10**9, bytes_accessed=8 * rows * 128, transcendentals=10**7),
        name="attention_backward",
    )(info, qkv, qkv, qkv, do, o, lse, ids_col, ids_row)


def spans(ids, me):
    blocks = ids.shape[0] // BLOCK
    per_block = ids.reshape(blocks, BLOCK)
    low = jnp.sum(ids[None, :] < per_block[:, :1], axis=1) // BLOCK
    high = (jnp.sum(ids[None, :] <= per_block[:, -1:], axis=1) + BLOCK - 1) // BLOCK
    return jnp.stack([low, high, jnp.full((blocks,), me.astype(low.dtype))]).astype(jnp.int32)


def own_index(axis):
    return lax.axis_index(axis).astype(jnp.uint32)


def swap(value, axis, mask):
    size = lax.axis_size(axis)
    return lax.ppermute(value, axis, [(i, i ^ mask) for i in range(size)])


def bits(size):
    return [1 << b for b in range(size.bit_length() - 1)]


def flipped(index, size):
    flags = bits(size)
    return sum(((index >> n) & 1) << (len(flags) - 1 - n) for n in range(len(flags)))


def trade(pieces, axis):
    return [pieces[0]] + [swap(pieces[k], axis, k) for k in range(1, len(pieces))]


def to_absolute(pieces, me):
    stacked = jnp.stack(pieces)
    return [lax.dynamic_index_in_dim(stacked, (me ^ c), 0, False) for c in range(len(pieces))]


class Halving:
    def __init__(self, names, shape):
        self.me = {n: (own_index(n[0]) >> (n[1].bit_length() - 1)) & 1 for n in names}
        self.names, self.terms, self.fixed, self.shape = list(names), [], {}, shape

    def cut(self, term, chosen):
        array, names, part = term
        starts, sizes = [], []
        for n in names:
            starts.append(chosen.get(n, jnp.uint32(0)))
            sizes.append(1 if n in chosen else 2)
        for low, high in part:
            starts.append(jnp.uint32(low))
            sizes.append(high - low)
        left = [2 for n in names if n not in chosen]
        return lax.dynamic_slice(array, starts, sizes).reshape(left + [h - l for l, h in part])

    def total(self, chosen):
        pieces = [self.cut(t, chosen).astype(f32) for t in self.terms]
        return sum(pieces[1:], pieces[0])

    def outgoing(self, name):
        return self.total({**self.fixed, name: 1 - self.me[name]}).astype(bf16)

    def arrived(self, name, value):
        self.fixed[name] = self.me[name]
        names = [n for n in self.names if n not in self.fixed]
        self.terms.append((value, names, [(0, d) for d in self.shape]))

    def exchange(self, name):
        self.arrived(name, swap(self.outgoing(name), *name))

    def result(self):
        return self.total(self.fixed)


def normalize(values, gain, shift):
    average = jnp.mean(values, axis=-1, keepdims=True)
    centered = values - average
    inverse = lax.rsqrt(jnp.mean(centered * centered, axis=-1, keepdims=True) + EPSILON)
    normed = centered * inverse
    return normed * gain + shift, normed, inverse


def normalize_back(upstream, normed, inverse, gain):
    scaled = upstream * gain
    plain = jnp.mean(scaled, axis=-1, keepdims=True)
    cross = jnp.mean(scaled * normed, axis=-1, keepdims=True)
    result = inverse * (scaled - plain - normed * cross)
    return result, jnp.sum(upstream * normed, axis=0), jnp.sum(upstream, axis=0)


def shards(
    tokens, time_feat, cotangent, segment_ids, time_weight, time_bias, query_weight, query_bias, key_weight,
    value_weight, value_bias, output_weight, output_bias, mixing_gain, mixing_bias, up_weight, up_bias,
    down_weight, down_bias, final_gain, final_bias,
):
    me_dp, me = own_index("dp"), own_index("ctx")
    dp, ctx = lax.axis_size("dp"), lax.axis_size("ctx")
    devices = dp * ctx
    piece, width = tokens.shape[1], tokens.shape[2]
    hidden = up_weight.shape[1]
    own, ratio = width // devices, hidden // width
    cols = width // ctx
    per_chunk = piece // BLOCK
    tokens, cotangent, ids = tokens[0], cotangent[0], segment_ids[0]

    held = {0: tokens, ctx // 2: swap(tokens, "ctx", ctx // 2)}
    vectors = [
        time_bias, query_bias, value_bias, output_bias, mixing_gain, mixing_bias, down_bias, final_gain, final_bias
    ]
    small = jnp.concatenate([jnp.stack(vectors), up_bias.reshape(ratio, own)]).T
    small = jnp.pad(small, ((0, 0), (0, 128 - small.shape[1])))
    pieces = []
    for k in range(ctx):
        at = (me ^ k) * cols
        parts = [
            lax.dynamic_slice_in_dim(w, at + p * 128, 128, 1)
            for p in range(cols // 128)
            for w in (query_weight, key_weight, value_weight)
        ] + [lax.dynamic_slice_in_dim(time_weight, at, cols, 1)]
        pieces.append(jnp.concatenate(parts + [small], axis=1))
    first = jnp.concatenate(to_absolute(trade(pieces, "ctx"), me))
    second = jnp.concatenate(
        [up_weight, output_weight] + [down_weight[n * own : (n + 1) * own] for n in range(ratio)], axis=1
    )
    second, first = lax.optimization_barrier((second, first))
    second = lax.all_gather(second, BOTH, axis=0, tiled=True)
    up_full, output_full = second[:, :hidden], second[:, hidden : hidden + width]
    down_full = jnp.stack(
        [second[:, hidden + n * width : hidden + (n + 1) * width].reshape(devices, own, width) for n in range(1, 1 + ratio)],
        axis=1,
    ).reshape(hidden, width)

    first = first[None]
    for n, bit in enumerate(reversed(bits(dp))):
        if n == 1:
            first, held[ctx // 2] = lax.optimization_barrier((first, held[ctx // 2]))
        first = jnp.concatenate([first, swap(first, "dp", bit)])
    for bit in reversed(bits(ctx)[:-1]):
        held.update({k | bit: swap(v, "ctx", bit) for k, v in list(held.items())})
    token_chunks = [held[k] for k in range(ctx)]
    first = jnp.concatenate(
        [
            lax.dynamic_index_in_dim(first, flipped((me_dp ^ c), dp), 0, False)
            for c in range(dp)
        ]
    )
    qkv_weight = first[:, : 3 * cols]
    table = first[:, 4 * cols :].astype(f32).T
    time_shift_bias, query_shift, value_shift, output_shift, gain_one, bias_one, down_shift, gain_two, bias_two = [
        table[n] for n in range(len(vectors))
    ]
    up_shift = table[len(vectors) : len(vectors) + ratio].reshape(ratio, devices, own).transpose(1, 0, 2).reshape(hidden)
    shift_cols = trade([nn(time_feat, first[:, 3 * cols : 4 * cols])] * ctx, "ctx")
    time_shift = jnp.concatenate(to_absolute(shift_cols, me), axis=1) + time_shift_bias
    qkv_shift = []
    for p in range(cols // 128):
        at = me * cols + p * 128
        qkv_shift.append(lax.dynamic_slice_in_dim(query_shift, at, 128))
        qkv_shift.append(jnp.zeros((128,), f32))
        qkv_shift.append(lax.dynamic_slice_in_dim(value_shift, at, 128))
    qkv_shift = jnp.concatenate(qkv_shift)
    start_row = (jnp.concatenate(token_chunks).astype(f32) + time_shift).astype(bf16)
    residual_in = tokens.astype(f32) + time_shift
    qkv = (nn(start_row, qkv_weight) + qkv_shift).astype(bf16)

    info = spans(ids, me)
    ids_col, ids_row = ids.reshape(-1, 1), ids.reshape(-1, 1, BLOCK)
    mixed, logsum = attention_forward(info, qkv, ids_col, ids_row, per_chunk)
    returned = trade([mixed[k * piece : (k + 1) * piece] for k in range(ctx)], "ctx")
    returned, down_full = lax.optimization_barrier((returned, down_full))
    attended = jnp.concatenate(to_absolute(returned, me), axis=1)

    branch = nn(attended, output_full) + output_shift
    hidden_one, normed_one, inverse_one = normalize(residual_in + branch, gain_one, bias_one)
    hidden_low = hidden_one.astype(bf16)
    pre_gelu = nn(hidden_low, up_full) + up_shift
    share = 0.5 * (1.0 + lax.erf(pre_gelu * 0.5**0.5))
    activated = (pre_gelu * share).astype(bf16)
    slope = (share + pre_gelu * jnp.exp(-0.5 * pre_gelu * pre_gelu) * 0.3989422804014327).astype(bf16)
    activated, slope = lax.optimization_barrier((activated, slope))
    feed_out = nn(activated, down_full) + down_shift
    result, normed_two, inverse_two = normalize(hidden_one + feed_out, gain_two, bias_two)
    layer_out = result.astype(bf16)

    upstream = cotangent.astype(f32)
    grad_two, gain_two_grad, bias_two_grad = normalize_back(upstream, normed_two, inverse_two, gain_two)
    grad_feed = grad_two.astype(bf16)
    down_grad = tn(activated, grad_feed).astype(bf16)
    down_shift_grad = jnp.sum(grad_feed.astype(f32), axis=0)
    grad_inner = (nt(grad_feed, down_full) * slope.astype(f32)).astype(bf16)
    dp_names, ctx_names = [("dp", b) for b in bits(dp)], [("ctx", b) for b in bits(ctx)]
    names = dp_names[::-1] + ctx_names[::-1]
    core, turn, rest = ctx_names[0], dp_names[:2] + ctx_names[1:], dp_names[2:]
    whole = {}

    def share(label, array, height):
        size = (height, array.shape[-1])
        whole[label] = Halving(names, size)
        whole[label].terms = [(array.reshape([2] * len(names) + list(size)), names, [(0, d) for d in size])]
        whole[label].exchange(core)

    def stream(label, part, turned):
        sums = Halving(names, [high - low for low, high in part])
        sums.fixed = {core: sums.me[core]}
        sums.terms = [(array, left, part) for array, left, _ in whole[label].terms]
        return sums, turn[turned:] + turn[:turned] + rest

    def depart(moving, beside):
        going = [s.outgoing(name) for s, name in moving]
        going, beside = lax.optimization_barrier((going, beside))
        return [(s, name, swap(value, *name)) for (s, name), value in zip(moving, going)], beside

    def land(flights, beside):
        values, beside = lax.optimization_barrier(([value for _, _, value in flights], beside))
        for (s, name, _), value in zip(flights, values):
            s.arrived(name, value)
        return beside

    def following(pairs):
        return [(s, o.pop(0)) for s, o in pairs if o]

    share("down", down_grad, ratio * own)
    streams = [stream("down", [(0, ratio * own), (0, width)], 0)]
    ahead, grad_inner = depart(following(streams), grad_inner)
    up_grad = tn(hidden_low, grad_inner).astype(bf16)
    up_shift_grad = jnp.sum(grad_inner.astype(f32), axis=0)
    grad_hidden = grad_two + nt(grad_inner, up_full)
    grad_one, gain_one_grad, bias_one_grad = normalize_back(grad_hidden, normed_one, inverse_one, gain_one)
    grad_branch = grad_one.astype(bf16)
    output_grad = tn(attended, grad_branch).astype(bf16)
    output_shift_grad = jnp.sum(grad_branch.astype(f32), axis=0)
    vector_grads = jnp.stack(
        [output_shift_grad, gain_one_grad, bias_one_grad, down_shift_grad, gain_two_grad, bias_two_grad]
    )
    vector_grads = lax.optimization_barrier(vector_grads).reshape(6, devices, own).transpose(1, 0, 2).reshape(devices, 6 * own)
    vector_grads = jnp.concatenate([vector_grads, up_shift_grad.reshape(devices, ratio * own)], axis=1)
    vector_grads = jnp.pad(vector_grads, ((0, 0), (0, width - vector_grads.shape[1]))).astype(bf16)
    extra = 8
    rest_grad = jnp.concatenate(
        [output_grad.reshape(devices, own, width), jnp.broadcast_to(vector_grads[:, None], (devices, extra, width))],
        axis=1,
    )

    share("up", up_grad, own)
    share("rest", rest_grad, own + extra)
    streams += [
        stream("up", [(0, own), (0, hidden // 2)], 2),
        stream("up", [(0, own), (hidden // 2, hidden)], 0),
        stream("rest", [(0, own + extra), (0, width)], 0),
    ]

    grad_attended = nt(grad_branch, output_full).astype(bf16)
    pieces = [lax.dynamic_slice_in_dim(grad_attended, (me ^ k) * cols, cols, 1) for k in range(ctx)]
    grad_mixed = jnp.concatenate(trade(pieces, "ctx"))
    grad_mixed = land(ahead, grad_mixed)

    def weight_stream(product):
        size = (ctx * own, product.shape[1])
        sums = Halving(dp_names[::-1], size)
        array = product.reshape([2] * len(dp_names) + list(size))
        sums.terms = [(array, dp_names[::-1], [(0, d) for d in size])]
        return sums, list(dp_names)

    def products(grad):
        return tn(start_row, grad), jnp.sum(grad.astype(f32), axis=0)

    grads, pair_streams, qkv_sum = [], [], []
    for pair in range(cols // 128):
        flights, grad_mixed = depart(following(streams + pair_streams), grad_mixed)
        grad = attention_backward(pair, info, qkv, grad_mixed, mixed, logsum, ids_col, ids_row, per_chunk)
        if pair == 0:
            grad_mixed, grad, (product, total) = land(flights, (grad_mixed, grad, products(grad)))
        else:
            grad_mixed, grad = land(flights, (grad_mixed, grad))
            product, total = products(grad)
        grads.append(grad)
        pair_streams.append(weight_stream(product))
        qkv_sum.append(total)

    qkv_sum = jnp.concatenate(qkv_sum)
    row_sum = jnp.sum(grad_one, axis=0, keepdims=True) + lax.dot_general(
        qkv_sum[None],
        qkv_weight.astype(f32),
        (((1,), (1,)), ((), ())),
        precision=lax.Precision.HIGHEST,
        preferred_element_type=f32,
    )
    message = jnp.concatenate(
        [row_sum]
        + [qkv_sum[None, (3 * p + n) * 128 : (3 * p + n + 1) * 128] for n in (0, 2) for p in range(cols // 128)]
        + [time_feat.astype(f32)],
        axis=1,
    )
    message_names = dp_names[::-1]

    rows = jnp.concatenate(grads, axis=1).reshape(ctx // 2, 2, piece, 3 * cols)
    odd = nt(rows[:, 1].reshape(-1, 3 * cols), qkv_weight).astype(bf16)
    flights, (rows, odd, message) = depart(following(streams + pair_streams), (rows, odd, message))
    odd = swap(odd, *core)
    reply = swap(message, *message_names.pop(0))
    even = nt(rows[:, 0].reshape(-1, 3 * cols), qkv_weight)
    even, odd, message, reply = land(flights, (even, odd, message, reply))
    message = jnp.concatenate([message, reply])
    even = (even + odd.astype(f32)).reshape(ctx // 2, piece, width)
    away = [even[n].astype(bf16) for n in range(1, ctx // 2)]
    kept, came = [], None
    while any(o for _, o in streams + pair_streams) or message_names:
        fast, slow = following(pair_streams), following(streams)
        flights, (away, message) = depart(fast + slow, (away, message))
        if came is None:
            came = [swap(value, "ctx", 2 * n + 2) for n, value in enumerate(away)]
        if message_names:
            message = jnp.concatenate([message, swap(message, *message_names.pop(0))])
        kept += flights[len(fast) :]
        flights = flights[: len(fast)]
        if any(o for _, o in streams):
            flights, kept = flights + kept, []
        if not any(o for _, o in pair_streams):
            flights, kept = flights + kept, []
        message, came = land(flights, (message, came)) if not kept else (land(flights, message), came)
    summed = jnp.concatenate([s.result() for s, _ in pair_streams], axis=1).reshape(ctx, own, 3 * cols)
    summed = [lax.dynamic_index_in_dim(summed, (me ^ k), 0, False) for k in range(ctx)]
    summed, message = lax.optimization_barrier((summed, message))
    blocks_out = to_absolute(trade(summed, "ctx"), me)
    message = jnp.stack(trade([message] * ctx, "ctx"))
    tokens_grad = (grad_one + sum([c.astype(f32) for c in came], even[0])).astype(bf16)
    down_weight_grad, up_left, up_right, rest_left = [s.result() for s, _ in streams]
    up_weight_grad = jnp.concatenate([up_left, up_right], axis=1)
    output_weight_grad, vector_grads = rest_left[:own], rest_left[own]
    output_bias_grad, mixing_gain_grad, mixing_bias_grad, down_bias_grad, final_gain_grad, final_bias_grad = [
        vector_grads[n * own : (n + 1) * own] for n in range(6)
    ]
    up_bias_grad = vector_grads[6 * own : (6 + ratio) * own]

    mine = (me_dp * ctx + me) * own
    row_sums = jnp.sum(message[:, :, :width], axis=0)
    time_weight_grad = lax.dot_general(
        lax.dynamic_slice_in_dim(message[0, :, width + 2 * cols :], mine, own, 1),
        row_sums,
        (((0,), (0,)), ((), ())),
        precision=lax.Precision.HIGHEST,
        preferred_element_type=f32,
    )
    time_bias_grad = lax.dynamic_slice_in_dim(jnp.sum(row_sums, axis=0), mine, own)
    sums = jnp.sum(message[:, :, width : width + 2 * cols], axis=1)
    sums = lax.dynamic_index_in_dim(sums, mine // cols ^ me, 0, False)
    query_bias_grad = lax.dynamic_slice_in_dim(sums[:cols], mine % cols, own)
    value_bias_grad = lax.dynamic_slice_in_dim(sums[cols:], mine % cols, own)

    query_weight_grad, key_weight_grad, value_weight_grad = [
        jnp.concatenate(
            [
                block[:, (3 * p + n) * 128 : (3 * p + n + 1) * 128]
                for block in blocks_out
                for p in range(cols // 128)
            ],
            axis=1,
        )
        for n in range(3)
    ]
    return (
        layer_out[None],
        tokens_grad[None],
        time_weight_grad,
        time_bias_grad,
        query_weight_grad,
        query_bias_grad,
        key_weight_grad,
        value_weight_grad,
        value_bias_grad,
        output_weight_grad,
        output_bias_grad,
        mixing_gain_grad,
        mixing_bias_grad,
        up_weight_grad,
        up_bias_grad,
        down_weight_grad,
        down_bias_grad,
        final_gain_grad,
        final_bias_grad,
    )


def solution(mesh):
    rows, split_rows, split = P("dp", "ctx", None), P(BOTH, None), P(BOTH)
    return jax.shard_map(
        shards,
        mesh=mesh,
        in_specs=(
            rows, P("dp", None), rows, P("dp", None), split_rows, split, split_rows, split, split_rows, split_rows,
            split, split_rows, split, split, split, split_rows, split, split_rows, split, split, split,
        ),
        out_specs=(
            rows, rows, split_rows, split, split_rows, split, split_rows, split_rows, split, split_rows, split, split,
            split, split_rows, split, split_rows, split, split, split,
        ),
        check_vma=False,
    )
```

```python
import functools

import jax
import jax.numpy as jnp
from jax import lax
from jax.experimental import pallas as pl
from jax.experimental.pallas import tpu as pltpu
from jax.sharding import PartitionSpec as P

HEAD_DIM = 64
BLOCK = 256
MASKED = -1e30
EPSILON = 1e-05
SCALE = HEAD_DIM**-0.5
SCALE_LOG2 = SCALE * 1.4426950408889634
BOTH = ("dp", "ctx")
f32, bf16 = jnp.float32, jnp.bfloat16


def nn(left, right):
    return jnp.dot(left, right, preferred_element_type=f32)


def tn(left, right):
    return lax.dot_general(left, right, (((0,), (0,)), ((), ())), preferred_element_type=f32)


def nt(left, right):
    return lax.dot_general(left, right, (((1,), (1,)), ((), ())), preferred_element_type=f32)


def head_only(pair, which):
    lane = lax.broadcasted_iota(jnp.int32, pair.shape, 1)
    keep = (lane < HEAD_DIM) if which == 0 else (lane >= HEAD_DIM)
    return jnp.where(keep, pair, jnp.zeros_like(pair))


def place(block, me, per_chunk):
    return lax.bitwise_xor(block // per_chunk, me) * per_chunk + lax.rem(block, per_chunk)


def forward_kernel(per_chunk, pairs, info, qkv_ref, idc_ref, idr_ref, o_ref, lse_ref, o_acc, m_acc, l_acc):
    i = pl.program_id(0)
    me = info[2, 0]
    m_acc[...] = jnp.full_like(m_acc, MASKED)
    l_acc[...] = jnp.zeros_like(l_acc)
    o_acc[...] = jnp.zeros_like(o_acc)
    ids_q = idr_ref[pl.ds(i, 1)][0]
    here = pl.multiple_of(place(i, me, per_chunk) * BLOCK, BLOCK)

    queries = []
    for p in range(pairs):
        pair = qkv_ref[pl.ds(here, BLOCK), (3 * p) * 128 : (3 * p + 1) * 128]
        queries += [head_only(pair, 0), head_only(pair, 1)]

    def step(j, carry):
        at = pl.multiple_of(place(j, me, per_chunk) * BLOCK, BLOCK)
        same = idc_ref[pl.ds(pl.multiple_of(j * BLOCK, BLOCK), BLOCK), :] == ids_q
        heads = range(2 * pairs)
        peak = [m_acc[h] for h in heads]
        count = [l_acc[h] for h in heads]
        mixed = [o_acc[h * HEAD_DIM : (h + 1) * HEAD_DIM] for h in heads]
        values, scores = [], []
        for p in range(pairs):
            k_pair = qkv_ref[pl.ds(at, BLOCK), (3 * p + 1) * 128 : (3 * p + 2) * 128]
            values.append(qkv_ref[pl.ds(at, BLOCK), (3 * p + 2) * 128 : (3 * p + 3) * 128])
            scores += [nt(k_pair, queries[2 * p + w]) for w in range(2)]
        for h in heads:
            t = jnp.where(same, scores[h] * SCALE_LOG2, MASKED)
            new = jnp.maximum(peak[h], jnp.max(t, axis=0, keepdims=True))
            alpha = jnp.exp2(peak[h] - new)
            e = jnp.exp2(t - new)
            count[h] = count[h] * alpha + jnp.sum(e, axis=0, keepdims=True)
            peak[h] = new
            w = h % 2
            mixed[h] = mixed[h] * alpha + tn(values[h // 2], e.astype(bf16))[w * HEAD_DIM : (w + 1) * HEAD_DIM]
        for h in heads:
            m_acc[h], l_acc[h] = peak[h], count[h]
            o_acc[h * HEAD_DIM : (h + 1) * HEAD_DIM] = mixed[h]
        return carry

    lax.fori_loop(info[0, i], info[1, i], step, 0)
    for p in range(pairs):
        parts = []
        for w in range(2):
            h = 2 * p + w
            parts.append(o_acc[h * HEAD_DIM : (h + 1) * HEAD_DIM] / l_acc[h])
            lse_ref[0, h : h + 1, :] = m_acc[h] + jnp.log2(l_acc[h])
        o_ref[:, p * 128 : (p + 1) * 128] = jnp.concatenate(parts, axis=0).T.astype(bf16)


def attention_forward(info, qkv, ids_col, ids_row, per_chunk):
    rows, width = qkv.shape[0], qkv.shape[1] // 3
    blocks, heads = rows // BLOCK, width // HEAD_DIM
    return pl.pallas_call(
        functools.partial(forward_kernel, per_chunk, heads // 2),
        grid_spec=pltpu.PrefetchScalarGridSpec(
            num_scalar_prefetch=1,
            grid=(blocks,),
            in_specs=[
                pl.BlockSpec((rows, 3 * width), lambda i, info: (0, 0)),
                pl.BlockSpec((rows, 1), lambda i, info: (0, 0)),
                pl.BlockSpec((blocks, 1, BLOCK), lambda i, info: (0, 0, 0)),
            ],
            out_specs=[
                pl.BlockSpec((BLOCK, width), lambda i, info: (place(i, info[2, 0], per_chunk), 0)),
                pl.BlockSpec((1, heads, BLOCK), lambda i, info: (i, 0, 0)),
            ],
            scratch_shapes=[
                pltpu.VMEM((width, BLOCK), f32),
                pltpu.VMEM((heads, 1, BLOCK), f32),
                pltpu.VMEM((heads, 1, BLOCK), f32),
            ],
        ),
        out_shape=[
            jax.ShapeDtypeStruct((rows, width), bf16),
            jax.ShapeDtypeStruct((blocks, heads, BLOCK), f32),
        ],
        cost_estimate=pl.CostEstimate(flops=30 * 10**9, bytes_accessed=6 * rows * width, transcendentals=10**7),
        name="attention_forward",
    )(info, qkv, ids_col, ids_row)


def backward_kernel(
    per_chunk, first, info, q_ref, k_ref, v_ref, do_ref, o_ref, lse_ref, idc_ref, idr_ref,
    out_ref, delta_ref, dq_acc, dk_acc, dv_acc,
):
    j = pl.program_id(0)
    blocks = pl.num_programs(0)
    me = info[2, 0]

    @pl.when(j == 0)
    def _():
        dq_acc[...] = jnp.zeros_like(dq_acc)

        def fill(i, carry):
            at = pl.multiple_of(place(i, me, per_chunk) * BLOCK, BLOCK)
            prod = (do_ref[pl.ds(at, BLOCK), :].astype(f32) * o_ref[pl.ds(at, BLOCK), :].astype(f32)).T
            for w in range(2):
                delta_ref[i, w : w + 1, :] = jnp.sum(prod[w * HEAD_DIM : (w + 1) * HEAD_DIM], axis=0, keepdims=True)
            return carry

        lax.fori_loop(0, blocks, fill, 0)

    dk_acc[...] = jnp.zeros_like(dk_acc)
    dv_acc[...] = jnp.zeros_like(dv_acc)
    k_turned = k_ref[...].T
    feature = lax.broadcasted_iota(jnp.int32, k_turned.shape, 0)
    turned = [
        jnp.where(feature < HEAD_DIM, k_turned, jnp.zeros_like(k_turned)),
        jnp.where(feature >= HEAD_DIM, k_turned, jnp.zeros_like(k_turned)),
    ]
    ids_k = idc_ref[pl.ds(pl.multiple_of(j * BLOCK, BLOCK), BLOCK), :]

    def step(i, carry):
        at = pl.multiple_of(place(i, me, per_chunk) * BLOCK, BLOCK)
        same = ids_k == idr_ref[pl.ds(i, 1)][0]
        k_pair, v_pair = k_ref[...], v_ref[...]
        q_pair, do_pair = q_ref[pl.ds(at, BLOCK), :], do_ref[pl.ds(at, BLOCK), :]
        es, dss, qs, dos = [], [], [], []
        for w in range(2):
            q_one, do_one = head_only(q_pair, w), head_only(do_pair, w)
            t = nt(k_pair, q_one) * SCALE_LOG2 - lse_ref[i, first + w : first + w + 1, :]
            e = jnp.exp2(jnp.where(same, t, MASKED))
            ds = (e * (nt(v_pair, do_one) - delta_ref[i, w : w + 1, :])).astype(bf16)
            es.append(e.astype(bf16))
            dss.append(ds)
            qs.append(q_one)
            dos.append(do_one)
        dv_acc[...] += nn(jnp.concatenate(es, axis=1), jnp.concatenate(dos, axis=0))
        dk_acc[...] += nn(jnp.concatenate(dss, axis=1), jnp.concatenate(qs, axis=0))
        dq_acc[i] += nn(jnp.concatenate(turned, axis=1), jnp.concatenate(dss, axis=0))
        return carry

    lax.fori_loop(info[0, j], info[1, j], step, 0)
    mine = pl.multiple_of(place(j, me, per_chunk) * BLOCK, BLOCK)
    out_ref[pl.ds(mine, BLOCK), 128:256] = (dk_acc[...] * SCALE).astype(bf16)
    out_ref[pl.ds(mine, BLOCK), 256:384] = dv_acc[...].astype(bf16)

    @pl.when(j == blocks - 1)
    def _():
        def turn_back(i, carry):
            at = pl.multiple_of(place(i, me, per_chunk) * BLOCK, BLOCK)
            out_ref[pl.ds(at, BLOCK), 0:128] = (dq_acc[i] * SCALE).T.astype(bf16)
            return carry

        lax.fori_loop(0, blocks, turn_back, 0)


def attention_backward(pair, info, qkv, do, o, lse, ids_col, ids_row, per_chunk):
    rows, width = o.shape
    blocks, heads = rows // BLOCK, width // HEAD_DIM
    return pl.pallas_call(
        functools.partial(backward_kernel, per_chunk, 2 * pair),
        grid_spec=pltpu.PrefetchScalarGridSpec(
            num_scalar_prefetch=1,
            grid=(blocks,),
            in_specs=[
                pl.BlockSpec((rows, 128), lambda i, info: (0, 3 * pair)),
                pl.BlockSpec((BLOCK, 128), lambda i, info: (place(i, info[2, 0], per_chunk), 3 * pair + 1)),
                pl.BlockSpec((BLOCK, 128), lambda i, info: (place(i, info[2, 0], per_chunk), 3 * pair + 2)),
                pl.BlockSpec((rows, 128), lambda i, info: (0, pair)),
                pl.BlockSpec((rows, 128), lambda i, info: (0, pair)),
                pl.BlockSpec((blocks, heads, BLOCK), lambda i, info: (0, 0, 0)),
                pl.BlockSpec((rows, 1), lambda i, info: (0, 0)),
                pl.BlockSpec((blocks, 1, BLOCK), lambda i, info: (0, 0, 0)),
            ],
            out_specs=pl.BlockSpec((rows, 384), lambda i, info: (0, 0)),
            scratch_shapes=[
                pltpu.VMEM((blocks, 2, BLOCK), f32),
                pltpu.VMEM((blocks, 128, BLOCK), f32),
                pltpu.VMEM((BLOCK, 128), f32),
                pltpu.VMEM((BLOCK, 128), f32),
            ],
        ),
        out_shape=jax.ShapeDtypeStruct((rows, 384), bf16),
        cost_estimate=pl.CostEstimate(flops=25 * 10**9, bytes_accessed=8 * rows * 128, transcendentals=10**7),
        name="attention_backward",
    )(info, qkv, qkv, qkv, do, o, lse, ids_col, ids_row)


def spans(ids, me):
    blocks = ids.shape[0] // BLOCK
    per_block = ids.reshape(blocks, BLOCK)
    low = jnp.sum(ids[None, :] < per_block[:, :1], axis=1) // BLOCK
    high = (jnp.sum(ids[None, :] <= per_block[:, -1:], axis=1) + BLOCK - 1) // BLOCK
    return jnp.stack([low, high, jnp.full((blocks,), me.astype(low.dtype))]).astype(jnp.int32)


def own_index(axis):
    return lax.axis_index(axis).astype(jnp.uint32)


def swap(value, axis, mask):
    size = lax.axis_size(axis)
    return lax.ppermute(value, axis, [(i, i ^ mask) for i in range(size)])


def bits(size):
    return [1 << b for b in range(size.bit_length() - 1)]


def trade(pieces, axis):
    return [pieces[0]] + [swap(pieces[k], axis, k) for k in range(1, len(pieces))]


def to_absolute(pieces, me):
    stacked = jnp.stack(pieces)
    return [lax.dynamic_index_in_dim(stacked, (me ^ c), 0, False) for c in range(len(pieces))]


class Halving:
    def __init__(self, names, shape):
        self.me = {n: (own_index(n[0]) >> (n[1].bit_length() - 1)) & 1 for n in names}
        self.names, self.terms, self.fixed, self.shape = list(names), [], {}, shape

    def cut(self, term, chosen):
        array, names, part = term
        starts, sizes = [], []
        for n in names:
            starts.append(chosen.get(n, jnp.uint32(0)))
            sizes.append(1 if n in chosen else 2)
        for low, high in part:
            starts.append(jnp.uint32(low))
            sizes.append(high - low)
        left = [2 for n in names if n not in chosen]
        return lax.dynamic_slice(array, starts, sizes).reshape(left + [h - l for l, h in part])

    def total(self, chosen):
        pieces = [self.cut(t, chosen).astype(f32) for t in self.terms]
        return sum(pieces[1:], pieces[0])

    def outgoing(self, name):
        return self.total({**self.fixed, name: 1 - self.me[name]}).astype(bf16)

    def arrived(self, name, value):
        self.fixed[name] = self.me[name]
        names = [n for n in self.names if n not in self.fixed]
        self.terms.append((value, names, [(0, d) for d in self.shape]))

    def exchange(self, name):
        self.arrived(name, swap(self.outgoing(name), *name))

    def result(self):
        return self.total(self.fixed)


def normalize(values, gain, shift):
    average = jnp.mean(values, axis=-1, keepdims=True)
    centered = values - average
    inverse = lax.rsqrt(jnp.mean(centered * centered, axis=-1, keepdims=True) + EPSILON)
    normed = centered * inverse
    return normed * gain + shift, normed, inverse


def normalize_back(upstream, normed, inverse, gain):
    scaled = upstream * gain
    plain = jnp.mean(scaled, axis=-1, keepdims=True)
    cross = jnp.mean(scaled * normed, axis=-1, keepdims=True)
    result = inverse * (scaled - plain - normed * cross)
    return result, jnp.sum(upstream * normed, axis=0), jnp.sum(upstream, axis=0)


def shards(
    tokens, time_feat, cotangent, segment_ids, time_weight, time_bias, query_weight, query_bias, key_weight,
    value_weight, value_bias, output_weight, output_bias, mixing_gain, mixing_bias, up_weight, up_bias,
    down_weight, down_bias, final_gain, final_bias,
):
    me_dp, me = own_index("dp"), own_index("ctx")
    dp, ctx = lax.axis_size("dp"), lax.axis_size("ctx")
    devices = dp * ctx
    piece, width = tokens.shape[1], tokens.shape[2]
    hidden = up_weight.shape[1]
    own, ratio = width // devices, hidden // width
    cols = width // ctx
    per_chunk = piece // BLOCK
    tokens, cotangent, ids = tokens[0], cotangent[0], segment_ids[0]

    held = {0: tokens, ctx // 2: swap(tokens, "ctx", ctx // 2)}
    vectors = [
        time_bias, query_bias, value_bias, output_bias, mixing_gain, mixing_bias, down_bias, final_gain, final_bias
    ]
    small = jnp.concatenate([jnp.stack(vectors), up_bias.reshape(ratio, own)]).T
    small = jnp.pad(small, ((0, 0), (0, 128 - small.shape[1])))
    pieces = []
    for k in range(ctx):
        at = (me ^ k) * cols
        parts = [
            lax.dynamic_slice_in_dim(w, at + p * 128, 128, 1)
            for p in range(cols // 128)
            for w in (query_weight, key_weight, value_weight)
        ] + [lax.dynamic_slice_in_dim(time_weight, at, cols, 1)]
        pieces.append(jnp.concatenate(parts + [small], axis=1))
    first = jnp.concatenate(to_absolute(trade(pieces, "ctx"), me))
    second = jnp.concatenate(
        [up_weight, output_weight] + [down_weight[n * own : (n + 1) * own] for n in range(ratio)], axis=1
    )
    second, first = lax.optimization_barrier((second, first))
    second = lax.all_gather(second, BOTH, axis=0, tiled=True)
    up_full, output_full = second[:, :hidden], second[:, hidden : hidden + width]
    down_full = jnp.stack(
        [second[:, hidden + n * width : hidden + (n + 1) * width].reshape(devices, own, width) for n in range(1, 1 + ratio)],
        axis=1,
    ).reshape(hidden, width)

    first = first[None]
    for n, bit in enumerate(reversed(bits(dp))):
        if n == 1:
            first, held[ctx // 2] = lax.optimization_barrier((first, held[ctx // 2]))
        other, side = swap(first, "dp", bit), jnp.minimum(me_dp & bit, 1)
        own_side = lax.broadcasted_iota(jnp.uint32, (1, 2, 1, 1), 1) == side
        first = jnp.where(own_side, first[:, None], other[:, None])
        first = first.reshape((-1,) + first.shape[2:])
    for bit in reversed(bits(ctx)[:-1]):
        held.update({k | bit: swap(v, "ctx", bit) for k, v in list(held.items())})
    token_chunks = [held[k] for k in range(ctx)]
    first = first.reshape(width, -1)
    qkv_weight = first[:, : 3 * cols]
    table = first[:, 4 * cols :].astype(f32).T
    time_shift_bias, query_shift, value_shift, output_shift, gain_one, bias_one, down_shift, gain_two, bias_two = [
        table[n] for n in range(len(vectors))
    ]
    up_shift = table[len(vectors) : len(vectors) + ratio].reshape(ratio, devices, own).transpose(1, 0, 2).reshape(hidden)
    shift_cols = trade([nn(time_feat, first[:, 3 * cols : 4 * cols])] * ctx, "ctx")
    time_shift = jnp.concatenate(to_absolute(shift_cols, me), axis=1) + time_shift_bias
    qkv_shift = []
    for p in range(cols // 128):
        at = me * cols + p * 128
        qkv_shift.append(lax.dynamic_slice_in_dim(query_shift, at, 128))
        qkv_shift.append(jnp.zeros((128,), f32))
        qkv_shift.append(lax.dynamic_slice_in_dim(value_shift, at, 128))
    qkv_shift = jnp.concatenate(qkv_shift)
    start_row = (jnp.concatenate(token_chunks).astype(f32) + time_shift).astype(bf16)
    residual_in = tokens.astype(f32) + time_shift
    qkv = (nn(start_row, qkv_weight) + qkv_shift).astype(bf16)

    info = spans(ids, me)
    ids_col, ids_row = ids.reshape(-1, 1), ids.reshape(-1, 1, BLOCK)
    mixed, logsum = attention_forward(info, qkv, ids_col, ids_row, per_chunk)
    returned = trade([mixed[k * piece : (k + 1) * piece] for k in range(ctx)], "ctx")
    returned, down_full = lax.optimization_barrier((returned, down_full))
    attended = jnp.concatenate(to_absolute(returned, me), axis=1)

    branch = nn(attended, output_full) + output_shift
    hidden_one, normed_one, inverse_one = normalize(residual_in + branch, gain_one, bias_one)
    hidden_low = hidden_one.astype(bf16)
    pre_gelu = nn(hidden_low, up_full) + up_shift
    share = 0.5 * (1.0 + lax.erf(pre_gelu * 0.5**0.5))
    activated = (pre_gelu * share).astype(bf16)
    slope = (share + pre_gelu * jnp.exp(-0.5 * pre_gelu * pre_gelu) * 0.3989422804014327).astype(bf16)
    activated, slope = lax.optimization_barrier((activated, slope))
    feed_out = nn(activated, down_full) + down_shift
    result, normed_two, inverse_two = normalize(hidden_one + feed_out, gain_two, bias_two)
    layer_out = result.astype(bf16)

    upstream = cotangent.astype(f32)
    grad_two, gain_two_grad, bias_two_grad = normalize_back(upstream, normed_two, inverse_two, gain_two)
    grad_feed = grad_two.astype(bf16)
    down_grad = tn(activated, grad_feed).astype(bf16)
    down_shift_grad = jnp.sum(grad_feed.astype(f32), axis=0)
    grad_inner = (nt(grad_feed, down_full) * slope.astype(f32)).astype(bf16)
    dp_names, ctx_names = [("dp", b) for b in bits(dp)], [("ctx", b) for b in bits(ctx)]
    names = dp_names[::-1] + ctx_names[::-1]
    core, turn, rest = ctx_names[0], dp_names[:2] + ctx_names[1:], dp_names[2:]
    whole = {}

    def share(label, array, height):
        size = (height, array.shape[-1])
        whole[label] = Halving(names, size)
        whole[label].terms = [(array.reshape([2] * len(names) + list(size)), names, [(0, d) for d in size])]
        whole[label].exchange(core)

    def stream(label, part, turned):
        sums = Halving(names, [high - low for low, high in part])
        sums.fixed = {core: sums.me[core]}
        sums.terms = [(array, left, part) for array, left, _ in whole[label].terms]
        return sums, turn[turned:] + turn[:turned] + rest

    def depart(moving, beside):
        going = [s.outgoing(name) for s, name in moving]
        going, beside = lax.optimization_barrier((going, beside))
        return [(s, name, swap(value, *name)) for (s, name), value in zip(moving, going)], beside

    def land(flights, beside):
        values, beside = lax.optimization_barrier(([value for _, _, value in flights], beside))
        for (s, name, _), value in zip(flights, values):
            s.arrived(name, value)
        return beside

    def following(pairs):
        return [(s, o.pop(0)) for s, o in pairs if o]

    share("down", down_grad, ratio * own)
    streams = [stream("down", [(0, ratio * own), (0, width)], 0)]
    ahead, grad_inner = depart(following(streams), grad_inner)
    up_grad = tn(hidden_low, grad_inner).astype(bf16)
    up_shift_grad = jnp.sum(grad_inner.astype(f32), axis=0)
    grad_hidden = grad_two + nt(grad_inner, up_full)
    grad_one, gain_one_grad, bias_one_grad = normalize_back(grad_hidden, normed_one, inverse_one, gain_one)
    grad_branch = grad_one.astype(bf16)
    output_grad = tn(attended, grad_branch).astype(bf16)
    output_shift_grad = jnp.sum(grad_branch.astype(f32), axis=0)
    vector_grads = jnp.stack(
        [output_shift_grad, gain_one_grad, bias_one_grad, down_shift_grad, gain_two_grad, bias_two_grad]
    )
    vector_grads = lax.optimization_barrier(vector_grads).reshape(6, devices, own).transpose(1, 0, 2).reshape(devices, 6 * own)
    vector_grads = jnp.concatenate([vector_grads, up_shift_grad.reshape(devices, ratio * own)], axis=1)
    vector_grads = jnp.pad(vector_grads, ((0, 0), (0, width - vector_grads.shape[1]))).astype(bf16)
    extra = 8
    rest_grad = jnp.concatenate(
        [output_grad.reshape(devices, own, width), jnp.broadcast_to(vector_grads[:, None], (devices, extra, width))],
        axis=1,
    )

    share("up", up_grad, own)
    share("rest", rest_grad, own + extra)
    streams += [
        stream("up", [(0, own), (0, hidden // 2)], 2),
        stream("up", [(0, own), (hidden // 2, hidden)], 0),
        stream("rest", [(0, own + extra), (0, width)], 0),
    ]

    grad_attended = nt(grad_branch, output_full).astype(bf16)
    pieces = [lax.dynamic_slice_in_dim(grad_attended, (me ^ k) * cols, cols, 1) for k in range(ctx)]
    grad_mixed = jnp.concatenate(trade(pieces, "ctx"))
    grad_mixed = land(ahead, grad_mixed)

    def weight_stream(product):
        size = (ctx * own, product.shape[1])
        sums = Halving(dp_names[::-1], size)
        array = product.reshape([2] * len(dp_names) + list(size))
        sums.terms = [(array, dp_names[::-1], [(0, d) for d in size])]
        return sums, list(dp_names)

    def products(grad):
        return tn(start_row, grad), jnp.sum(grad.astype(f32), axis=0)

    grads, pair_streams, qkv_sum = [], [], []
    for pair in range(cols // 128):
        flights, grad_mixed = depart(following(streams + pair_streams), grad_mixed)
        grad = attention_backward(pair, info, qkv, grad_mixed, mixed, logsum, ids_col, ids_row, per_chunk)
        if pair == 0:
            grad_mixed, grad, (product, total) = land(flights, (grad_mixed, grad, products(grad)))
        else:
            grad_mixed, grad = land(flights, (grad_mixed, grad))
            product, total = products(grad)
        grads.append(grad)
        pair_streams.append(weight_stream(product))
        qkv_sum.append(total)

    qkv_sum = jnp.concatenate(qkv_sum)
    row_sum = jnp.sum(grad_one, axis=0, keepdims=True) + lax.dot_general(
        qkv_sum[None],
        qkv_weight.astype(f32),
        (((1,), (1,)), ((), ())),
        precision=lax.Precision.HIGHEST,
        preferred_element_type=f32,
    )
    message = jnp.concatenate(
        [row_sum]
        + [qkv_sum[None, (3 * p + n) * 128 : (3 * p + n + 1) * 128] for n in (0, 2) for p in range(cols // 128)]
        + [time_feat.astype(f32)],
        axis=1,
    )
    message_names = dp_names[::-1]

    rows = jnp.concatenate(grads, axis=1).reshape(ctx // 2, 2, piece, 3 * cols)
    odd = nt(rows[:, 1].reshape(-1, 3 * cols), qkv_weight).astype(bf16)
    flights, (rows, odd, message) = depart(following(streams + pair_streams), (rows, odd, message))
    odd = swap(odd, *core)
    reply = swap(message, *message_names.pop(0))
    even = nt(rows[:, 0].reshape(-1, 3 * cols), qkv_weight)
    even, odd, message, reply = land(flights, (even, odd, message, reply))
    message = jnp.concatenate([message, reply])
    even = (even + odd.astype(f32)).reshape(ctx // 2, piece, width)
    away = [even[n].astype(bf16) for n in range(1, ctx // 2)]
    kept, came = [], None
    while any(o for _, o in streams + pair_streams) or message_names:
        fast, slow = following(pair_streams), following(streams)
        flights, (away, message) = depart(fast + slow, (away, message))
        if came is None:
            came = [swap(value, "ctx", 2 * n + 2) for n, value in enumerate(away)]
        if message_names:
            message = jnp.concatenate([message, swap(message, *message_names.pop(0))])
        kept += flights[len(fast) :]
        flights = flights[: len(fast)]
        if any(o for _, o in streams):
            flights, kept = flights + kept, []
        if not any(o for _, o in pair_streams):
            flights, kept = flights + kept, []
        message, came = land(flights, (message, came)) if not kept else (land(flights, message), came)
    summed = jnp.concatenate([s.result() for s, _ in pair_streams], axis=1).reshape(ctx, own, 3 * cols)
    summed = [lax.dynamic_index_in_dim(summed, (me ^ k), 0, False) for k in range(ctx)]
    summed, message = lax.optimization_barrier((summed, message))
    blocks_out = to_absolute(trade(summed, "ctx"), me)
    message = jnp.stack(trade([message] * ctx, "ctx"))
    tokens_grad = (grad_one + sum([c.astype(f32) for c in came], even[0])).astype(bf16)
    down_weight_grad, up_left, up_right, rest_left = [s.result() for s, _ in streams]
    up_weight_grad = jnp.concatenate([up_left, up_right], axis=1)
    output_weight_grad, vector_grads = rest_left[:own], rest_left[own]
    output_bias_grad, mixing_gain_grad, mixing_bias_grad, down_bias_grad, final_gain_grad, final_bias_grad = [
        vector_grads[n * own : (n + 1) * own] for n in range(6)
    ]
    up_bias_grad = vector_grads[6 * own : (6 + ratio) * own]

    mine = (me_dp * ctx + me) * own
    row_sums = jnp.sum(message[:, :, :width], axis=0)
    time_weight_grad = lax.dot_general(
        lax.dynamic_slice_in_dim(message[0, :, width + 2 * cols :], mine, own, 1),
        row_sums,
        (((0,), (0,)), ((), ())),
        precision=lax.Precision.HIGHEST,
        preferred_element_type=f32,
    )
    time_bias_grad = lax.dynamic_slice_in_dim(jnp.sum(row_sums, axis=0), mine, own)
    sums = jnp.sum(message[:, :, width : width + 2 * cols], axis=1)
    sums = lax.dynamic_index_in_dim(sums, mine // cols ^ me, 0, False)
    query_bias_grad = lax.dynamic_slice_in_dim(sums[:cols], mine % cols, own)
    value_bias_grad = lax.dynamic_slice_in_dim(sums[cols:], mine % cols, own)

    query_weight_grad, key_weight_grad, value_weight_grad = [
        jnp.concatenate(
            [
                block[:, (3 * p + n) * 128 : (3 * p + n + 1) * 128]
                for block in blocks_out
                for p in range(cols // 128)
            ],
            axis=1,
        )
        for n in range(3)
    ]
    return (
        layer_out[None],
        tokens_grad[None],
        time_weight_grad,
        time_bias_grad,
        query_weight_grad,
        query_bias_grad,
        key_weight_grad,
        value_weight_grad,
        value_bias_grad,
        output_weight_grad,
        output_bias_grad,
        mixing_gain_grad,
        mixing_bias_grad,
        up_weight_grad,
        up_bias_grad,
        down_weight_grad,
        down_bias_grad,
        final_gain_grad,
        final_bias_grad,
    )


def solution(mesh):
    rows, split_rows, split = P("dp", "ctx", None), P(BOTH, None), P(BOTH)
    return jax.shard_map(
        shards,
        mesh=mesh,
        in_specs=(
            rows, P("dp", None), rows, P("dp", None), split_rows, split, split_rows, split, split_rows, split_rows,
            split, split_rows, split, split, split, split_rows, split, split_rows, split, split, split,
        ),
        out_specs=(
            rows, rows, split_rows, split, split_rows, split, split_rows, split_rows, split, split_rows, split, split,
            split, split_rows, split, split_rows, split, split, split,
        ),
        check_vma=False,
    )
```

```python
import functools

import jax
import jax.numpy as jnp
from jax import lax
from jax.experimental import pallas as pl
from jax.experimental.pallas import tpu as pltpu
from jax.sharding import PartitionSpec as P

HEAD_DIM = 64
BLOCK = 256
MASKED = -1e30
EPSILON = 1e-05
SCALE = HEAD_DIM**-0.5
SCALE_LOG2 = SCALE * 1.4426950408889634
BOTH = ("dp", "ctx")
f32, bf16 = jnp.float32, jnp.bfloat16


def nn(left, right):
    return jnp.dot(left, right, preferred_element_type=f32)


def tn(left, right):
    return lax.dot_general(left, right, (((0,), (0,)), ((), ())), preferred_element_type=f32)


def nt(left, right):
    return lax.dot_general(left, right, (((1,), (1,)), ((), ())), preferred_element_type=f32)


def head_only(pair, which):
    lane = lax.broadcasted_iota(jnp.int32, pair.shape, 1)
    keep = (lane < HEAD_DIM) if which == 0 else (lane >= HEAD_DIM)
    return jnp.where(keep, pair, jnp.zeros_like(pair))


def place(block, me, per_chunk):
    return lax.bitwise_xor(block // per_chunk, me) * per_chunk + lax.rem(block, per_chunk)


def forward_kernel(per_chunk, pairs, info, qkv_ref, idc_ref, idr_ref, o_ref, lse_ref, o_acc, m_acc, l_acc):
    i = pl.program_id(0)
    me = info[2, 0]
    m_acc[...] = jnp.full_like(m_acc, MASKED)
    l_acc[...] = jnp.zeros_like(l_acc)
    o_acc[...] = jnp.zeros_like(o_acc)
    ids_q = idr_ref[pl.ds(i, 1)][0]
    here = pl.multiple_of(place(i, me, per_chunk) * BLOCK, BLOCK)

    queries = []
    for p in range(pairs):
        pair = qkv_ref[pl.ds(here, BLOCK), (3 * p) * 128 : (3 * p + 1) * 128]
        queries += [head_only(pair, 0), head_only(pair, 1)]

    def step(j, carry):
        at = pl.multiple_of(place(j, me, per_chunk) * BLOCK, BLOCK)
        same = idc_ref[pl.ds(pl.multiple_of(j * BLOCK, BLOCK), BLOCK), :] == ids_q
        heads = range(2 * pairs)
        peak = [m_acc[h] for h in heads]
        count = [l_acc[h] for h in heads]
        mixed = [o_acc[h * HEAD_DIM : (h + 1) * HEAD_DIM] for h in heads]
        values, scores = [], []
        for p in range(pairs):
            k_pair = qkv_ref[pl.ds(at, BLOCK), (3 * p + 1) * 128 : (3 * p + 2) * 128]
            values.append(qkv_ref[pl.ds(at, BLOCK), (3 * p + 2) * 128 : (3 * p + 3) * 128])
            scores += [nt(k_pair, queries[2 * p + w]) for w in range(2)]
        for h in heads:
            t = jnp.where(same, scores[h] * SCALE_LOG2, MASKED)
            new = jnp.maximum(peak[h], jnp.max(t, axis=0, keepdims=True))
            alpha = jnp.exp2(peak[h] - new)
            e = jnp.exp2(t - new)
            count[h] = count[h] * alpha + jnp.sum(e, axis=0, keepdims=True)
            peak[h] = new
            w = h % 2
            mixed[h] = mixed[h] * alpha + tn(values[h // 2], e.astype(bf16))[w * HEAD_DIM : (w + 1) * HEAD_DIM]
        for h in heads:
            m_acc[h], l_acc[h] = peak[h], count[h]
            o_acc[h * HEAD_DIM : (h + 1) * HEAD_DIM] = mixed[h]
        return carry

    lax.fori_loop(info[0, i], info[1, i], step, 0)
    for p in range(pairs):
        parts = []
        for w in range(2):
            h = 2 * p + w
            parts.append(o_acc[h * HEAD_DIM : (h + 1) * HEAD_DIM] / l_acc[h])
            lse_ref[0, h : h + 1, :] = m_acc[h] + jnp.log2(l_acc[h])
        o_ref[:, p * 128 : (p + 1) * 128] = jnp.concatenate(parts, axis=0).T.astype(bf16)


def attention_forward(info, qkv, ids_col, ids_row, per_chunk):
    rows, width = qkv.shape[0], qkv.shape[1] // 3
    blocks, heads = rows // BLOCK, width // HEAD_DIM
    return pl.pallas_call(
        functools.partial(forward_kernel, per_chunk, heads // 2),
        grid_spec=pltpu.PrefetchScalarGridSpec(
            num_scalar_prefetch=1,
            grid=(blocks,),
            in_specs=[
                pl.BlockSpec((rows, 3 * width), lambda i, info: (0, 0)),
                pl.BlockSpec((rows, 1), lambda i, info: (0, 0)),
                pl.BlockSpec((blocks, 1, BLOCK), lambda i, info: (0, 0, 0)),
            ],
            out_specs=[
                pl.BlockSpec((BLOCK, width), lambda i, info: (place(i, info[2, 0], per_chunk), 0)),
                pl.BlockSpec((1, heads, BLOCK), lambda i, info: (i, 0, 0)),
            ],
            scratch_shapes=[
                pltpu.VMEM((width, BLOCK), f32),
                pltpu.VMEM((heads, 1, BLOCK), f32),
                pltpu.VMEM((heads, 1, BLOCK), f32),
            ],
        ),
        out_shape=[
            jax.ShapeDtypeStruct((rows, width), bf16),
            jax.ShapeDtypeStruct((blocks, heads, BLOCK), f32),
        ],
        cost_estimate=pl.CostEstimate(flops=30 * 10**9, bytes_accessed=6 * rows * width, transcendentals=10**7),
        name="attention_forward",
    )(info, qkv, ids_col, ids_row)


def backward_kernel(
    per_chunk, first, info, q_ref, k_ref, v_ref, do_ref, o_ref, lse_ref, idc_ref, idr_ref,
    out_ref, delta_ref, dq_acc, dk_acc, dv_acc,
):
    j = pl.program_id(0)
    blocks = pl.num_programs(0)
    me = info[2, 0]

    @pl.when(j == 0)
    def _():
        dq_acc[...] = jnp.zeros_like(dq_acc)

        def fill(i, carry):
            at = pl.multiple_of(place(i, me, per_chunk) * BLOCK, BLOCK)
            prod = (do_ref[pl.ds(at, BLOCK), :].astype(f32) * o_ref[pl.ds(at, BLOCK), :].astype(f32)).T
            for w in range(2):
                delta_ref[i, w : w + 1, :] = jnp.sum(prod[w * HEAD_DIM : (w + 1) * HEAD_DIM], axis=0, keepdims=True)
            return carry

        lax.fori_loop(0, blocks, fill, 0)

    dk_acc[...] = jnp.zeros_like(dk_acc)
    dv_acc[...] = jnp.zeros_like(dv_acc)
    k_turned = k_ref[...].T
    feature = lax.broadcasted_iota(jnp.int32, k_turned.shape, 0)
    turned = [
        jnp.where(feature < HEAD_DIM, k_turned, jnp.zeros_like(k_turned)),
        jnp.where(feature >= HEAD_DIM, k_turned, jnp.zeros_like(k_turned)),
    ]
    ids_k = idc_ref[pl.ds(pl.multiple_of(j * BLOCK, BLOCK), BLOCK), :]

    def step(i, carry):
        at = pl.multiple_of(place(i, me, per_chunk) * BLOCK, BLOCK)
        same = ids_k == idr_ref[pl.ds(i, 1)][0]
        k_pair, v_pair = k_ref[...], v_ref[...]
        q_pair, do_pair = q_ref[pl.ds(at, BLOCK), :], do_ref[pl.ds(at, BLOCK), :]
        es, dss, qs, dos = [], [], [], []
        for w in range(2):
            q_one, do_one = head_only(q_pair, w), head_only(do_pair, w)
            t = nt(k_pair, q_one) * SCALE_LOG2 - lse_ref[i, first + w : first + w + 1, :]
            e = jnp.exp2(jnp.where(same, t, MASKED))
            ds = (e * (nt(v_pair, do_one) - delta_ref[i, w : w + 1, :])).astype(bf16)
            es.append(e.astype(bf16))
            dss.append(ds)
            qs.append(q_one)
            dos.append(do_one)
        dv_acc[...] += nn(jnp.concatenate(es, axis=1), jnp.concatenate(dos, axis=0))
        dk_acc[...] += nn(jnp.concatenate(dss, axis=1), jnp.concatenate(qs, axis=0))
        dq_acc[i] += nn(jnp.concatenate(turned, axis=1), jnp.concatenate(dss, axis=0))
        return carry

    lax.fori_loop(info[0, j], info[1, j], step, 0)
    mine = pl.multiple_of(place(j, me, per_chunk) * BLOCK, BLOCK)
    out_ref[pl.ds(mine, BLOCK), 128:256] = (dk_acc[...] * SCALE).astype(bf16)
    out_ref[pl.ds(mine, BLOCK), 256:384] = dv_acc[...].astype(bf16)

    @pl.when(j == blocks - 1)
    def _():
        def turn_back(i, carry):
            at = pl.multiple_of(place(i, me, per_chunk) * BLOCK, BLOCK)
            out_ref[pl.ds(at, BLOCK), 0:128] = (dq_acc[i] * SCALE).T.astype(bf16)
            return carry

        lax.fori_loop(0, blocks, turn_back, 0)


def attention_backward(pair, info, qkv, do, o, lse, ids_col, ids_row, per_chunk):
    rows, width = o.shape
    blocks, heads = rows // BLOCK, width // HEAD_DIM
    return pl.pallas_call(
        functools.partial(backward_kernel, per_chunk, 2 * pair),
        grid_spec=pltpu.PrefetchScalarGridSpec(
            num_scalar_prefetch=1,
            grid=(blocks,),
            in_specs=[
                pl.BlockSpec((rows, 128), lambda i, info: (0, 3 * pair)),
                pl.BlockSpec((BLOCK, 128), lambda i, info: (place(i, info[2, 0], per_chunk), 3 * pair + 1)),
                pl.BlockSpec((BLOCK, 128), lambda i, info: (place(i, info[2, 0], per_chunk), 3 * pair + 2)),
                pl.BlockSpec((rows, 128), lambda i, info: (0, pair)),
                pl.BlockSpec((rows, 128), lambda i, info: (0, pair)),
                pl.BlockSpec((blocks, heads, BLOCK), lambda i, info: (0, 0, 0)),
                pl.BlockSpec((rows, 1), lambda i, info: (0, 0)),
                pl.BlockSpec((blocks, 1, BLOCK), lambda i, info: (0, 0, 0)),
            ],
            out_specs=pl.BlockSpec((rows, 384), lambda i, info: (0, 0)),
            scratch_shapes=[
                pltpu.VMEM((blocks, 2, BLOCK), f32),
                pltpu.VMEM((blocks, 128, BLOCK), f32),
                pltpu.VMEM((BLOCK, 128), f32),
                pltpu.VMEM((BLOCK, 128), f32),
            ],
        ),
        out_shape=jax.ShapeDtypeStruct((rows, 384), bf16),
        cost_estimate=pl.CostEstimate(flops=25 * 10**9, bytes_accessed=8 * rows * 128, transcendentals=10**7),
        name="attention_backward",
    )(info, qkv, qkv, qkv, do, o, lse, ids_col, ids_row)


def spans(ids, me):
    blocks = ids.shape[0] // BLOCK
    per_block = ids.reshape(blocks, BLOCK)
    low = jnp.sum(ids[None, :] < per_block[:, :1], axis=1) // BLOCK
    high = (jnp.sum(ids[None, :] <= per_block[:, -1:], axis=1) + BLOCK - 1) // BLOCK
    return jnp.stack([low, high, jnp.full((blocks,), me.astype(low.dtype))]).astype(jnp.int32)


def own_index(axis):
    return lax.axis_index(axis).astype(jnp.uint32)


def swap(value, axis, mask):
    size = lax.axis_size(axis)
    return lax.ppermute(value, axis, [(i, i ^ mask) for i in range(size)])


def bits(size):
    return [1 << b for b in range(size.bit_length() - 1)]


def flipped(index, size):
    flags = bits(size)
    return sum(((index >> n) & 1) << (len(flags) - 1 - n) for n in range(len(flags)))


def trade(pieces, axis):
    return [pieces[0]] + [swap(pieces[k], axis, k) for k in range(1, len(pieces))]


def to_absolute(pieces, me):
    stacked = jnp.stack(pieces)
    return [lax.dynamic_index_in_dim(stacked, (me ^ c), 0, False) for c in range(len(pieces))]


class Halving:
    def __init__(self, names, shape):
        self.me = {n: (own_index(n[0]) >> (n[1].bit_length() - 1)) & 1 for n in names}
        self.names, self.terms, self.fixed, self.shape = list(names), [], {}, shape

    def cut(self, term, chosen):
        array, names, part = term
        starts, sizes = [], []
        for n in names:
            starts.append(chosen.get(n, jnp.uint32(0)))
            sizes.append(1 if n in chosen else 2)
        for low, high in part:
            starts.append(jnp.uint32(low))
            sizes.append(high - low)
        left = [2 for n in names if n not in chosen]
        return lax.dynamic_slice(array, starts, sizes).reshape(left + [h - l for l, h in part])

    def total(self, chosen):
        pieces = [self.cut(t, chosen).astype(f32) for t in self.terms]
        return sum(pieces[1:], pieces[0])

    def outgoing(self, name):
        return self.total({**self.fixed, name: 1 - self.me[name]}).astype(bf16)

    def arrived(self, name, value):
        self.fixed[name] = self.me[name]
        names = [n for n in self.names if n not in self.fixed]
        self.terms.append((value, names, [(0, d) for d in self.shape]))

    def exchange(self, name):
        self.arrived(name, swap(self.outgoing(name), *name))

    def result(self):
        return self.total(self.fixed)


def normalize(values, gain, shift):
    average = jnp.mean(values, axis=-1, keepdims=True)
    centered = values - average
    inverse = lax.rsqrt(jnp.mean(centered * centered, axis=-1, keepdims=True) + EPSILON)
    normed = centered * inverse
    return normed * gain + shift, normed, inverse


def normalize_back(upstream, normed, inverse, gain):
    scaled = upstream * gain
    plain = jnp.mean(scaled, axis=-1, keepdims=True)
    cross = jnp.mean(scaled * normed, axis=-1, keepdims=True)
    result = inverse * (scaled - plain - normed * cross)
    return result, jnp.sum(upstream * normed, axis=0), jnp.sum(upstream, axis=0)


def shards(
    tokens, time_feat, cotangent, segment_ids, time_weight, time_bias, query_weight, query_bias, key_weight,
    value_weight, value_bias, output_weight, output_bias, mixing_gain, mixing_bias, up_weight, up_bias,
    down_weight, down_bias, final_gain, final_bias,
):
    me_dp, me = own_index("dp"), own_index("ctx")
    dp, ctx = lax.axis_size("dp"), lax.axis_size("ctx")
    devices = dp * ctx
    piece, width = tokens.shape[1], tokens.shape[2]
    hidden = up_weight.shape[1]
    own, ratio = width // devices, hidden // width
    cols = width // ctx
    per_chunk = piece // BLOCK
    tokens, cotangent, ids = tokens[0], cotangent[0], segment_ids[0]

    held = {0: tokens, ctx // 2: swap(tokens, "ctx", ctx // 2)}
    vectors = [
        time_bias, query_bias, value_bias, output_bias, mixing_gain, mixing_bias, down_bias, final_gain, final_bias
    ]
    small = jnp.concatenate([jnp.stack(vectors), up_bias.reshape(ratio, own)]).T
    small = jnp.pad(small, ((0, 0), (0, 128 - small.shape[1])))
    pieces = []
    for k in range(ctx):
        at = (me ^ k) * cols
        parts = [
            lax.dynamic_slice_in_dim(w, at + p * 128, 128, 1)
            for p in range(cols // 128)
            for w in (query_weight, key_weight, value_weight)
        ] + [lax.dynamic_slice_in_dim(time_weight, at, cols, 1)]
        pieces.append(jnp.concatenate(parts + [small], axis=1))
    first = jnp.concatenate(to_absolute(trade(pieces, "ctx"), me))
    second = jnp.concatenate(
        [up_weight, output_weight] + [down_weight[n * own : (n + 1) * own] for n in range(ratio)], axis=1
    )
    second, first = lax.optimization_barrier((second, first))
    second = lax.all_gather(second, BOTH, axis=0, tiled=True)
    up_full, output_full = second[:, :hidden], second[:, hidden : hidden + width]
    down_full = jnp.stack(
        [second[:, hidden + n * width : hidden + (n + 1) * width].reshape(devices, own, width) for n in range(1, 1 + ratio)],
        axis=1,
    ).reshape(hidden, width)

    first = first[None]
    for n, bit in enumerate(reversed(bits(dp))):
        if n == 1:
            first, held[ctx // 2] = lax.optimization_barrier((first, held[ctx // 2]))
        first = jnp.concatenate([first, swap(first, "dp", bit)])
    for bit in reversed(bits(ctx)[:-1]):
        held.update({k | bit: swap(v, "ctx", bit) for k, v in list(held.items())})
    token_chunks = [held[k] for k in range(ctx)]
    first = jnp.concatenate(
        [
            lax.dynamic_index_in_dim(first, flipped((me_dp ^ c), dp), 0, False)
            for c in range(dp)
        ]
    )
    qkv_weight = first[:, : 3 * cols]
    table = first[:, 4 * cols :].astype(f32).T
    time_shift_bias, query_shift, value_shift, output_shift, gain_one, bias_one, down_shift, gain_two, bias_two = [
        table[n] for n in range(len(vectors))
    ]
    up_shift = table[len(vectors) : len(vectors) + ratio].reshape(ratio, devices, own).transpose(1, 0, 2).reshape(hidden)
    shift_cols = trade([nn(time_feat, first[:, 3 * cols : 4 * cols])] * ctx, "ctx")
    time_shift = jnp.concatenate(to_absolute(shift_cols, me), axis=1) + time_shift_bias
    qkv_shift = []
    for p in range(cols // 128):
        at = me * cols + p * 128
        qkv_shift.append(lax.dynamic_slice_in_dim(query_shift, at, 128))
        qkv_shift.append(jnp.zeros((128,), f32))
        qkv_shift.append(lax.dynamic_slice_in_dim(value_shift, at, 128))
    qkv_shift = jnp.concatenate(qkv_shift)
    start_row = (jnp.concatenate(token_chunks).astype(f32) + time_shift).astype(bf16)
    residual_in = tokens.astype(f32) + time_shift
    qkv = (nn(start_row, qkv_weight) + qkv_shift).astype(bf16)

    info = spans(ids, me)
    ids_col, ids_row = ids.reshape(-1, 1), ids.reshape(-1, 1, BLOCK)
    mixed, logsum = attention_forward(info, qkv, ids_col, ids_row, per_chunk)
    returned = trade([mixed[k * piece : (k + 1) * piece] for k in range(ctx)], "ctx")
    returned, down_full = lax.optimization_barrier((returned, down_full))
    attended = jnp.concatenate(to_absolute(returned, me), axis=1)

    branch = nn(attended, output_full) + output_shift
    hidden_one, normed_one, inverse_one = normalize(residual_in + branch, gain_one, bias_one)
    hidden_low = hidden_one.astype(bf16)
    pre_gelu = nn(hidden_low, up_full) + up_shift
    share = 0.5 * (1.0 + lax.erf(pre_gelu * 0.5**0.5))
    activated = (pre_gelu * share).astype(bf16)
    slope = (share + pre_gelu * jnp.exp(-0.5 * pre_gelu * pre_gelu) * 0.3989422804014327).astype(bf16)
    activated, slope = lax.optimization_barrier((activated, slope))
    feed_out = nn(activated, down_full) + down_shift
    result, normed_two, inverse_two = normalize(hidden_one + feed_out, gain_two, bias_two)
    layer_out = result.astype(bf16)

    upstream = cotangent.astype(f32)
    grad_two, gain_two_grad, bias_two_grad = normalize_back(upstream, normed_two, inverse_two, gain_two)
    grad_feed = grad_two.astype(bf16)
    down_grad = tn(activated, grad_feed).astype(bf16)
    down_shift_grad = jnp.sum(grad_feed.astype(f32), axis=0)
    grad_inner = (nt(grad_feed, down_full) * slope.astype(f32)).astype(bf16)
    dp_names, ctx_names = [("dp", b) for b in bits(dp)], [("ctx", b) for b in bits(ctx)]
    names = dp_names[::-1] + ctx_names[::-1]
    core, turn, rest = ctx_names[0], dp_names[:2] + ctx_names[1:], dp_names[2:]
    whole = {}

    def share(label, array, height):
        size = (height, array.shape[-1])
        whole[label] = Halving(names, size)
        whole[label].terms = [(array.reshape([2] * len(names) + list(size)), names, [(0, d) for d in size])]
        whole[label].exchange(core)

    def stream(label, part, turned):
        sums = Halving(names, [high - low for low, high in part])
        sums.fixed = {core: sums.me[core]}
        sums.terms = [(array, left, part) for array, left, _ in whole[label].terms]
        return sums, turn[turned:] + turn[:turned] + rest

    def depart(moving, beside):
        going = [s.outgoing(name) for s, name in moving]
        going, beside = lax.optimization_barrier((going, beside))
        return [(s, name, swap(value, *name)) for (s, name), value in zip(moving, going)], beside

    def land(flights, beside):
        values, beside = lax.optimization_barrier(([value for _, _, value in flights], beside))
        for (s, name, _), value in zip(flights, values):
            s.arrived(name, value)
        return beside

    def following(pairs):
        return [(s, o.pop(0)) for s, o in pairs if o]

    share("down", down_grad, ratio * own)
    streams = [stream("down", [(0, ratio * own), (0, width)], 0)]
    ahead, grad_inner = depart(following(streams), grad_inner)
    up_grad = tn(hidden_low, grad_inner).astype(bf16)
    up_shift_grad = jnp.sum(grad_inner.astype(f32), axis=0)
    grad_hidden = grad_two + nt(grad_inner, up_full)
    grad_one, gain_one_grad, bias_one_grad = normalize_back(grad_hidden, normed_one, inverse_one, gain_one)
    grad_branch = grad_one.astype(bf16)
    output_grad = tn(attended, grad_branch).astype(bf16)
    output_shift_grad = jnp.sum(grad_branch.astype(f32), axis=0)
    vector_grads = jnp.stack(
        [output_shift_grad, gain_one_grad, bias_one_grad, down_shift_grad, gain_two_grad, bias_two_grad]
    )
    vector_grads = lax.optimization_barrier(vector_grads).reshape(6, devices, own).transpose(1, 0, 2).reshape(devices, 6 * own)
    vector_grads = jnp.concatenate([vector_grads, up_shift_grad.reshape(devices, ratio * own)], axis=1)
    vector_grads = jnp.pad(vector_grads, ((0, 0), (0, width - vector_grads.shape[1]))).astype(bf16)
    extra = 8
    rest_grad = jnp.concatenate(
        [output_grad.reshape(devices, own, width), jnp.broadcast_to(vector_grads[:, None], (devices, extra, width))],
        axis=1,
    )

    share("up", up_grad, own)
    share("rest", rest_grad, own + extra)
    streams += [
        stream("up", [(0, own), (0, 5 * hidden // 8)], 2),
        stream("up", [(0, own), (5 * hidden // 8, hidden)], 0),
        stream("rest", [(0, own + extra), (0, width)], 0),
    ]

    grad_attended = nt(grad_branch, output_full).astype(bf16)
    pieces = [lax.dynamic_slice_in_dim(grad_attended, (me ^ k) * cols, cols, 1) for k in range(ctx)]
    grad_mixed = jnp.concatenate(trade(pieces, "ctx"))
    grad_mixed = land(ahead, grad_mixed)

    def weight_stream(product):
        size = (ctx * own, product.shape[1])
        sums = Halving(dp_names[::-1], size)
        array = product.reshape([2] * len(dp_names) + list(size))
        sums.terms = [(array, dp_names[::-1], [(0, d) for d in size])]
        return sums, list(dp_names)

    def products(grad):
        return tn(start_row, grad), jnp.sum(grad.astype(f32), axis=0)

    grads, pair_streams, qkv_sum = [], [], []
    for pair in range(cols // 128):
        flights, grad_mixed = depart(following(streams + pair_streams), grad_mixed)
        grad = attention_backward(pair, info, qkv, grad_mixed, mixed, logsum, ids_col, ids_row, per_chunk)
        if pair == 0:
            grad_mixed, grad, (product, total) = land(flights, (grad_mixed, grad, products(grad)))
        else:
            grad_mixed, grad = land(flights, (grad_mixed, grad))
            product, total = products(grad)
        grads.append(grad)
        pair_streams.append(weight_stream(product))
        qkv_sum.append(total)

    qkv_sum = jnp.concatenate(qkv_sum)
    row_sum = jnp.sum(grad_one, axis=0, keepdims=True) + lax.dot_general(
        qkv_sum[None],
        qkv_weight.astype(f32),
        (((1,), (1,)), ((), ())),
        precision=lax.Precision.HIGHEST,
        preferred_element_type=f32,
    )
    message = jnp.concatenate(
        [row_sum]
        + [qkv_sum[None, (3 * p + n) * 128 : (3 * p + n + 1) * 128] for n in (0, 2) for p in range(cols // 128)]
        + [time_feat.astype(f32)],
        axis=1,
    )
    message_names = dp_names[::-1]

    rows = jnp.concatenate(grads, axis=1).reshape(ctx // 2, 2, piece, 3 * cols)
    odd = nt(rows[:, 1].reshape(-1, 3 * cols), qkv_weight).astype(bf16)
    flights, (rows, odd, message) = depart(following(streams + pair_streams), (rows, odd, message))
    odd = swap(odd, *core)
    reply = swap(message, *message_names.pop(0))
    even = nt(rows[:, 0].reshape(-1, 3 * cols), qkv_weight)
    even, odd, message, reply = land(flights, (even, odd, message, reply))
    message = jnp.concatenate([message, reply])
    even = (even + odd.astype(f32)).reshape(ctx // 2, piece, width)
    away = [even[n].astype(bf16) for n in range(1, ctx // 2)]
    kept, came = [], None
    while any(o for _, o in streams + pair_streams) or message_names:
        fast, slow = following(pair_streams), following(streams)
        flights, (away, message) = depart(fast + slow, (away, message))
        if came is None:
            came = [swap(value, "ctx", 2 * n + 2) for n, value in enumerate(away)]
        if message_names:
            message = jnp.concatenate([message, swap(message, *message_names.pop(0))])
        kept += flights[len(fast) :]
        flights = flights[: len(fast)]
        if any(o for _, o in streams):
            flights, kept = flights + kept, []
        if not any(o for _, o in pair_streams):
            flights, kept = flights + kept, []
        message, came = land(flights, (message, came)) if not kept else (land(flights, message), came)
    summed = jnp.concatenate([s.result() for s, _ in pair_streams], axis=1).reshape(ctx, own, 3 * cols)
    summed = [lax.dynamic_index_in_dim(summed, (me ^ k), 0, False) for k in range(ctx)]
    summed, message = lax.optimization_barrier((summed, message))
    blocks_out = to_absolute(trade(summed, "ctx"), me)
    message = jnp.stack(trade([message] * ctx, "ctx"))
    tokens_grad = (grad_one + sum([c.astype(f32) for c in came], even[0])).astype(bf16)
    down_weight_grad, up_left, up_right, rest_left = [s.result() for s, _ in streams]
    up_weight_grad = jnp.concatenate([up_left, up_right], axis=1)
    output_weight_grad, vector_grads = rest_left[:own], rest_left[own]
    output_bias_grad, mixing_gain_grad, mixing_bias_grad, down_bias_grad, final_gain_grad, final_bias_grad = [
        vector_grads[n * own : (n + 1) * own] for n in range(6)
    ]
    up_bias_grad = vector_grads[6 * own : (6 + ratio) * own]

    mine = (me_dp * ctx + me) * own
    row_sums = jnp.sum(message[:, :, :width], axis=0)
    time_weight_grad = lax.dot_general(
        lax.dynamic_slice_in_dim(message[0, :, width + 2 * cols :], mine, own, 1),
        row_sums,
        (((0,), (0,)), ((), ())),
        precision=lax.Precision.HIGHEST,
        preferred_element_type=f32,
    )
    time_bias_grad = lax.dynamic_slice_in_dim(jnp.sum(row_sums, axis=0), mine, own)
    sums = jnp.sum(message[:, :, width : width + 2 * cols], axis=1)
    sums = lax.dynamic_index_in_dim(sums, mine // cols ^ me, 0, False)
    query_bias_grad = lax.dynamic_slice_in_dim(sums[:cols], mine % cols, own)
    value_bias_grad = lax.dynamic_slice_in_dim(sums[cols:], mine % cols, own)

    query_weight_grad, key_weight_grad, value_weight_grad = [
        jnp.concatenate(
            [
                block[:, (3 * p + n) * 128 : (3 * p + n + 1) * 128]
                for block in blocks_out
                for p in range(cols // 128)
            ],
            axis=1,
        )
        for n in range(3)
    ]
    return (
        layer_out[None],
        tokens_grad[None],
        time_weight_grad,
        time_bias_grad,
        query_weight_grad,
        query_bias_grad,
        key_weight_grad,
        value_weight_grad,
        value_bias_grad,
        output_weight_grad,
        output_bias_grad,
        mixing_gain_grad,
        mixing_bias_grad,
        up_weight_grad,
        up_bias_grad,
        down_weight_grad,
        down_bias_grad,
        final_gain_grad,
        final_bias_grad,
    )


def solution(mesh):
    rows, split_rows, split = P("dp", "ctx", None), P(BOTH, None), P(BOTH)
    return jax.shard_map(
        shards,
        mesh=mesh,
        in_specs=(
            rows, P("dp", None), rows, P("dp", None), split_rows, split, split_rows, split, split_rows, split_rows,
            split, split_rows, split, split, split, split_rows, split, split_rows, split, split, split,
        ),
        out_specs=(
            rows, rows, split_rows, split, split_rows, split, split_rows, split_rows, split, split_rows, split, split,
            split, split_rows, split, split_rows, split, split, split,
        ),
        check_vma=False,
    )
```
